32 devices in a mesh: gx: 8 (over z, core), gy: 4 (over y, x).
Axes of the slice: x: 2, y: 2, z: 4, core: 2. Of those that a mesh axis runs over, the one named last changes fastest.
Arguments:
- source: float32 [64, 512, 256], P('gx', 'gy'), may hold values from -8 to 8
- density: float32 [64, 512, 256], P('gx', 'gy'), may hold values from 0.08 to 1.7
Outputs:
- pressure: float32 [64, 512, 256], P('gx', 'gy')
- residual: float32 [64, 512, 256], P('gx', 'gy')
The draws below stay inside these ranges and needn't reach their ends.
All inputs are finite; a program needn't handle non-finite values.
Results may differ from the reference program's by a relative error of at most 0.00021.
Values sent between devices are 32-bit elements; how exact they have to be, the bound alone decides.
No kernel may reach another device: no remote copies, remote signals or barrier semaphores. Data moves between devices by JAX's collectives and lax.ppermute only.
A program may use at most 64 MiB of HBM per device.

```python
import math
import jax
import jax.numpy as jnp
from jax import lax

NZ = 256
ITERS = 2
NX = 64
NY = 512


def grid_axes():
    x_axis = (jnp.arange(NX, dtype=jnp.float32) + 0.5) / NX
    y_axis = (jnp.arange(NY, dtype=jnp.float32) + 0.5) / NY
    z_axis = (jnp.arange(NZ, dtype=jnp.float32) + 0.5) / NZ
    return (x_axis, y_axis, z_axis)


def bump(axis_values, center, width):
    return jnp.exp(-0.5 * ((axis_values - center) / width) ** 2)


def draw_source(key, part):
    x_axis, y_axis, z_axis = grid_axes()
    two_pi = 2.0 * math.pi
    smooth = jnp.zeros((NX, NY, NZ), jnp.float32)
    mode_key = jax.random.fold_in(key, 11)
    for mode_index in range(6):
        numbers = jax.random.uniform(jax.random.fold_in(mode_key, mode_index), (7,), jnp.float32)
        wave_x = 0.5 + 3.5 * numbers[0]
        wave_y = 0.5 + 5.5 * numbers[1]
        wave_z = 2.0 * numbers[2]
        amplitude = 1.2 * numbers[6] - 0.6
        profile_x = jnp.cos(two_pi * (wave_x * x_axis + numbers[3]))
        profile_y = jnp.cos(two_pi * (wave_y * y_axis + numbers[4]))
        profile_z = jnp.cos(two_pi * (wave_z * z_axis + numbers[5]))
        smooth = smooth + amplitude * profile_x[:, None, None] * profile_y[None, :, None] * profile_z[None, None, :]
    plume_key = jax.random.fold_in(key, 23)
    for plume_index in range(5):
        numbers = jax.random.uniform(jax.random.fold_in(plume_key, plume_index), (5,), jnp.float32)
        strength = (1.0 + 1.5 * numbers[3]) * jnp.where(numbers[4] < 0.5, -1.0, 1.0)
        smooth = smooth + strength * bump(x_axis, numbers[0], 0.07)[:, None, None] * bump(y_axis, numbers[1], 0.07)[None, :, None] * bump(z_axis, 0.2 + 0.6 * numbers[2], 0.2)[None, None, :]
    noise_key = jax.random.fold_in(key, 37)
    rough = 0.35 * jnp.clip(jax.random.normal(noise_key, (NX, NY, NZ), jnp.float32), -4.0, 4.0)
    return jnp.clip(smooth + rough, -8.0, 8.0)


def draw_density(key, part):
    x_axis, y_axis, z_axis = grid_axes()
    two_pi = 2.0 * math.pi
    numbers = jax.random.uniform(jax.random.fold_in(key, 5), (6,), jnp.float32)
    height = 0.45 + 0.15 * numbers[0] + 0.08 * jnp.cos(two_pi * ((0.5 + 1.5 * numbers[1]) * x_axis + numbers[2]))[:, None] * jnp.cos(two_pi * ((0.5 + 1.5 * numbers[3]) * y_axis + numbers[4]))[None, :]
    layer = jax.nn.sigmoid((z_axis[None, None, :] - height[:, :, None]) / 0.06)
    columns = jnp.zeros((NX, NY), jnp.float32)
    column_key = jax.random.fold_in(key, 17)
    for column_index in range(4):
        picks = jax.random.uniform(jax.random.fold_in(column_key, column_index), (3,), jnp.float32)
        columns = columns + (1.0 + picks[2]) * bump(x_axis, picks[0], 0.06)[:, None] * bump(y_axis, picks[1], 0.06)[None, :]
    heat = 2.0 * layer + columns[:, :, None]
    noise_key = jax.random.fold_in(key, 29)
    rough = jax.random.uniform(noise_key, (NX, NY, NZ), jnp.float32, -0.5, 0.5)
    hotness = 1.0 - jnp.exp(-heat)
    log_mean = math.log(1.2) + hotness * math.log(1.0 / 6.0)
    spread = math.log(2.0) + hotness * math.log(3.0)
    return jnp.exp(log_mean + spread * rough)


def setup_inputs(seed: int = 0) -> dict:
    streams_of = jax.random.split(jax.random.key(seed), 3)
    source = draw_source(jax.random.fold_in(streams_of[2], 71), 0)
    density = draw_density(jax.random.fold_in(streams_of[2], 71), 0)
    return dict(source=source, density=density)


def neighbours(padded):
    return [padded[2:, 1:-1, 1:-1], padded[:-2, 1:-1, 1:-1], padded[1:-1, 2:, 1:-1], padded[1:-1, :-2, 1:-1], padded[1:-1, 1:-1, 2:], padded[1:-1, 1:-1, :-2]]

def face_weights(density):
    nearby = neighbours(jnp.pad(density, 1))
    weights = [2.0 / (density + other) for other in nearby]
    diag_sum = weights[0]
    for weight_one in weights[1:]:
        diag_sum = diag_sum + weight_one
    return (weights, lax.rsqrt(diag_sum))

def scaled_apply(field, weights, scale_inv):
    scaled = scale_inv * field
    nearby = neighbours(jnp.pad(scaled, 1))
    total = weights[0] * nearby[0]
    for weight_one, other in zip(weights[1:], nearby[1:]):
        total = total + weight_one * other
    return field - scale_inv * total

def reference(source, density):
    weights, scale_inv = face_weights(density)
    residual = scale_inv * source
    shadow = scaled_apply(residual, weights, scale_inv)
    solution = jnp.zeros_like(source)
    direction = jnp.zeros_like(source)
    along = jnp.zeros_like(source)
    pushed = jnp.zeros_like(source)
    gamma_old = jnp.float32(1.0)
    alpha_old = jnp.float32(1.0)
    for iteration in range(ITERS):
        gamma_now = jnp.sum(residual * residual)
        delta_now = jnp.sum(shadow * residual)
        fresh = scaled_apply(shadow, weights, scale_inv)
        if iteration == 0:
            beta_now = jnp.float32(0.0)
            alpha_now = gamma_now / delta_now
        else:
            beta_now = gamma_now / gamma_old
            alpha_now = gamma_now / (delta_now - beta_now * gamma_now / alpha_old)
        pushed = fresh + beta_now * pushed
        along = shadow + beta_now * along
        direction = residual + beta_now * direction
        solution = solution + alpha_now * direction
        residual = residual - alpha_now * along
        shadow = shadow - alpha_now * pushed
        gamma_old = gamma_now
        alpha_old = alpha_now
    return (scale_inv * solution, residual)
```

```python
import functools

import jax
import jax.numpy as jnp
from jax import lax
from jax.experimental import pallas as pl
from jax.experimental.pallas import tpu as pltpu
from jax.sharding import PartitionSpec as P

ITERS = 2
TILE = 8
OFF = 16
TINY = 1e-3
PART = 16
VMEM = pltpu.VMEM


def swaps(nx, ny):
    at = lambda x, y: x * ny + y
    near, far, ynear, yfar = [], [], [], []
    for x in range(nx):
        for y in range(ny):
            near.append((at(x, y), at(x ^ 1, y)))
            other = x - 1 if x % 2 == 0 else x + 1
            inside = 0 <= other < nx
            far.append((at(x, y), at(other, y) if inside else at(x, y ^ 1)))
            ynear.append((at(x, y), at(x, y ^ 1)))
            beside = y - 1 if y % 2 == 0 else y + 1
            within = 0 <= beside < ny
            yfar.append((at(x, y), at(x, beside) if within else at(x ^ 1, y)))
    return near, far, ynear, yfar


def pack_rows(par, dlo, dhi, slo, shi, near, xs_out, dg_out):
    planes = dlo.shape[0]
    row = lax.broadcasted_iota(jnp.int32, (TILE, dlo.shape[2]), 0)

    def tiles(dens_lo, dens_hi, src_lo, src_hi):
        down = jnp.where(row < 3, dens_lo, jnp.where((row >= 4) & (row < 6), pltpu.roll(src_lo, 4, 0), 0.0))
        up = jnp.where(row > 4, dens_hi, jnp.where((row == 2) | (row == 3), pltpu.roll(src_hi, 4, 0), 0.0))
        return down, up

    yodd = par[1] == 1

    def put(k, down, up):
        xs_out[k] = jnp.where(yodd, down, up)
        dg_out[k] = jnp.where(yodd, up, down)

    for k in range(planes):
        put(k, *tiles(dlo[k], dhi[k], slo[k], shi[k]))
    last = near.shape[1] - TILE
    xodd = par[0] == 1

    for k in range(2):
        d = jnp.where(xodd, k + 1, k)
        s = jnp.where(xodd, 3 + k, 3 + k)
        down, up = tiles(near[d, :TILE], near[d, last:], near[s, :TILE], near[s, last:])
        put(planes + k, down, up)


def main_kernel(par, dens, src, near, far, rxs, rdg, rfc, r0_out, w0_out, n0_out, sc_out, mom_out,
                dx, sx, wx, wy, wz, sc, g0, g1):
    nx, ny, nz = dens.shape
    lo_rows, hi_rows = OFF - TILE, OFF + ny
    total = hi_rows + TILE
    xodd, yodd = par[0] == 1, par[1] == 1
    has_lo, has_hi, has_down, has_up = par[2] == 1, par[3] == 1, par[4] == 1, par[5] == 1
    zero_tile = jnp.zeros((TILE, nz), jnp.float32)
    row = lax.broadcasted_iota(jnp.int32, (TILE, nz), 0)
    own = slice(OFF, OFF + ny)

    for k in range(nx):
        dx[k + 3, own] = dens[k]
        sx[k + 3, own] = src[k]

    @pl.when(xodd)
    def _():
        for k in range(3):
            dx[k, own] = jnp.where(has_lo, near[k], 0.0)
            dx[nx + 3 + k, own] = jnp.where(has_hi, far[k], 0.0)
        for k in range(2):
            sx[1 + k, own] = jnp.where(has_lo, near[3 + k], 0.0)
            sx[nx + 3 + k, own] = jnp.where(has_hi, far[3 + k], 0.0)

    @pl.when(jnp.logical_not(xodd))
    def _():
        for k in range(3):
            dx[k, own] = jnp.where(has_lo, far[k], 0.0)
            dx[nx + 3 + k, own] = jnp.where(has_hi, near[k], 0.0)
        for k in range(2):
            sx[1 + k, own] = jnp.where(has_lo, far[3 + k], 0.0)
            sx[nx + 3 + k, own] = jnp.where(has_hi, near[3 + k], 0.0)

    def rows_of(e, lower, upper, inside):
        low = jnp.where(jnp.logical_and(has_down, inside), lower, 0.0)
        high = jnp.where(jnp.logical_and(has_up, inside), upper, 0.0)
        dx[e, lo_rows:OFF] = jnp.where(row > 4, low, 0.0)
        sx[e, lo_rows:OFF] = jnp.where(row > 5, pltpu.roll(low, 4, 0), 0.0)
        dx[e, hi_rows:total] = jnp.where(row < 3, high, 0.0)
        sx[e, hi_rows:total] = jnp.where(row < 2, pltpu.roll(high, 4, 0), 0.0)

    for k in range(nx):
        a, b = rxs[k], rdg[k]
        rows_of(k + 3, jnp.where(yodd, a, b), jnp.where(yodd, b, a), True)
    for k in range(2):
        a, b = rxs[nx + k], rdg[nx + k]
        rows_of(jnp.where(xodd, 1 + k, nx + 3 + k), jnp.where(yodd, a, b), jnp.where(yodd, b, a), jnp.where(xodd, has_lo, has_hi))
        a, b = rfc[k], rfc[2 + k]
        rows_of(jnp.where(xodd, nx + 3 + k, 1 + k), jnp.where(yodd, a, b), jnp.where(yodd, b, a), jnp.where(xodd, has_hi, has_lo))
    for e in (0, nx + 5):
        rows_of(e, zero_tile, zero_tile, False)
    for e in range(nx + 6):
        dx[e, lo_rows - TILE:lo_rows] = zero_tile
        dx[e, total:total + TILE] = zero_tile
        g0[e, lo_rows - TILE:lo_rows] = zero_tile
        g0[e, total:total + TILE] = zero_tile
        wy[e, lo_rows - TILE:lo_rows] = zero_tile
        wy[e, total:total + TILE] = zero_tile

    R = 24 if (total - lo_rows) % 24 == 0 else TILE
    lane = lax.broadcasted_iota(jnp.int32, (R, nz), 1)
    inner = lane < nz - 1
    first = lane == 0

    def weight(total_density):
        return 2.0 / jnp.maximum(total_density, TINY)

    for r in range(lo_rows, total, R):
        wx[0, r:r + R] = weight(dx[0, r:r + R] + dx[1, r:r + R])

    def faces(e, carry):
        for r in range(lo_rows, total, R):
            c = dx[e, r:r + R]
            x_up = weight(c + dx[e + 1, r:r + R])
            y_up = weight(c + dx[e, r + 1:r + R + 1])
            z_up = weight(c + jnp.where(inner, pltpu.roll(c, nz - 1, 1), 0.0))
            wx[e, r:r + R] = x_up
            wy[e, r:r + R] = y_up
            z_in = jnp.where(inner, z_up, 0.0)
            wz[e, r:r + R] = z_in
            z_down = jnp.where(first, weight(c), pltpu.roll(z_in, 1, 1))
            diag = x_up + wx[e - 1, r:r + R] + y_up + wy[e, r - 1:r + R - 1] + z_up + z_down
            s = jnp.where(c > 0, lax.rsqrt(diag), 0.0)
            sc[e, r:r + R] = s
            g0[e, r:r + R] = s * (s * sx[e, r:r + R])
        return carry

    lax.fori_loop(1, nx + 5, faces, 0)

    def couple(g, e, r, n):
        c = g[e, r:r + n]
        w = wz[e, r:r + n]
        t = wx[e, r:r + n] * g[e + 1, r:r + n] + wx[e - 1, r:r + n] * g[e - 1, r:r + n]
        t = t + wy[e, r:r + n] * g[e, r + 1:r + n + 1] + wy[e, r - 1:r + n - 1] * g[e, r - 1:r + n - 1]
        return t + w * pltpu.roll(c, nz - 1, 1) + pltpu.roll(w * c, 1, 1)

    def first_apply(e, carry):
        for r in range(lo_rows, total, R):
            s = sc[e, r:r + R]
            r0 = s * sx[e, r:r + R]
            w0 = r0 - s * couple(g0, e, r, R)
            g1[e, r:r + R] = s * w0
        return carry

    lax.fori_loop(2, nx + 4, first_apply, 0)

    Q = 32 if ny % 32 == 0 else TILE
    zero = jnp.zeros((TILE, nz), jnp.float32)

    def fold(v):
        out = v[:TILE]
        for q in range(TILE, Q, TILE):
            out = out + v[q:q + TILE]
        return out

    def second_apply(i, sums):
        e = i + 3
        sums = list(sums)
        for r in range(OFF, OFF + ny, Q):
            s = sc[e, r:r + Q]
            r0 = s * sx[e, r:r + Q]
            w0 = r0 - s * couple(g0, e, r, Q)
            n0 = w0 - s * couple(g1, e, r, Q)
            sc_out[i, r - OFF:r - OFF + Q] = s
            r0_out[i, r - OFF:r - OFF + Q] = r0
            w0_out[i, r - OFF:r - OFF + Q] = w0
            n0_out[i, r - OFF:r - OFF + Q] = n0
            for k, (a, b) in enumerate(((r0, r0), (w0, r0), (w0, w0), (n0, w0), (n0, r0))):
                sums[k] = sums[k] + fold(a * b)
        return tuple(sums)

    sums = lax.fori_loop(0, nx, second_apply, (zero,) * 5)
    place = lax.broadcasted_iota(jnp.int32, (1, 128), 1) // PART
    out = jnp.zeros((1, 128), jnp.float32)
    for k, v in enumerate(sums):
        v = jnp.sum(v, axis=0, keepdims=True)
        p = v[:, :128]
        for q in range(128, nz, 128):
            p = p + v[:, q:q + 128]
        width = 64
        while width >= PART:
            p = p + pltpu.roll(p, width, 1)
            width //= 2
        out = jnp.where(place == k, p, out)
    mom_out[...] = out


def last_kernel(mom, r0_ref, w0_ref, n0_ref, sc_ref, p_out, r_out):
    place = lax.broadcasted_iota(jnp.int32, mom.shape, 1) // PART
    m = mom[...]

    def whole(v):
        return jnp.sum(jnp.sum(v, axis=0, keepdims=True), axis=1, keepdims=True)

    def lanes(k):
        return pltpu.roll(m, (128 - k * PART) % 128, 1) if k else m

    head = place == 0
    m0, m1, m2, m3, m4 = (jnp.where(head, lanes(k), 0.0) for k in range(5))
    gamma0 = whole(m0)
    delta0 = whole(m1)
    a0 = gamma0 / delta0
    gamma1 = whole(m0 - a0 * (m1 + m1 - a0 * m2))
    delta1 = whole(m1 - a0 * (m4 + m2 - a0 * m3))
    b1 = gamma1 / gamma0
    a1 = gamma1 / (delta1 - b1 * gamma1 / a0)
    nx, ny, nz = r0_ref.shape
    Q = 32 if ny % 32 == 0 else TILE
    for i in range(nx):
        for r in range(0, ny, Q):
            at = (i, slice(r, r + Q))
            r0, w0 = r0_ref[at], w0_ref[at]
            r1 = r0 - a0 * w0
            w1 = w0 - a0 * n0_ref[at]
            along = w1 + b1 * w0
            direction = r1 + b1 * r0
            p_out[at] = sc_ref[at] * (a0 * r0 + a1 * direction)
            r_out[at] = r1 - a1 * along


def shards(nx_dev, ny_dev, source, density):
    both = ("gx", "gy")
    near_pairs, far_pairs, ynear_pairs, yfar_pairs = swaps(nx_dev, ny_dev)
    nx, ny, nz = density.shape
    ix, iy = lax.axis_index("gx"), lax.axis_index("gy")
    xodd, yodd = ix % 2, iy % 2
    flags = [xodd, yodd, ix > 0, ix < nx_dev - 1, iy > 0, iy < ny_dev - 1]
    par = jnp.stack([jnp.asarray(f, jnp.int32) for f in flags])

    def planes(upper):
        d = lax.dynamic_slice_in_dim(density, jnp.where(upper, nx - 3, 0), 3, 0)
        s = lax.dynamic_slice_in_dim(source, jnp.where(upper, nx - 2, 0), 2, 0)
        return jnp.concatenate([d, s], axis=0)

    far = lax.ppermute(planes(xodd == 1), both, far_pairs)
    near = lax.ppermute(planes(xodd == 0), both, near_pairs)

    smem = pl.BlockSpec(memory_space=pltpu.SMEM)
    vmem = pl.BlockSpec(memory_space=VMEM)
    low = pl.BlockSpec((nx, TILE, nz), lambda i: (0, 0, 0))
    high = pl.BlockSpec((nx, TILE, nz), lambda i: (0, ny // TILE - 1, 0))
    rows = jax.ShapeDtypeStruct((nx + 2, TILE, nz), jnp.float32)
    xs, dg = pl.pallas_call(
        pack_rows, grid=(1,), out_shape=(rows, rows),
        in_specs=[smem, low, high, low, high, vmem], out_specs=(vmem, vmem), name="pack_rows",
    )(par, density, density, source, source, near)
    rxs = lax.ppermute(xs, both, ynear_pairs)
    rdg = lax.ppermute(dg, both, yfar_pairs)
    begin = jnp.where(xodd == 1, nx - 2, 0)
    corner = jnp.concatenate([lax.dynamic_slice_in_dim(v, begin, 2, 0) for v in (rxs, rdg)], axis=0)
    rfc = lax.ppermute(corner, both, far_pairs)

    whole = jax.ShapeDtypeStruct(density.shape, jnp.float32)
    ext = VMEM((nx + 6, ny + 2 * OFF, nz), jnp.float32)
    r0, w0, n0, sc, mom = pl.pallas_call(
        main_kernel, out_shape=(whole, whole, whole, whole, jax.ShapeDtypeStruct((1, 128), jnp.float32)),
        in_specs=[smem] + [vmem] * 7, out_specs=(vmem,) * 5, scratch_shapes=[ext] * 8, name="main_kernel",
    )(par, density, source, near, far, rxs, rdg, rfc)

    n = nx_dev * ny_dev
    sent = jnp.broadcast_to(mom[None], (n, 1, 128))
    got = lax.all_to_all(sent, both, 0, 0, tiled=True).reshape(n, 128)
    return pl.pallas_call(
        last_kernel, out_shape=(whole, whole), in_specs=[vmem] * 5, out_specs=(vmem, vmem), name="last_kernel",
    )(got, r0, w0, n0, sc)


def solution(mesh):
    spec = P("gx", "gy", None)
    body = functools.partial(shards, mesh.shape["gx"], mesh.shape["gy"])
    return jax.shard_map(body, mesh=mesh, in_specs=(spec, spec), out_specs=(spec, spec), check_vma=False)
```

```python
import functools

import jax
import jax.numpy as jnp
from jax import lax
from jax.experimental import pallas as pl
from jax.experimental.pallas import tpu as pltpu
from jax.sharding import PartitionSpec as P

ITERS = 2
TILE = 8
LANES = 128
OFF = 16
DEEP = 3
PART = 16
SUMS = 5
MIB = 1 << 20
VMEM = pltpu.VMEM


def swaps(nx, ny):
    at = lambda x, y: x * ny + y
    near, far, ynear, yfar = [], [], [], []
    for x in range(nx):
        for y in range(ny):
            near.append((at(x, y), at(x ^ 1, y)))
            other = x - 1 if x % 2 == 0 else x + 1
            inside = 0 <= other < nx
            far.append((at(x, y), at(other, y) if inside else at(x, y ^ 1)))
            ynear.append((at(x, y), at(x, y ^ 1)))
            beside = y - 1 if y % 2 == 0 else y + 1
            within = 0 <= beside < ny
            yfar.append((at(x, y), at(x, beside) if within else at(x ^ 1, y)))
    return near, far, ynear, yfar


def take_planes(par, dens, src, near_out, far_out):
    nx = dens.shape[0]
    xodd = par[0] == 1
    for out, first, second in ((near_out, jnp.where(xodd, 0, nx - 3), jnp.where(xodd, 0, nx - 2)),
                               (far_out, jnp.where(xodd, nx - 3, 0), jnp.where(xodd, nx - 2, 0))):
        for k in range(3):
            out[k] = dens[first + k]
        for k in range(2):
            out[3 + k] = src[second + k]


def take_rows(par, dens, src, near, xs_out, dg_out):
    nx, ny, nz = dens.shape
    row = lax.broadcasted_iota(jnp.int32, (TILE, nz), 0)
    xodd, yodd = par[0] == 1, par[1] == 1

    def put(k, d, s):
        down = jnp.where(row < 3, d(slice(0, TILE)), pltpu.roll(s(slice(0, TILE)), 4, 0))
        up = jnp.where(row > 4, d(slice(ny - TILE, ny)), pltpu.roll(s(slice(ny - TILE, ny)), 4, 0))
        xs_out[k] = jnp.where(yodd, down, up)
        dg_out[k] = jnp.where(yodd, up, down)

    for k in range(nx):
        put(k, lambda rows: dens[k, rows], lambda rows: src[k, rows])
    for k in range(2):
        put(nx + k, lambda rows: near[jnp.where(xodd, k + 1, k), rows], lambda rows: near[3 + k, rows])


def halves(nz):
    return [(h, slice(h * LANES, (h + 1) * LANES)) for h in range(nz // LANES)]


def put_plane(ref, e, rows, value):
    for h, lanes in halves(value.shape[-1]):
        ref[e, h, rows] = value[:, lanes]


def put_rows(dx, sx, e, low, high, ny):
    for value, at, in_rows in ((low, slice(OFF - TILE, OFF), None), (high, slice(OFF + ny, OFF + ny + TILE), None)):
        put_plane(dx, e, at, 0.5 * value)
        put_plane(sx, e, at, pltpu.roll(value, 4, 0))


def weigh(dx, sx, wx, wy, wz, sc, g0, lo, count):
    _, nh, rows, _ = dx.shape
    tiles = range(OFF - TILE, rows - OFF + TILE, TILE)
    lane = lax.broadcasted_iota(jnp.int32, (TILE, LANES), 1)
    inner, first = lane < LANES - 1, lane == 0
    for r in tiles:
        for h in range(nh):
            wx[lo - 1, h, pl.ds(r, TILE)] = 1.0 / (dx[lo - 1, h, pl.ds(r, TILE)] + dx[lo, h, pl.ds(r, TILE)])

    def plane(k, carry):
        e = lo + k
        for r in tiles:
            c = [dx[e, h, pl.ds(r, TILE)] for h in range(nh)]
            turned = [pltpu.roll(v, LANES - 1, 1) for v in c]
            z_up, z_in = [], []
            for h in range(nh):
                after = jnp.where(inner, turned[h], turned[h + 1] if h + 1 < nh else 0.0)
                w = 1.0 / (c[h] + after)
                z_up.append(w)
                z_in.append(w if h + 1 < nh else jnp.where(inner, w, 0.0))
                wz[e, h, pl.ds(r, TILE)] = z_in[h]
            back = [pltpu.roll(v, 1, 1) for v in z_in]
            for h in range(nh):
                x_up = 1.0 / (c[h] + dx[e + 1, h, pl.ds(r, TILE)])
                y_up = 1.0 / (c[h] + dx[e, h, pl.ds(r + 1, TILE)])
                wx[e, h, pl.ds(r, TILE)] = x_up
                wy[e, h, pl.ds(r, TILE)] = y_up
                z_down = jnp.where(first, back[h - 1] if h else 1.0 / c[0], back[h])
                diag = (x_up + wx[e - 1, h, pl.ds(r, TILE)]) + (y_up + wy[e, h, pl.ds(r - 1, TILE)]) + (z_up[h] + z_down)
                s = lax.rsqrt(diag)
                sc[e, h, pl.ds(r, TILE)] = s
                g0[e, h, pl.ds(r, TILE)] = s * (s * sx[e, h, pl.ds(r, TILE)])
        return carry

    lax.fori_loop(0, count, plane, 0)


def couple(g, wx, wy, wz, e, r, nh, inner, first):
    here = pl.ds(r, TILE)
    c = [g[e, h, here] for h in range(nh)]
    w = [wz[e, h, here] for h in range(nh)]
    ahead = [pltpu.roll(v, LANES - 1, 1) for v in c]
    behind = [pltpu.roll(a * b, 1, 1) for a, b in zip(w, c)]
    out = []
    for h in range(nh):
        t = wx[e, h, here] * g[e + 1, h, here] + wx[e - 1, h, here] * g[e - 1, h, here]
        t = t + (wy[e, h, here] * g[e, h, pl.ds(r + 1, TILE)] + wy[e, h, pl.ds(r - 1, TILE)] * g[e, h, pl.ds(r - 1, TILE)])
        after = jnp.where(inner, ahead[h], ahead[h + 1]) if h + 1 < nh else ahead[h]
        before = jnp.where(first, behind[h - 1], behind[h])
        out.append(t + (w[h] * after + before))
    return out


def apply_first(sx, wx, wy, wz, sc, g0, g1, w0, lo, count):
    _, nh, rows, _ = sx.shape
    lane = lax.broadcasted_iota(jnp.int32, (TILE, LANES), 1)
    inner, first = lane < LANES - 1, lane == 0

    def plane(k, carry):
        e = lo + k
        for r in range(OFF - TILE, rows - OFF + TILE, TILE):
            t = couple(g0, wx, wy, wz, e, r, nh, inner, first)
            for h in range(nh):
                s = sc[e, h, pl.ds(r, TILE)]
                v = s * sx[e, h, pl.ds(r, TILE)] - s * t[h]
                w0[e, h, pl.ds(r, TILE)] = v
                g1[e, h, pl.ds(r, TILE)] = s * v
        return carry

    lax.fori_loop(0, count, plane, 0)


def clear_outside(par, g1, e, has_x):
    _, nh, rows, _ = g1.shape
    zero = jnp.zeros((TILE, LANES), jnp.float32)
    for flag, at in ((par[4], OFF - TILE), (par[5], rows - OFF)):

        @pl.when(flag == 0)
        def _():
            for k in range(g1.shape[0]):
                for h in range(nh):
                    g1[k, h, pl.ds(at, TILE)] = zero

    @pl.when(has_x == 0)
    def _():
        for r in range(OFF - TILE, rows - OFF + TILE, TILE):
            for h in range(nh):
                g1[e, h, pl.ds(r, TILE)] = zero


def apply_second(sx, wx, wy, wz, sc, g1, w0, n0, lo, count, sums):
    _, nh, rows, _ = sx.shape
    lane = lax.broadcasted_iota(jnp.int32, (TILE, LANES), 1)
    inner, first = lane < LANES - 1, lane == 0

    def plane(k, sums):
        e = lo + k
        sums = list(sums)
        for r in range(OFF, rows - OFF, TILE):
            t = couple(g1, wx, wy, wz, e, r, nh, inner, first)
            for h in range(nh):
                s = sc[e, h, pl.ds(r, TILE)]
                a = s * sx[e, h, pl.ds(r, TILE)]
                b = w0[e, h, pl.ds(r, TILE)]
                c = b - s * t[h]
                n0[e, h, pl.ds(r, TILE)] = c
                for i, term in enumerate((a * a, b * a, b * b, c * b, c * a)):
                    sums[i] = sums[i] + term
        return tuple(sums)

    return lax.fori_loop(0, count, plane, tuple(sums))


def near_kernel(par, dens, src, near, rxs, rdg, dx, sx, wx, wy, wz, sc, g0, g1, w0, n0, mom):
    nx, ny, nz = dens.shape
    xodd, yodd = par[0] == 1, par[1] == 1
    has_near = jnp.where(xodd, par[2], par[3]) == 1
    has_down, has_up = par[4] == 1, par[5] == 1
    own = slice(OFF, OFF + ny)
    for k in range(nx):
        put_plane(dx, k + DEEP, own, 0.5 * dens[k])
        put_plane(sx, k + DEEP, own, src[k])
    beyond = jnp.where(xodd, 0, nx + 3)
    for k in range(3):
        put_plane(dx, beyond + k, own, jnp.where(has_near, 0.5 * near[k], 0.0))
    beyond = jnp.where(xodd, 1, nx + 3)
    for k in range(2):
        put_plane(sx, beyond + k, own, jnp.where(has_near, near[3 + k], 0.0))
    for k in range(nx + 2):
        a, b = rxs[k], rdg[k]
        low, high = jnp.where(yodd, a, b), jnp.where(yodd, b, a)
        inside = True if k < nx else has_near
        low = jnp.where(jnp.logical_and(has_down, inside), low, 0.0)
        high = jnp.where(jnp.logical_and(has_up, inside), high, 0.0)
        put_rows(dx, sx, k + DEEP if k < nx else beyond + k - nx, low, high, ny)
    weigh(dx, sx, wx, wy, wz, sc, g0, jnp.where(xodd, 1, 4), nx + 1)
    apply_first(sx, wx, wy, wz, sc, g0, g1, w0, jnp.where(xodd, 2, 5), nx - 1)
    clear_outside(par, g1, jnp.where(xodd, 2, nx + 3), jnp.where(xodd, par[2], par[3]))
    zero = jnp.zeros((TILE, LANES), jnp.float32)
    sums = apply_second(sx, wx, wy, wz, sc, g1, w0, n0, jnp.where(xodd, 3, 6), nx - 3, (zero,) * SUMS)
    for i in range(SUMS):
        mom[i] = sums[i]


def far_kernel(par, far, rfc, part, dx_in, sx_in, wx_in, wy_in, wz_in, sc_in, g0_in, g1_in, w0_in, n0_in,
               mom, dx, sx, wx, wy, wz, sc, g0, g1, w0, n0):
    ny, nz = far.shape[1:]
    nx = dx.shape[0] - 2 * DEEP
    xodd, yodd = par[0] == 1, par[1] == 1
    has = jnp.where(xodd, par[3], par[2])
    has_far = has == 1
    has_down, has_up = jnp.logical_and(has_far, par[4] == 1), jnp.logical_and(has_far, par[5] == 1)
    own = slice(OFF, OFF + ny)
    beyond = jnp.where(xodd, nx + 3, 0)
    for k in range(3):
        put_plane(dx, beyond + k, own, jnp.where(has_far, 0.5 * far[k], 0.0))
    beyond = jnp.where(xodd, nx + 3, 1)
    for k in range(2):
        put_plane(sx, beyond + k, own, jnp.where(has_far, far[3 + k], 0.0))
        a, b = rfc[k], rfc[2 + k]
        low, high = jnp.where(yodd, a, b), jnp.where(yodd, b, a)
        put_rows(dx, sx, beyond + k, jnp.where(has_down, low, 0.0), jnp.where(has_up, high, 0.0), ny)
    weigh(dx, sx, wx, wy, wz, sc, g0, jnp.where(xodd, nx + 2, 1), 3)
    apply_first(sx, wx, wy, wz, sc, g0, g1, w0, jnp.where(xodd, nx + 1, 2), 3)
    clear_outside(par, g1, jnp.where(xodd, nx + 3, 2), has)
    sums = apply_second(sx, wx, wy, wz, sc, g1, w0, n0, jnp.where(xodd, nx, 3), 3, [part[i] for i in range(SUMS)])
    place = lax.broadcasted_iota(jnp.int32, (1, LANES), 1) // PART
    out = jnp.zeros((1, LANES), jnp.float32)
    for k, v in enumerate(sums):
        p = jnp.sum(v, axis=0, keepdims=True)
        width = LANES // 2
        while width >= PART:
            p = p + pltpu.roll(p, width, 1)
            width //= 2
        out = jnp.where(place == k, p, out)
    mom[...] = out


def last_kernel(mom, sx, sc, w0, n0, p_out, r_out):
    place = lax.broadcasted_iota(jnp.int32, mom.shape, 1) // PART
    m = mom[...]

    def whole(v):
        return jnp.sum(jnp.sum(v, axis=0, keepdims=True), axis=1, keepdims=True)

    def lanes(k):
        return pltpu.roll(m, (LANES - k * PART) % LANES, 1) if k else m

    head = place == 0
    m0, m1, m2, m3, m4 = (jnp.where(head, lanes(k), 0.0) for k in range(SUMS))
    gamma0 = whole(m0)
    delta0 = whole(m1)
    a0 = gamma0 / delta0
    gamma1 = whole(m0 - a0 * (m1 + m1 - a0 * m2))
    delta1 = whole(m1 - a0 * (m4 + m2 - a0 * m3))
    b1 = gamma1 / gamma0
    a1 = gamma1 / (delta1 - b1 * gamma1 / a0)
    nx, ny, nz = p_out.shape
    a0, b1, a1 = (jnp.broadcast_to(v, (TILE, LANES)) for v in (a0, b1, a1))

    def plane(i, carry):
        e = i + DEEP
        for r in range(0, ny, TILE):
            for h, at in halves(nz):
                here = pl.ds(OFF + r, TILE)
                s = sc[e, h, here]
                r0 = s * sx[e, h, here]
                v0 = w0[e, h, here]
                r1 = r0 - a0 * v0
                along = (v0 - a0 * n0[e, h, here]) + b1 * v0
                direction = r1 + b1 * r0
                p_out[i, pl.ds(r, TILE), at] = s * (a0 * r0 + a1 * direction)
                r_out[i, pl.ds(r, TILE), at] = r1 - a1 * along
        return carry

    lax.fori_loop(0, nx, plane, 0)


def shards(nx_dev, ny_dev, source, density):
    both = ("gx", "gy")
    near_pairs, far_pairs, ynear_pairs, yfar_pairs = swaps(nx_dev, ny_dev)
    nx, ny, nz = density.shape
    ix, iy = lax.axis_index("gx"), lax.axis_index("gy")
    xodd = ix % 2
    flags = [xodd, iy % 2, ix > 0, ix < nx_dev - 1, iy > 0, iy < ny_dev - 1]
    par = jnp.stack([jnp.asarray(f, jnp.int32) for f in flags])
    smem = pl.BlockSpec(memory_space=pltpu.SMEM)
    vmem = pl.BlockSpec(memory_space=VMEM)

    def call(body, n_in, outs, limit, **more):
        specs = [smem] + [vmem] * (n_in - 1)
        return pl.pallas_call(
            body, out_shape=outs, in_specs=specs, out_specs=jax.tree.map(lambda _: vmem, outs), name=body.__name__,
            compiler_params=pltpu.CompilerParams(vmem_limit_bytes=limit * MIB), **more,
        )

    planes = VMEM((5, ny, nz), jnp.float32)
    near, far = call(take_planes, 3, (planes, planes), 8)(par, density, source)
    near = lax.ppermute(near, both, near_pairs)
    far = lax.ppermute(far, both, far_pairs)
    rows = VMEM((nx + 2, TILE, nz), jnp.float32)
    xs, dg = call(take_rows, 4, (rows, rows), 8)(par, density, source, near)
    rxs = lax.ppermute(xs, both, ynear_pairs)
    rdg = lax.ppermute(dg, both, yfar_pairs)
    begin = jnp.where(xodd == 1, nx - 2, 0)
    corner = jnp.concatenate([lax.dynamic_slice_in_dim(v, begin, 2, 0) for v in (rxs, rdg)], axis=0)
    rfc = lax.ppermute(corner, both, far_pairs)

    ext = VMEM((nx + 2 * DEEP, nz // LANES, ny + 2 * OFF, LANES), jnp.float32)
    *held, part = call(near_kernel, 6, (ext,) * 10 + (VMEM((SUMS, TILE, LANES), jnp.float32),), 8)(par, density, source, near, rxs, rdg)
    mom, *held = call(far_kernel, 14, (VMEM((1, LANES), jnp.float32),) + (ext,) * 10, 8, input_output_aliases={4 + k: 1 + k for k in range(10)})(
        par, far, rfc, part, *held)
    dx, sx, wx, wy, wz, sc, g0, g1, w0, n0 = held

    n = nx_dev * ny_dev
    sent = jnp.broadcast_to(mom[None], (n, 1, LANES))
    got = lax.all_to_all(sent, both, 0, 0, tiled=True).reshape(n, LANES)
    whole = jax.ShapeDtypeStruct(density.shape, jnp.float32)
    return pl.pallas_call(
        last_kernel, out_shape=(whole, whole), in_specs=[vmem] * 5, out_specs=(vmem, vmem), name="last_kernel",
        compiler_params=pltpu.CompilerParams(vmem_limit_bytes=8 * MIB),
    )(got, sx, sc, w0, n0)


def solution(mesh):
    spec = P("gx", "gy", None)
    body = functools.partial(shards, mesh.shape["gx"], mesh.shape["gy"])
    return jax.shard_map(body, mesh=mesh, in_specs=(spec, spec), out_specs=(spec, spec), check_vma=False)
```

```python
import functools

import jax
import jax.numpy as jnp
from jax import lax
from jax.experimental import pallas as pl
from jax.experimental.pallas import tpu as pltpu
from jax.sharding import PartitionSpec as P


TILE = 8
LANES = 128
OFF = 16
DEEP = 3
PART = 16
SUMS = 5
MIB = 1 << 20
VMEM = pltpu.VMEM


def swaps(nx, ny):
    at = lambda x, y: x * ny + y
    near, far, ynear, yfar = [], [], [], []
    for x in range(nx):
        for y in range(ny):
            near.append((at(x, y), at(x ^ 1, y)))
            other = x - 1 if x % 2 == 0 else x + 1
            inside = 0 <= other < nx
            far.append((at(x, y), at(other, y) if inside else at(x, y ^ 1)))
            ynear.append((at(x, y), at(x, y ^ 1)))
            beside = y - 1 if y % 2 == 0 else y + 1
            within = 0 <= beside < ny
            yfar.append((at(x, y), at(x, beside) if within else at(x ^ 1, y)))
    return near, far, ynear, yfar


def take_kernel(par, dens, src, near_out, far_out, xs_out, dg_out, dlo, dhi, slo, shi, sems):
    nx, ny, nz = dens.shape
    xodd, yodd = par[0] == 1, par[1] == 1
    copies = [
        (dens.at[:, pl.ds(0, TILE)], dlo), (dens.at[:, pl.ds(ny - TILE, TILE)], dhi),
        (src.at[:, pl.ds(0, TILE)], slo), (src.at[:, pl.ds(ny - TILE, TILE)], shi),
    ]
    for out, d, s in ((near_out, jnp.where(xodd, 0, nx - 3), jnp.where(xodd, 0, nx - 2)),
                      (far_out, jnp.where(xodd, nx - 3, 0), jnp.where(xodd, nx - 2, 0))):
        copies += [(dens.at[pl.ds(d + k, 1)], out.at[pl.ds(k, 1)]) for k in range(3)]
        copies += [(src.at[pl.ds(s + k, 1)], out.at[pl.ds(3 + k, 1)]) for k in range(2)]
    copies = [pltpu.make_async_copy(a, b, sems.at[i]) for i, (a, b) in enumerate(copies)]
    for copy in copies:
        copy.start()
    for copy in copies[:4]:
        copy.wait()
    row = lax.broadcasted_iota(jnp.int32, (TILE, nz), 0)
    for k in range(nx):
        down = jnp.where(row < 3, dlo[k], pltpu.roll(slo[k], 4, 0))
        up = jnp.where(row > 4, dhi[k], pltpu.roll(shi[k], 4, 0))
        xs_out[k] = jnp.where(yodd, down, up)
        dg_out[k] = jnp.where(yodd, up, down)
    for copy in copies[4:]:
        copy.wait()


def halves(nz):
    return [(h, slice(h * LANES, (h + 1) * LANES)) for h in range(nz // LANES)]


def put_plane(ref, e, rows, value):
    for h, lanes in halves(value.shape[-1]):
        ref[e, h, rows] = value[:, lanes]


def put_rows(dx, sx, e, low, high, ny):
    for value, at in ((low, slice(OFF - TILE, OFF)), (high, slice(OFF + ny, OFF + ny + TILE))):
        put_plane(dx, e, at, 0.5 * value)
        put_plane(sx, e, at, pltpu.roll(value, 4, 0))


def weigh(dx, sx, wx, wy, wz, sc, g0, lo, count):
    _, nh, rows, _ = dx.shape
    tiles = range(OFF - TILE, rows - OFF + TILE, TILE)
    lane = lax.broadcasted_iota(jnp.int32, (TILE, LANES), 1)
    inner, first = lane < LANES - 1, lane == 0
    for r in tiles:
        for h in range(nh):
            wx[lo - 1, h, pl.ds(r, TILE)] = 1.0 / (dx[lo - 1, h, pl.ds(r, TILE)] + dx[lo, h, pl.ds(r, TILE)])

    def plane(k, carry):
        e = lo + k
        for r in tiles:
            c = [dx[e, h, pl.ds(r, TILE)] for h in range(nh)]
            turned = [pltpu.roll(v, LANES - 1, 1) for v in c]
            z_up, z_in = [], []
            for h in range(nh):
                after = jnp.where(inner, turned[h], turned[h + 1] if h + 1 < nh else 0.0)
                w = 1.0 / (c[h] + after)
                z_up.append(w)
                z_in.append(w if h + 1 < nh else jnp.where(inner, w, 0.0))
                wz[e, h, pl.ds(r, TILE)] = z_in[h]
            back = [pltpu.roll(v, 1, 1) for v in z_in]
            for h in range(nh):
                x_up = 1.0 / (c[h] + dx[e + 1, h, pl.ds(r, TILE)])
                y_up = 1.0 / (c[h] + dx[e, h, pl.ds(r + 1, TILE)])
                wx[e, h, pl.ds(r, TILE)] = x_up
                wy[e, h, pl.ds(r, TILE)] = y_up
                z_down = jnp.where(first, back[h - 1] if h else 1.0 / c[0], back[h])
                y_down = 1.0 / (c[h] + dx[e, h, pl.ds(r - 1, TILE)])
                diag = (x_up + wx[e - 1, h, pl.ds(r, TILE)]) + (y_up + y_down) + (z_up[h] + z_down)
                s = lax.rsqrt(diag)
                sc[e, h, pl.ds(r, TILE)] = s
                g0[e, h, pl.ds(r, TILE)] = s * (s * sx[e, h, pl.ds(r, TILE)])
        return carry

    lax.fori_loop(0, count, plane, 0)


def couple(g, wx, wy, wz, e, r, nh, inner, first):
    here = pl.ds(r, TILE)
    c = [g[e, h, here] for h in range(nh)]
    w = [wz[e, h, here] for h in range(nh)]
    ahead = [pltpu.roll(v, LANES - 1, 1) for v in c]
    behind = [pltpu.roll(a * b, 1, 1) for a, b in zip(w, c)]
    out = []
    for h in range(nh):
        t = wx[e, h, here] * g[e + 1, h, here] + wx[e - 1, h, here] * g[e - 1, h, here]
        t = t + (wy[e, h, here] * g[e, h, pl.ds(r + 1, TILE)] + wy[e, h, pl.ds(r - 1, TILE)] * g[e, h, pl.ds(r - 1, TILE)])
        after = jnp.where(inner, ahead[h], ahead[h + 1]) if h + 1 < nh else ahead[h]
        before = jnp.where(first, behind[h - 1], behind[h])
        out.append(t + (w[h] * after + before))
    return out


def apply_first(sx, wx, wy, wz, sc, g0, g1, w0, lo, count):
    _, nh, rows, _ = sx.shape
    lane = lax.broadcasted_iota(jnp.int32, (TILE, LANES), 1)
    inner, first = lane < LANES - 1, lane == 0

    def plane(k, carry):
        e = lo + k
        for r in range(OFF - TILE, rows - OFF + TILE, TILE):
            t = couple(g0, wx, wy, wz, e, r, nh, inner, first)
            for h in range(nh):
                s = sc[e, h, pl.ds(r, TILE)]
                v = s * sx[e, h, pl.ds(r, TILE)] - s * t[h]
                w0[e, h, pl.ds(r, TILE)] = v
                g1[e, h, pl.ds(r, TILE)] = s * v
        return carry

    lax.fori_loop(0, count, plane, 0)


def clear_outside(par, g1, e, has_x):
    _, nh, rows, _ = g1.shape
    zero = jnp.zeros((TILE, LANES), jnp.float32)
    for flag, at in ((par[4], OFF - TILE), (par[5], rows - OFF)):

        @pl.when(flag == 0)
        def _():
            for k in range(g1.shape[0]):
                for h in range(nh):
                    g1[k, h, pl.ds(at, TILE)] = zero

    @pl.when(has_x == 0)
    def _():
        for r in range(OFF - TILE, rows - OFF + TILE, TILE):
            for h in range(nh):
                g1[e, h, pl.ds(r, TILE)] = zero


def apply_second(sx, wx, wy, wz, sc, g1, w0, n0, lo, count, sums):
    _, nh, rows, _ = sx.shape
    lane = lax.broadcasted_iota(jnp.int32, (TILE, LANES), 1)
    inner, first = lane < LANES - 1, lane == 0

    def plane(k, sums):
        e = lo + k
        sums = list(sums)
        for r in range(OFF, rows - OFF, TILE):
            t = couple(g1, wx, wy, wz, e, r, nh, inner, first)
            for h in range(nh):
                s = sc[e, h, pl.ds(r, TILE)]
                a = s * sx[e, h, pl.ds(r, TILE)]
                b = w0[e, h, pl.ds(r, TILE)]
                c = b - s * t[h]
                n0[e, h, pl.ds(r, TILE)] = c
                for i, term in enumerate((a * a, b * a, b * b, c * b, c * a)):
                    sums[i] = sums[i] + term
        return tuple(sums)

    return lax.fori_loop(0, count, plane, tuple(sums))


def near_kernel(par, dens, src, near, rxs, rdg, rnc, dx, sx, wx, wy, wz, sc, g0, g1, w0, n0, mom):
    nx, ny, _ = dens.shape
    xodd, yodd = par[0] == 1, par[1] == 1
    has_near = jnp.where(xodd, par[2], par[3]) == 1
    has_down, has_up = par[4] == 1, par[5] == 1
    own = slice(OFF, OFF + ny)
    for k in range(nx):
        put_plane(dx, k + DEEP, own, 0.5 * dens[k])
        put_plane(sx, k + DEEP, own, src[k])
    beyond = jnp.where(xodd, 0, nx + 3)
    for k in range(3):
        put_plane(dx, beyond + k, own, jnp.where(has_near, 0.5 * near[k], 0.0))
    beyond = jnp.where(xodd, 1, nx + 3)
    for k in range(2):
        put_plane(sx, beyond + k, own, jnp.where(has_near, near[3 + k], 0.0))
    for k in range(nx + 2):
        inside = True if k < nx else has_near
        a, b = (rxs[k], rdg[k]) if k < nx else (rnc[k - nx], rnc[2 + k - nx])
        low, high = jnp.where(yodd, a, b), jnp.where(yodd, b, a)
        low = jnp.where(jnp.logical_and(has_down, inside), low, 0.0)
        high = jnp.where(jnp.logical_and(has_up, inside), high, 0.0)
        put_rows(dx, sx, k + DEEP if k < nx else beyond + k - nx, low, high, ny)
    weigh(dx, sx, wx, wy, wz, sc, g0, jnp.where(xodd, 1, 4), nx + 1)
    apply_first(sx, wx, wy, wz, sc, g0, g1, w0, jnp.where(xodd, 2, 5), nx - 1)
    clear_outside(par, g1, jnp.where(xodd, 2, nx + 3), jnp.where(xodd, par[2], par[3]))
    zero = jnp.zeros((TILE, LANES), jnp.float32)
    sums = apply_second(sx, wx, wy, wz, sc, g1, w0, n0, jnp.where(xodd, 3, 6), nx - 3, (zero,) * SUMS)
    for i in range(SUMS):
        mom[i] = sums[i]


def far_kernel(par, far, rfc, part, dx_in, sx_in, wx_in, wy_in, wz_in, sc_in, g0_in, g1_in, w0_in, n0_in,
               mom, dx, sx, wx, wy, wz, sc, g0, g1, w0, n0):
    ny, _ = far.shape[1:]
    nx = dx.shape[0] - 2 * DEEP
    xodd, yodd = par[0] == 1, par[1] == 1
    has = jnp.where(xodd, par[3], par[2])
    has_far = has == 1
    has_down, has_up = jnp.logical_and(has_far, par[4] == 1), jnp.logical_and(has_far, par[5] == 1)
    own = slice(OFF, OFF + ny)
    beyond = jnp.where(xodd, nx + 3, 0)
    for k in range(3):
        put_plane(dx, beyond + k, own, jnp.where(has_far, 0.5 * far[k], 0.0))
    beyond = jnp.where(xodd, nx + 3, 1)
    for k in range(2):
        put_plane(sx, beyond + k, own, jnp.where(has_far, far[3 + k], 0.0))
        a, b = rfc[k], rfc[2 + k]
        low, high = jnp.where(yodd, a, b), jnp.where(yodd, b, a)
        put_rows(dx, sx, beyond + k, jnp.where(has_down, low, 0.0), jnp.where(has_up, high, 0.0), ny)
    weigh(dx, sx, wx, wy, wz, sc, g0, jnp.where(xodd, nx + 2, 1), 3)
    apply_first(sx, wx, wy, wz, sc, g0, g1, w0, jnp.where(xodd, nx + 1, 2), 3)
    clear_outside(par, g1, jnp.where(xodd, nx + 3, 2), has)
    sums = apply_second(sx, wx, wy, wz, sc, g1, w0, n0, jnp.where(xodd, nx, 3), 3, [part[i] for i in range(SUMS)])
    place = lax.broadcasted_iota(jnp.int32, (1, LANES), 1) // PART
    out = jnp.zeros((1, LANES), jnp.float32)
    for k, v in enumerate(sums):
        p = jnp.sum(v, axis=0, keepdims=True)
        width = LANES // 2
        while width >= PART:
            p = p + pltpu.roll(p, width, 1)
            width //= 2
        out = jnp.where(place == k, p, out)
    mom[...] = out


def last_kernel(mom, sx, sc, w0, n0, p_out, r_out, p_buf, r_buf, sems):
    place = lax.broadcasted_iota(jnp.int32, mom.shape, 1) // PART
    m = mom[...]

    def whole(v):
        return jnp.sum(jnp.sum(v, axis=0, keepdims=True), axis=1, keepdims=True)

    def lanes(k):
        return pltpu.roll(m, (LANES - k * PART) % LANES, 1) if k else m

    head = place == 0
    m0, m1, m2, m3, m4 = (jnp.where(head, lanes(k), 0.0) for k in range(SUMS))
    gamma0 = whole(m0)
    delta0 = whole(m1)
    a0 = gamma0 / delta0
    gamma1 = whole(m0 - a0 * (m1 + m1 - a0 * m2))
    delta1 = whole(m1 - a0 * (m4 + m2 - a0 * m3))
    b1 = gamma1 / gamma0
    a1 = gamma1 / (delta1 - b1 * gamma1 / a0)
    nx, ny, nz = p_out.shape
    c = jnp.broadcast_to(a0 + (a1 + a1 * b1), (TILE, LANES))
    d = jnp.broadcast_to(a0 * a1, (TILE, LANES))

    def out(i):
        return (pltpu.make_async_copy(p_buf.at[pl.ds(i, 1)], p_out.at[pl.ds(i, 1)], sems.at[0, i]),
                pltpu.make_async_copy(r_buf.at[pl.ds(i, 1)], r_out.at[pl.ds(i, 1)], sems.at[1, i]))

    def plane(i, carry):
        e = i + DEEP
        for r in range(0, ny, TILE):
            for h, at in halves(nz):
                here = pl.ds(OFF + r, TILE)
                s = sc[e, h, here]
                r0 = s * sx[e, h, here]
                v0 = w0[e, h, here]
                p_buf[i, pl.ds(r, TILE), at] = s * (c * r0 - d * v0)
                r_buf[i, pl.ds(r, TILE), at] = r0 - c * v0 + d * n0[e, h, here]
        for copy in out(i):
            copy.start()
        return carry

    lax.fori_loop(0, nx, plane, 0)
    for i in range(nx):
        for copy in out(i):
            copy.wait()


def shards(nx_dev, ny_dev, source, density):
    both = ("gx", "gy")
    near_pairs, far_pairs, ynear_pairs, yfar_pairs = swaps(nx_dev, ny_dev)
    nx, ny, nz = density.shape
    ix, iy = lax.axis_index("gx"), lax.axis_index("gy")
    xodd = ix % 2
    flags = [xodd, iy % 2, ix > 0, ix < nx_dev - 1, iy > 0, iy < ny_dev - 1]
    par = jnp.stack([jnp.asarray(f, jnp.int32) for f in flags])
    smem = pl.BlockSpec(memory_space=pltpu.SMEM)
    vmem = pl.BlockSpec(memory_space=VMEM)

    def call(body, n_in, outs, limit, **more):
        specs = [smem] + [vmem] * (n_in - 1)
        return pl.pallas_call(
            body, out_shape=outs, in_specs=specs, out_specs=jax.tree.map(lambda _: vmem, outs),
            compiler_params=pltpu.CompilerParams(vmem_limit_bytes=limit * MIB), **more,
        )

    hbm = pl.BlockSpec(memory_space=pltpu.HBM)

    def send(value, pairs):
        return lax.ppermute(value, both, pairs)

    planes, rows = VMEM((5, ny, nz), jnp.float32), VMEM((nx, TILE, nz), jnp.float32)
    near, far, xs, dg = pl.pallas_call(
        take_kernel, out_shape=(planes, planes, rows, rows), in_specs=[smem, hbm, hbm], out_specs=(vmem,) * 4,
        scratch_shapes=[rows] * 4 + [pltpu.SemaphoreType.DMA((14,))], name="take_kernel",
        compiler_params=pltpu.CompilerParams(vmem_limit_bytes=8 * MIB),
    )(par, *(pltpu.with_memory_space_constraint(v, pltpu.HBM) for v in (density, source)))
    near = send(near, near_pairs)
    rxs = send(xs, ynear_pairs)
    rdg = send(dg, yfar_pairs)
    far = send(far, far_pairs)

    def corner(begin):
        return jnp.concatenate([lax.dynamic_slice_in_dim(v, begin, 2, 0) for v in (rxs, rdg)], axis=0)

    rfc = send(corner(jnp.where(xodd == 1, nx - 2, 0)), far_pairs)
    rnc = send(corner(jnp.where(xodd == 1, 0, nx - 2)), near_pairs)

    ext = VMEM((nx + 2 * DEEP, nz // LANES, ny + 2 * OFF, LANES), jnp.float32)
    *held, part = call(near_kernel, 7, (ext,) * 10 + (VMEM((SUMS, TILE, LANES), jnp.float32),), 8)(par, density, source, near, rxs, rdg, rnc)
    mom, *held = call(far_kernel, 14, (VMEM((1, LANES), jnp.float32),) + (ext,) * 10, 8, input_output_aliases={4 + k: 1 + k for k in range(10)})(
        par, far, rfc, part, *held)
    _, sx, _, _, _, sc, _, _, w0, n0 = held

    n = nx_dev * ny_dev
    sent = jnp.broadcast_to(mom[None], (n, 1, LANES))
    got = lax.all_to_all(sent, both, 0, 0, tiled=True).reshape(n, LANES)
    whole = jax.ShapeDtypeStruct(density.shape, jnp.float32)
    plane = VMEM(density.shape, jnp.float32)
    return pl.pallas_call(
        last_kernel, out_shape=(whole, whole), in_specs=[vmem] * 5, out_specs=(hbm, hbm), name="last_kernel",
        scratch_shapes=[plane, plane, pltpu.SemaphoreType.DMA((2, nx))],
        compiler_params=pltpu.CompilerParams(vmem_limit_bytes=8 * MIB),
    )(got, sx, sc, w0, n0)


def solution(mesh):
    spec = P("gx", "gy", None)
    body = functools.partial(shards, mesh.shape["gx"], mesh.shape["gy"])
    return jax.shard_map(body, mesh=mesh, in_specs=(spec, spec), out_specs=(spec, spec), check_vma=False)
```

```python
import functools

import jax
import jax.numpy as jnp
from jax import lax
from jax.experimental import pallas as pl
from jax.experimental.pallas import tpu as pltpu
from jax.sharding import PartitionSpec as P


TILE = 8
LANES = 128
OFF = 16
DEEP = 3
PART = 16
SUMS = 5
MIB = 1 << 20
VMEM = pltpu.VMEM


def swaps(nx, ny):
    at = lambda x, y: x * ny + y
    near, far, ynear, yfar = [], [], [], []
    for x in range(nx):
        for y in range(ny):
            near.append((at(x, y), at(x ^ 1, y)))
            other = x - 1 if x % 2 == 0 else x + 1
            inside = 0 <= other < nx
            far.append((at(x, y), at(other, y) if inside else at(x, (y + ny // 2) % ny)))
            ynear.append((at(x, y), at(x, y ^ 1)))
            beside = y - 1 if y % 2 == 0 else y + 1
            within = 0 <= beside < ny
            yfar.append((at(x, y), at(x, beside) if within else at(x ^ 1, y)))
    return near, far, ynear, yfar


def take_kernel(par, dens, src, far_out, near_out, xs_out, dg_out, dlo, dhi, slo, shi, far_buf, near_buf, xs_buf, dg_buf, sems, out_sems):
    nx, ny, nz = dens.shape
    xodd, yodd = par[0] == 1, par[1] == 1
    moves = []
    for buf, out, d, s in ((far_buf, far_out, jnp.where(xodd, nx - 3, 0), jnp.where(xodd, nx - 2, 0)),
                           (near_buf, near_out, jnp.where(xodd, 0, nx - 3), jnp.where(xodd, 0, nx - 2))):
        for ref, first, count, at in ((dens, d, 3, 0), (src, s, 2, 3)):
            for k in range(count):
                here = pl.ds(at + k, 1)
                moves.append((ref.at[pl.ds(first + k, 1)], buf.at[here], out.at[here]))
    slabs = [(dens.at[:, pl.ds(0, TILE)], dlo), (dens.at[:, pl.ds(ny - TILE, TILE)], dhi),
             (src.at[:, pl.ds(0, TILE)], slo), (src.at[:, pl.ds(ny - TILE, TILE)], shi)]
    slabs = [pltpu.make_async_copy(a, b, sems.at[len(moves) + i]) for i, (a, b) in enumerate(slabs)]
    reads = [pltpu.make_async_copy(a, b, sems.at[i]) for i, (a, b, _) in enumerate(moves)]
    writes = [pltpu.make_async_copy(b, c, out_sems.at[i]) for i, (_, b, c) in enumerate(moves)]
    writes += [pltpu.make_async_copy(b, c, out_sems.at[len(moves) + i]) for i, (b, c) in enumerate(((xs_buf, xs_out), (dg_buf, dg_out)))]
    for copy in slabs + reads:
        copy.start()
    for copy in slabs:
        copy.wait()
    row = lax.broadcasted_iota(jnp.int32, (TILE, nz), 0)
    for k in range(nx):
        down = jnp.where(row < 3, dlo[k], pltpu.roll(slo[k], 4, 0))
        up = jnp.where(row > 4, dhi[k], pltpu.roll(shi[k], 4, 0))
        xs_buf[k] = jnp.where(yodd, down, up)
        dg_buf[k] = jnp.where(yodd, up, down)
    for copy in writes[len(moves):]:
        copy.start()
    for read, write in zip(reads, writes):
        read.wait()
        write.start()
    for copy in writes:
        copy.wait()


def halves(nz):
    return [(h, slice(h * LANES, (h + 1) * LANES)) for h in range(nz // LANES)]


def put_plane(ref, e, rows, value):
    for h, lanes in halves(value.shape[-1]):
        ref[e, h, rows] = value[:, lanes]


def put_rows(dx, sx, e, low, high, ny):
    for value, at in ((low, slice(OFF - TILE, OFF)), (high, slice(OFF + ny, OFF + ny + TILE))):
        put_plane(dx, e, at, 0.5 * value)
        put_plane(sx, e, at, pltpu.roll(value, 4, 0))


def weigh(dx, sx, wx, wy, wz, sc, g0, lo, count, tiles):
    nh = dx.shape[1]
    lane = lax.broadcasted_iota(jnp.int32, (TILE, LANES), 1)
    inner, first = lane < LANES - 1, lane == 0
    for r in tiles:
        for h in range(nh):
            wx[lo - 1, h, pl.ds(r, TILE)] = 1.0 / (dx[lo - 1, h, pl.ds(r, TILE)] + dx[lo, h, pl.ds(r, TILE)])

    def plane(k, carry):
        e = lo + k
        for r in tiles:
            c = [dx[e, h, pl.ds(r, TILE)] for h in range(nh)]
            turned = [pltpu.roll(v, LANES - 1, 1) for v in c]
            z_up, z_in = [], []
            for h in range(nh):
                after = jnp.where(inner, turned[h], turned[h + 1] if h + 1 < nh else 0.0)
                w = 1.0 / (c[h] + after)
                z_up.append(w)
                z_in.append(w if h + 1 < nh else jnp.where(inner, w, 0.0))
                wz[e, h, pl.ds(r, TILE)] = z_in[h]
            back = [pltpu.roll(v, 1, 1) for v in z_in]
            for h in range(nh):
                x_up = 1.0 / (c[h] + dx[e + 1, h, pl.ds(r, TILE)])
                y_up = 1.0 / (c[h] + dx[e, h, pl.ds(r + 1, TILE)])
                wx[e, h, pl.ds(r, TILE)] = x_up
                wy[e, h, pl.ds(r, TILE)] = y_up
                z_down = jnp.where(first, back[h - 1] if h else 1.0 / c[0], back[h])
                y_down = 1.0 / (c[h] + dx[e, h, pl.ds(r - 1, TILE)])
                diag = (x_up + wx[e - 1, h, pl.ds(r, TILE)]) + (y_up + y_down) + (z_up[h] + z_down)
                s = lax.rsqrt(diag)
                sc[e, h, pl.ds(r, TILE)] = s
                g0[e, h, pl.ds(r, TILE)] = s * (s * sx[e, h, pl.ds(r, TILE)])
        return carry

    lax.fori_loop(0, count, plane, 0)


def couple(g, wx, wy, wz, e, r, nh, inner, first):
    here = pl.ds(r, TILE)
    c = [g[e, h, here] for h in range(nh)]
    w = [wz[e, h, here] for h in range(nh)]
    ahead = [pltpu.roll(v, LANES - 1, 1) for v in c]
    behind = [pltpu.roll(a * b, 1, 1) for a, b in zip(w, c)]
    out = []
    for h in range(nh):
        t = wx[e, h, here] * g[e + 1, h, here] + wx[e - 1, h, here] * g[e - 1, h, here]
        t = t + (wy[e, h, here] * g[e, h, pl.ds(r + 1, TILE)] + wy[e, h, pl.ds(r - 1, TILE)] * g[e, h, pl.ds(r - 1, TILE)])
        after = jnp.where(inner, ahead[h], ahead[h + 1]) if h + 1 < nh else ahead[h]
        before = jnp.where(first, behind[h - 1], behind[h])
        out.append(t + (w[h] * after + before))
    return out


def apply_first(sx, wx, wy, wz, sc, g0, g1, w0, lo, count, tiles):
    nh = sx.shape[1]
    lane = lax.broadcasted_iota(jnp.int32, (TILE, LANES), 1)
    inner, first = lane < LANES - 1, lane == 0

    def plane(k, carry):
        e = lo + k
        for r in tiles:
            t = couple(g0, wx, wy, wz, e, r, nh, inner, first)
            for h in range(nh):
                s = sc[e, h, pl.ds(r, TILE)]
                v = s * sx[e, h, pl.ds(r, TILE)] - s * t[h]
                w0[e, h, pl.ds(r, TILE)] = v
                g1[e, h, pl.ds(r, TILE)] = s * v
        return carry

    lax.fori_loop(0, count, plane, 0)


def clear_rows(par, g1):
    _, nh, rows, _ = g1.shape
    zero = jnp.zeros((TILE, LANES), jnp.float32)
    for flag, at in ((par[4], OFF - TILE), (par[5], rows - OFF)):

        @pl.when(flag == 0)
        def _():
            for k in range(g1.shape[0]):
                for h in range(nh):
                    g1[k, h, pl.ds(at, TILE)] = zero


def clear_plane(g1, e, has, tiles):
    zero = jnp.zeros((TILE, LANES), jnp.float32)

    @pl.when(has == 0)
    def _():
        for r in tiles:
            for h in range(g1.shape[1]):
                g1[e, h, pl.ds(r, TILE)] = zero


def apply_second(sx, wx, wy, wz, sc, g1, w0, n0, lo, count, tiles, sums):
    nh = sx.shape[1]
    lane = lax.broadcasted_iota(jnp.int32, (TILE, LANES), 1)
    inner, first = lane < LANES - 1, lane == 0

    def plane(k, sums):
        e = lo + k
        sums = list(sums)
        for r in tiles:
            t = couple(g1, wx, wy, wz, e, r, nh, inner, first)
            for h in range(nh):
                s = sc[e, h, pl.ds(r, TILE)]
                a = s * sx[e, h, pl.ds(r, TILE)]
                b = w0[e, h, pl.ds(r, TILE)]
                c = b - s * t[h]
                n0[e, h, pl.ds(r, TILE)] = c
                for i, term in enumerate((a * a, b * a, b * b, c * b, c * a)):
                    sums[i] = sums[i] + term
        return tuple(sums)

    return lax.fori_loop(0, count, plane, tuple(sums))


def row_tiles(ny, inset):
    return list(range(OFF + inset * TILE, OFF + ny - inset * TILE, TILE))


def outer_tiles(ny, reach, inset):
    inside = row_tiles(ny, inset)
    return [r for r in row_tiles(ny, -reach) if r not in inside]


def near_side(par):
    xodd = par[0] == 1
    return jnp.where(xodd, 1, 4), jnp.where(xodd, 2, 5), jnp.where(xodd, 3, 6), jnp.where(xodd, par[2], par[3])


def inner_kernel(par, dens, src, near, dx, sx, wx, wy, wz, sc, g0, g1, w0, n0, mom):
    nx, ny, _ = dens.shape
    xodd = par[0] == 1
    first, second, third, has = near_side(par)
    has_near = has == 1
    own = slice(OFF, OFF + ny)
    for k in range(nx):
        put_plane(dx, k + DEEP, own, 0.5 * dens[k])
        put_plane(sx, k + DEEP, own, src[k])
    beyond = jnp.where(xodd, 0, nx + 3)
    for k in range(3):
        put_plane(dx, beyond + k, own, jnp.where(has_near, 0.5 * near[k], 0.0))
    beyond = jnp.where(xodd, 1, nx + 3)
    for k in range(2):
        put_plane(sx, beyond + k, own, jnp.where(has_near, near[3 + k], 0.0))
    weigh(dx, sx, wx, wy, wz, sc, g0, first, nx + 1, row_tiles(ny, 1))
    apply_first(sx, wx, wy, wz, sc, g0, g1, w0, second, nx - 1, row_tiles(ny, 2))
    clear_plane(g1, jnp.where(xodd, 2, nx + 3), has, row_tiles(ny, 2))
    zero = jnp.zeros((TILE, LANES), jnp.float32)
    sums = apply_second(sx, wx, wy, wz, sc, g1, w0, n0, third, nx - 3, row_tiles(ny, 3), (zero,) * SUMS)
    for i in range(SUMS):
        mom[i] = sums[i]


def edge_kernel(par, rxs, rdg, rnc, part, *refs):
    mom, dx, sx, wx, wy, wz, sc, g0, g1, w0, n0 = refs[10:]
    nx = dx.shape[0] - 2 * DEEP
    ny = dx.shape[2] - 2 * OFF
    xodd, yodd = par[0] == 1, par[1] == 1
    first, second, third, has = near_side(par)
    has_near, has_down, has_up = has == 1, par[4] == 1, par[5] == 1
    beyond = jnp.where(xodd, 1, nx + 3)
    for k in range(nx + 2):
        inside = True if k < nx else has_near
        a, b = (rxs[k], rdg[k]) if k < nx else (rnc[k - nx], rnc[2 + k - nx])
        low, high = jnp.where(yodd, a, b), jnp.where(yodd, b, a)
        low = jnp.where(jnp.logical_and(has_down, inside), low, 0.0)
        high = jnp.where(jnp.logical_and(has_up, inside), high, 0.0)
        put_rows(dx, sx, k + DEEP if k < nx else beyond + k - nx, low, high, ny)
    weigh(dx, sx, wx, wy, wz, sc, g0, first, nx + 1, outer_tiles(ny, 1, 1))
    apply_first(sx, wx, wy, wz, sc, g0, g1, w0, second, nx - 1, outer_tiles(ny, 1, 2))
    clear_plane(g1, jnp.where(xodd, 2, nx + 3), has, outer_tiles(ny, 1, 2))
    clear_rows(par, g1)
    sums = apply_second(sx, wx, wy, wz, sc, g1, w0, n0, third, nx - 3, outer_tiles(ny, 0, 3), [part[i] for i in range(SUMS)])
    for i in range(SUMS):
        mom[i] = sums[i]


def far_kernel(par, far, rfc, part, dx_in, sx_in, wx_in, wy_in, wz_in, sc_in, g0_in, g1_in, w0_in, n0_in,
               mom, dx, sx, wx, wy, wz, sc, g0, g1, w0, n0):
    ny, _ = far.shape[1:]
    nx = dx.shape[0] - 2 * DEEP
    xodd, yodd = par[0] == 1, par[1] == 1
    has = jnp.where(xodd, par[3], par[2])
    has_far = has == 1
    has_down, has_up = jnp.logical_and(has_far, par[4] == 1), jnp.logical_and(has_far, par[5] == 1)
    own = slice(OFF, OFF + ny)
    beyond = jnp.where(xodd, nx + 3, 0)
    for k in range(3):
        put_plane(dx, beyond + k, own, jnp.where(has_far, 0.5 * far[k], 0.0))
    beyond = jnp.where(xodd, nx + 3, 1)
    for k in range(2):
        put_plane(sx, beyond + k, own, jnp.where(has_far, far[3 + k], 0.0))
        a, b = rfc[k], rfc[2 + k]
        low, high = jnp.where(yodd, a, b), jnp.where(yodd, b, a)
        put_rows(dx, sx, beyond + k, jnp.where(has_down, low, 0.0), jnp.where(has_up, high, 0.0), ny)
    weigh(dx, sx, wx, wy, wz, sc, g0, jnp.where(xodd, nx + 2, 1), 3, row_tiles(ny, -1))
    apply_first(sx, wx, wy, wz, sc, g0, g1, w0, jnp.where(xodd, nx + 1, 2), 3, row_tiles(ny, -1))
    clear_plane(g1, jnp.where(xodd, nx + 3, 2), has, row_tiles(ny, -1))
    clear_rows(par, g1)
    sums = apply_second(sx, wx, wy, wz, sc, g1, w0, n0, jnp.where(xodd, nx, 3), 3, row_tiles(ny, 0), [part[i] for i in range(SUMS)])
    place = lax.broadcasted_iota(jnp.int32, (1, LANES), 1) // PART
    out = jnp.zeros((1, LANES), jnp.float32)
    for k, v in enumerate(sums):
        p = jnp.sum(v, axis=0, keepdims=True)
        width = LANES // 2
        while width >= PART:
            p = p + pltpu.roll(p, width, 1)
            width //= 2
        out = jnp.where(place == k, p, out)
    mom[...] = out


def last_kernel(mom, sx, sc, w0, n0, p_out, r_out, p_buf, r_buf, sems):
    place = lax.broadcasted_iota(jnp.int32, mom.shape, 1) // PART
    m = mom[...]

    def whole(v):
        return jnp.sum(jnp.sum(v, axis=0, keepdims=True), axis=1, keepdims=True)

    def lanes(k):
        return pltpu.roll(m, (LANES - k * PART) % LANES, 1) if k else m

    head = place == 0
    m0, m1, m2, m3, m4 = (jnp.where(head, lanes(k), 0.0) for k in range(SUMS))
    gamma0 = whole(m0)
    delta0 = whole(m1)
    a0 = gamma0 / delta0
    gamma1 = whole(m0 - a0 * (m1 + m1 - a0 * m2))
    delta1 = whole(m1 - a0 * (m4 + m2 - a0 * m3))
    b1 = gamma1 / gamma0
    a1 = gamma1 / (delta1 - b1 * gamma1 / a0)
    nx, ny, nz = p_out.shape
    c = jnp.broadcast_to(a0 + (a1 + a1 * b1), (TILE, LANES))
    d = jnp.broadcast_to(a0 * a1, (TILE, LANES))

    def out(i):
        return (pltpu.make_async_copy(p_buf.at[pl.ds(i, 1)], p_out.at[pl.ds(i, 1)], sems.at[0, i]),
                pltpu.make_async_copy(r_buf.at[pl.ds(i, 1)], r_out.at[pl.ds(i, 1)], sems.at[1, i]))

    def plane(i, carry):
        e = i + DEEP
        for r in range(0, ny, TILE):
            for h, at in halves(nz):
                here = pl.ds(OFF + r, TILE)
                s = sc[e, h, here]
                r0 = s * sx[e, h, here]
                v0 = w0[e, h, here]
                p_buf[i, pl.ds(r, TILE), at] = s * (c * r0 - d * v0)
                r_buf[i, pl.ds(r, TILE), at] = r0 - c * v0 + d * n0[e, h, here]
        for copy in out(i):
            copy.start()
        return carry

    lax.fori_loop(0, nx, plane, 0)
    for i in range(nx):
        for copy in out(i):
            copy.wait()


def shards(nx_dev, ny_dev, source, density):
    both = ("gx", "gy")
    near_pairs, far_pairs, ynear_pairs, yfar_pairs = swaps(nx_dev, ny_dev)
    nx, ny, nz = density.shape
    ix, iy = lax.axis_index("gx"), lax.axis_index("gy")
    xodd = ix % 2
    flags = [xodd, iy % 2, ix > 0, ix < nx_dev - 1, iy > 0, iy < ny_dev - 1]
    par = jnp.stack([jnp.asarray(f, jnp.int32) for f in flags])
    smem = pl.BlockSpec(memory_space=pltpu.SMEM)
    vmem = pl.BlockSpec(memory_space=VMEM)

    def call(body, n_in, outs, limit, **more):
        specs = [smem] + [vmem] * (n_in - 1)
        return pl.pallas_call(
            body, out_shape=outs, in_specs=specs, out_specs=jax.tree.map(lambda _: vmem, outs),
            compiler_params=pltpu.CompilerParams(vmem_limit_bytes=limit * MIB), **more,
        )

    hbm = pl.BlockSpec(memory_space=pltpu.HBM)

    def send(value, pairs):
        return lax.ppermute(value, both, pairs)

    planes, rows = ((5, ny, nz), jnp.float32), ((nx, TILE, nz), jnp.float32)
    shapes = (planes, planes, rows, rows)
    far, near, xs, dg = pl.pallas_call(
        take_kernel, out_shape=tuple(jax.ShapeDtypeStruct(*v) for v in shapes), in_specs=[smem, hbm, hbm], out_specs=(hbm,) * 4,
        scratch_shapes=[VMEM(*rows)] * 4 + [VMEM(*v) for v in shapes] + [pltpu.SemaphoreType.DMA((14,)), pltpu.SemaphoreType.DMA((12,))],
        name="take_kernel", compiler_params=pltpu.CompilerParams(vmem_limit_bytes=8 * MIB),
    )(par, *(pltpu.with_memory_space_constraint(v, pltpu.HBM) for v in (density, source)))
    near = send(near, near_pairs)
    rxs = send(xs, ynear_pairs)
    rdg = send(dg, yfar_pairs)
    far = send(far, far_pairs)

    def corner(begin):
        return jnp.concatenate([lax.dynamic_slice_in_dim(v, begin, 2, 0) for v in (rxs, rdg)], axis=0)

    rfc = send(corner(jnp.where(xodd == 1, nx - 2, 0)), far_pairs)
    rnc = send(corner(jnp.where(xodd == 1, 0, nx - 2)), near_pairs)

    ext = VMEM((nx + 2 * DEEP, nz // LANES, ny + 2 * OFF, LANES), jnp.float32)
    sums = VMEM((SUMS, TILE, LANES), jnp.float32)
    *held, part = call(inner_kernel, 4, (ext,) * 10 + (sums,), 8)(par, density, source, near)
    part, *held = call(edge_kernel, 15, (sums,) + (ext,) * 10, 8, input_output_aliases={5 + k: 1 + k for k in range(10)})(
        par, rxs, rdg, rnc, part, *held)
    mom, *held = call(far_kernel, 14, (VMEM((1, LANES), jnp.float32),) + (ext,) * 10, 8, input_output_aliases={4 + k: 1 + k for k in range(10)})(
        par, far, rfc, part, *held)
    _, sx, _, _, _, sc, _, _, w0, n0 = held

    n = nx_dev * ny_dev
    sent = jnp.broadcast_to(mom[None], (n, 1, LANES))
    got = lax.all_to_all(sent, both, 0, 0, tiled=True).reshape(n, LANES)
    whole = jax.ShapeDtypeStruct(density.shape, jnp.float32)
    plane = VMEM(density.shape, jnp.float32)
    return pl.pallas_call(
        last_kernel, out_shape=(whole, whole), in_specs=[vmem] * 5, out_specs=(hbm, hbm), name="last_kernel",
        scratch_shapes=[plane, plane, pltpu.SemaphoreType.DMA((2, nx))],
        compiler_params=pltpu.CompilerParams(vmem_limit_bytes=8 * MIB),
    )(got, sx, sc, w0, n0)


def solution(mesh):
    spec = P("gx", "gy", None)
    body = functools.partial(shards, mesh.shape["gx"], mesh.shape["gy"])
    return jax.shard_map(body, mesh=mesh, in_specs=(spec, spec), out_specs=(spec, spec), check_vma=False)
```

```python
import functools

import jax
import jax.numpy as jnp
from jax import lax
from jax.experimental import pallas as pl
from jax.experimental.pallas import tpu as pltpu
from jax.sharding import PartitionSpec as P


TILE = 8
LANES = 128
OFF = 16
DEEP = 3
PART = 16
SUMS = 5
MIB = 1 << 20
VMEM = pltpu.VMEM


def swaps(nx, ny):
    at = lambda x, y: x * ny + y
    near, far, ynear, yfar = [], [], [], []
    for x in range(nx):
        for y in range(ny):
            near.append((at(x, y), at(x ^ 1, y)))
            other = x - 1 if x % 2 == 0 else x + 1
            inside = 0 <= other < nx
            far.append((at(x, y), at(other, y) if inside else at(x, (y + ny // 2) % ny)))
            ynear.append((at(x, y), at(x, y ^ 1)))
            beside = y - 1 if y % 2 == 0 else y + 1
            within = 0 <= beside < ny
            yfar.append((at(x, y), at(x, beside) if within else at(x ^ 1, y)))
    return near, far, ynear, yfar


def position(sizes):
    ix, iy = lax.axis_index("gx"), lax.axis_index("gy")
    flags = (ix % 2 == 1, iy % 2 == 1, ix > 0, ix < sizes[0] - 1, iy > 0, iy < sizes[1] - 1)
    return [jnp.where(f, 1, 0) for f in flags]


def load_kernel(sizes, dens_hbm, src_hbm, far, near, xs, dg, dens, src, sems):
    par = position(sizes)
    nx, ny, nz = dens.shape
    xodd, yodd = par[0] == 1, par[1] == 1
    copies = []
    for k in range(nx):
        for i, (a, b) in enumerate(((dens_hbm, dens), (src_hbm, src))):
            copies.append(pltpu.make_async_copy(a.at[pl.ds(k, 1)], b.at[pl.ds(k, 1)], sems.at[2 * k + i]))
    for copy in copies:
        copy.start()
    for copy in copies:
        copy.wait()
    for out, d, s in ((far, jnp.where(xodd, nx - 3, 0), jnp.where(xodd, nx - 2, 0)),
                      (near, jnp.where(xodd, 0, nx - 3), jnp.where(xodd, 0, nx - 2))):
        for k in range(3):
            out[k] = dens[d + k]
        for k in range(2):
            out[3 + k] = src[s + k]
    row = lax.broadcasted_iota(jnp.int32, (TILE, nz), 0)
    for k in range(nx):
        down = jnp.where(row < 3, dens[k, :TILE], pltpu.roll(src[k, :TILE], 4, 0))
        up = jnp.where(row > 4, dens[k, ny - TILE:], pltpu.roll(src[k, ny - TILE:], 4, 0))
        xs[k] = jnp.where(yodd, down, up)
        dg[k] = jnp.where(yodd, up, down)


def corner_kernel(sizes, rxs, rdg, far, near):
    xodd = position(sizes)[0] == 1
    nx = rxs.shape[0]
    for out, begin in ((far, jnp.where(xodd, nx - 2, 0)), (near, jnp.where(xodd, 0, nx - 2))):
        for k in range(2):
            out[k] = rxs[begin + k]
            out[2 + k] = rdg[begin + k]


def halves(nz):
    return [(h, slice(h * LANES, (h + 1) * LANES)) for h in range(nz // LANES)]


def put_plane(ref, e, rows, value):
    for h, lanes in halves(value.shape[-1]):
        ref[e, h, rows] = value[:, lanes]


def put_rows(dx, sx, e, low, high, ny):
    for value, at in ((low, slice(OFF - TILE, OFF)), (high, slice(OFF + ny, OFF + ny + TILE))):
        put_plane(dx, e, at, 0.5 * value)
        put_plane(sx, e, at, pltpu.roll(value, 4, 0))


def weigh(dx, sx, wx, wy, wz, sc, g0, lo, count, tiles):
    nh = dx.shape[1]
    lane = lax.broadcasted_iota(jnp.int32, (TILE, LANES), 1)
    inner, first = lane < LANES - 1, lane == 0
    for r in tiles:
        for h in range(nh):
            wx[lo - 1, h, pl.ds(r, TILE)] = 1.0 / (dx[lo - 1, h, pl.ds(r, TILE)] + dx[lo, h, pl.ds(r, TILE)])

    def plane(k, carry):
        e = lo + k
        for r in tiles:
            c = [dx[e, h, pl.ds(r, TILE)] for h in range(nh)]
            turned = [pltpu.roll(v, LANES - 1, 1) for v in c]
            z_up, z_in = [], []
            for h in range(nh):
                after = jnp.where(inner, turned[h], turned[h + 1] if h + 1 < nh else 0.0)
                w = 1.0 / (c[h] + after)
                z_up.append(w)
                z_in.append(w if h + 1 < nh else jnp.where(inner, w, 0.0))
                wz[e, h, pl.ds(r, TILE)] = z_in[h]
            back = [pltpu.roll(v, 1, 1) for v in z_in]
            for h in range(nh):
                x_up = 1.0 / (c[h] + dx[e + 1, h, pl.ds(r, TILE)])
                y_up = 1.0 / (c[h] + dx[e, h, pl.ds(r + 1, TILE)])
                wx[e, h, pl.ds(r, TILE)] = x_up
                wy[e, h, pl.ds(r, TILE)] = y_up
                z_down = jnp.where(first, back[h - 1] if h else 1.0 / c[0], back[h])
                y_down = 1.0 / (c[h] + dx[e, h, pl.ds(r - 1, TILE)])
                diag = (x_up + wx[e - 1, h, pl.ds(r, TILE)]) + (y_up + y_down) + (z_up[h] + z_down)
                s = lax.rsqrt(diag)
                sc[e, h, pl.ds(r, TILE)] = s
                g0[e, h, pl.ds(r, TILE)] = s * (s * sx[e, h, pl.ds(r, TILE)])
        return carry

    lax.fori_loop(0, count, plane, 0)


def couple(g, wx, wy, wz, e, r, nh, inner, first):
    here = pl.ds(r, TILE)
    c = [g[e, h, here] for h in range(nh)]
    w = [wz[e, h, here] for h in range(nh)]
    ahead = [pltpu.roll(v, LANES - 1, 1) for v in c]
    behind = [pltpu.roll(a * b, 1, 1) for a, b in zip(w, c)]
    out = []
    for h in range(nh):
        t = wx[e, h, here] * g[e + 1, h, here] + wx[e - 1, h, here] * g[e - 1, h, here]
        t = t + (wy[e, h, here] * g[e, h, pl.ds(r + 1, TILE)] + wy[e, h, pl.ds(r - 1, TILE)] * g[e, h, pl.ds(r - 1, TILE)])
        after = jnp.where(inner, ahead[h], ahead[h + 1]) if h + 1 < nh else ahead[h]
        before = jnp.where(first, behind[h - 1], behind[h])
        out.append(t + (w[h] * after + before))
    return out


def apply_first(sx, wx, wy, wz, sc, g0, g1, w0, lo, count, tiles):
    nh = sx.shape[1]
    lane = lax.broadcasted_iota(jnp.int32, (TILE, LANES), 1)
    inner, first = lane < LANES - 1, lane == 0

    def plane(k, carry):
        e = lo + k
        for r in tiles:
            t = couple(g0, wx, wy, wz, e, r, nh, inner, first)
            for h in range(nh):
                s = sc[e, h, pl.ds(r, TILE)]
                v = s * sx[e, h, pl.ds(r, TILE)] - s * t[h]
                w0[e, h, pl.ds(r, TILE)] = v
                g1[e, h, pl.ds(r, TILE)] = s * v
        return carry

    lax.fori_loop(0, count, plane, 0)


def clear_rows(par, g1):
    _, nh, rows, _ = g1.shape
    zero = jnp.zeros((TILE, LANES), jnp.float32)
    for flag, at in ((par[4], OFF - TILE), (par[5], rows - OFF)):

        @pl.when(flag == 0)
        def _():
            for k in range(g1.shape[0]):
                for h in range(nh):
                    g1[k, h, pl.ds(at, TILE)] = zero


def clear_plane(g1, e, has, tiles):
    zero = jnp.zeros((TILE, LANES), jnp.float32)

    @pl.when(has == 0)
    def _():
        for r in tiles:
            for h in range(g1.shape[1]):
                g1[e, h, pl.ds(r, TILE)] = zero


def apply_second(sx, wx, wy, wz, sc, g1, w0, n0, lo, count, tiles, sums):
    nh = sx.shape[1]
    lane = lax.broadcasted_iota(jnp.int32, (TILE, LANES), 1)
    inner, first = lane < LANES - 1, lane == 0

    def plane(k, sums):
        e = lo + k
        sums = list(sums)
        for r in tiles:
            t = couple(g1, wx, wy, wz, e, r, nh, inner, first)
            for h in range(nh):
                s = sc[e, h, pl.ds(r, TILE)]
                a = s * sx[e, h, pl.ds(r, TILE)]
                b = w0[e, h, pl.ds(r, TILE)]
                c = b - s * t[h]
                n0[e, h, pl.ds(r, TILE)] = c
                for i, term in enumerate((a * a, b * a, b * b, c * b, c * a)):
                    sums[i] = sums[i] + term
        return tuple(sums)

    return lax.fori_loop(0, count, plane, tuple(sums))


def row_tiles(ny, inset):
    return list(range(OFF + inset * TILE, OFF + ny - inset * TILE, TILE))


def outer_tiles(ny, reach, inset):
    inside = row_tiles(ny, inset)
    return [r for r in row_tiles(ny, -reach) if r not in inside]


def near_side(par):
    xodd = par[0] == 1
    return jnp.where(xodd, 1, 4), jnp.where(xodd, 2, 5), jnp.where(xodd, 3, 6), jnp.where(xodd, par[2], par[3])


def inner_kernel(sizes, dens, src, near, dx, sx, wx, wy, wz, sc, g0, g1, w0, n0, mom):
    par = position(sizes)
    nx, ny, _ = dens.shape
    xodd = par[0] == 1
    first, second, third, has = near_side(par)
    has_near = has == 1
    own = slice(OFF, OFF + ny)
    for k in range(nx):
        put_plane(dx, k + DEEP, own, 0.5 * dens[k])
        put_plane(sx, k + DEEP, own, src[k])
    beyond = jnp.where(xodd, 0, nx + 3)
    for k in range(3):
        put_plane(dx, beyond + k, own, jnp.where(has_near, 0.5 * near[k], 0.0))
    beyond = jnp.where(xodd, 1, nx + 3)
    for k in range(2):
        put_plane(sx, beyond + k, own, jnp.where(has_near, near[3 + k], 0.0))
    weigh(dx, sx, wx, wy, wz, sc, g0, first, nx + 1, row_tiles(ny, 1))
    apply_first(sx, wx, wy, wz, sc, g0, g1, w0, second, nx - 1, row_tiles(ny, 2))
    clear_plane(g1, jnp.where(xodd, 2, nx + 3), has, row_tiles(ny, 2))
    zero = jnp.zeros((TILE, LANES), jnp.float32)
    sums = apply_second(sx, wx, wy, wz, sc, g1, w0, n0, third, nx - 3, row_tiles(ny, 3), (zero,) * SUMS)
    for i in range(SUMS):
        mom[i] = sums[i]


def edge_kernel(sizes, rxs, rdg, rnc, part, *refs):
    par = position(sizes)
    mom, dx, sx, wx, wy, wz, sc, g0, g1, w0, n0 = refs[10:]
    nx = dx.shape[0] - 2 * DEEP
    ny = dx.shape[2] - 2 * OFF
    xodd, yodd = par[0] == 1, par[1] == 1
    first, second, third, has = near_side(par)
    has_near, has_down, has_up = has == 1, par[4] == 1, par[5] == 1
    beyond = jnp.where(xodd, 1, nx + 3)
    for k in range(nx + 2):
        inside = True if k < nx else has_near
        a, b = (rxs[k], rdg[k]) if k < nx else (rnc[k - nx], rnc[2 + k - nx])
        low, high = jnp.where(yodd, a, b), jnp.where(yodd, b, a)
        low = jnp.where(jnp.logical_and(has_down, inside), low, 0.0)
        high = jnp.where(jnp.logical_and(has_up, inside), high, 0.0)
        put_rows(dx, sx, k + DEEP if k < nx else beyond + k - nx, low, high, ny)
    weigh(dx, sx, wx, wy, wz, sc, g0, first, nx + 1, outer_tiles(ny, 1, 1))
    apply_first(sx, wx, wy, wz, sc, g0, g1, w0, second, nx - 1, outer_tiles(ny, 1, 2))
    clear_plane(g1, jnp.where(xodd, 2, nx + 3), has, outer_tiles(ny, 1, 2))
    clear_rows(par, g1)
    sums = apply_second(sx, wx, wy, wz, sc, g1, w0, n0, third, nx - 3, outer_tiles(ny, 0, 3), [part[i] for i in range(SUMS)])
    for i in range(SUMS):
        mom[i] = sums[i]


def far_kernel(sizes, far, rfc, part, dx_in, sx_in, wx_in, wy_in, wz_in, sc_in, g0_in, g1_in, w0_in, n0_in,
               mom, dx, sx, wx, wy, wz, sc, g0, g1, w0, n0):
    par = position(sizes)
    ny, _ = far.shape[1:]
    nx = dx.shape[0] - 2 * DEEP
    xodd, yodd = par[0] == 1, par[1] == 1
    has = jnp.where(xodd, par[3], par[2])
    has_far = has == 1
    has_down, has_up = jnp.logical_and(has_far, par[4] == 1), jnp.logical_and(has_far, par[5] == 1)
    own = slice(OFF, OFF + ny)
    beyond = jnp.where(xodd, nx + 3, 0)
    for k in range(3):
        put_plane(dx, beyond + k, own, jnp.where(has_far, 0.5 * far[k], 0.0))
    beyond = jnp.where(xodd, nx + 3, 1)
    for k in range(2):
        put_plane(sx, beyond + k, own, jnp.where(has_far, far[3 + k], 0.0))
        a, b = rfc[k], rfc[2 + k]
        low, high = jnp.where(yodd, a, b), jnp.where(yodd, b, a)
        put_rows(dx, sx, beyond + k, jnp.where(has_down, low, 0.0), jnp.where(has_up, high, 0.0), ny)
    weigh(dx, sx, wx, wy, wz, sc, g0, jnp.where(xodd, nx + 2, 1), 3, row_tiles(ny, -1))
    apply_first(sx, wx, wy, wz, sc, g0, g1, w0, jnp.where(xodd, nx + 1, 2), 3, row_tiles(ny, -1))
    clear_plane(g1, jnp.where(xodd, nx + 3, 2), has, row_tiles(ny, -1))
    clear_rows(par, g1)
    sums = apply_second(sx, wx, wy, wz, sc, g1, w0, n0, jnp.where(xodd, nx, 3), 3, row_tiles(ny, 0), [part[i] for i in range(SUMS)])
    place = lax.broadcasted_iota(jnp.int32, (1, LANES), 1) // PART
    out = jnp.zeros((1, LANES), jnp.float32)
    for k, v in enumerate(sums):
        p = jnp.sum(v, axis=0, keepdims=True)
        width = LANES // 2
        while width >= PART:
            p = p + pltpu.roll(p, width, 1)
            width //= 2
        out = jnp.where(place == k, p, out)
    mom[...] = out


def last_kernel(mom, sx, sc, w0, n0, p_out, r_out, p_buf, r_buf, sems):
    place = lax.broadcasted_iota(jnp.int32, mom.shape, 1) // PART
    m = mom[...]

    def whole(v):
        return jnp.sum(jnp.sum(v, axis=0, keepdims=True), axis=1, keepdims=True)

    def lanes(k):
        return pltpu.roll(m, (LANES - k * PART) % LANES, 1) if k else m

    head = place == 0
    m0, m1, m2, m3, m4 = (jnp.where(head, lanes(k), 0.0) for k in range(SUMS))
    gamma0 = whole(m0)
    delta0 = whole(m1)
    a0 = gamma0 / delta0
    gamma1 = whole(m0 - a0 * (m1 + m1 - a0 * m2))
    delta1 = whole(m1 - a0 * (m4 + m2 - a0 * m3))
    b1 = gamma1 / gamma0
    a1 = gamma1 / (delta1 - b1 * gamma1 / a0)
    nx, ny, nz = p_out.shape
    c = jnp.broadcast_to(a0 + (a1 + a1 * b1), (TILE, LANES))
    d = jnp.broadcast_to(a0 * a1, (TILE, LANES))

    def out(i):
        return (pltpu.make_async_copy(p_buf.at[pl.ds(i, 1)], p_out.at[pl.ds(i, 1)], sems.at[0, i]),
                pltpu.make_async_copy(r_buf.at[pl.ds(i, 1)], r_out.at[pl.ds(i, 1)], sems.at[1, i]))

    def plane(i, carry):
        e = i + DEEP
        for r in range(0, ny, TILE):
            for h, at in halves(nz):
                here = pl.ds(OFF + r, TILE)
                s = sc[e, h, here]
                r0 = s * sx[e, h, here]
                v0 = w0[e, h, here]
                p_buf[i, pl.ds(r, TILE), at] = s * (c * r0 - d * v0)
                r_buf[i, pl.ds(r, TILE), at] = r0 - c * v0 + d * n0[e, h, here]
        for copy in out(i):
            copy.start()
        return carry

    lax.fori_loop(0, nx, plane, 0)
    for i in range(nx):
        for copy in out(i):
            copy.wait()


def shards(nx_dev, ny_dev, source, density):
    both = ("gx", "gy")
    near_pairs, far_pairs, ynear_pairs, yfar_pairs = swaps(nx_dev, ny_dev)
    nx, ny, nz = density.shape
    sizes = (nx_dev, ny_dev)
    vmem = pl.BlockSpec(memory_space=VMEM)
    hbm = pl.BlockSpec(memory_space=pltpu.HBM)

    def call(body, n_in, outs, limit, **more):
        return pl.pallas_call(
            functools.partial(body, sizes), out_shape=outs, in_specs=[vmem] * n_in, out_specs=jax.tree.map(lambda _: vmem, outs),
            compiler_params=pltpu.CompilerParams(vmem_limit_bytes=limit * MIB), **more,
        )

    def send(value, pairs):
        return lax.ppermute(value, both, pairs)

    planes, rows, block = (VMEM(v, jnp.float32) for v in ((5, ny, nz), (nx, TILE, nz), density.shape))
    shapes = (planes, planes, rows, rows, block, block)
    far, near, xs, dg, dens, src = pl.pallas_call(
        functools.partial(load_kernel, sizes), out_shape=shapes, in_specs=[hbm] * 2, out_specs=(vmem,) * 6, name="load_kernel",
        scratch_shapes=[pltpu.SemaphoreType.DMA((2 * nx,))], compiler_params=pltpu.CompilerParams(vmem_limit_bytes=8 * MIB),
    )(*(pltpu.with_memory_space_constraint(v, pltpu.HBM) for v in (density, source)))
    far = send(far, far_pairs)
    near = send(near, near_pairs)
    rxs = send(xs, ynear_pairs)
    rdg = send(dg, yfar_pairs)
    corner = VMEM((4, TILE, nz), jnp.float32)
    rfc, rnc = call(corner_kernel, 2, (corner, corner), 4)(rxs, rdg)
    rfc = send(rfc, far_pairs)
    rnc = send(rnc, near_pairs)

    ext = VMEM((nx + 2 * DEEP, nz // LANES, ny + 2 * OFF, LANES), jnp.float32)
    sums = VMEM((SUMS, TILE, LANES), jnp.float32)
    *held, part = call(inner_kernel, 3, (ext,) * 10 + (sums,), 8)(dens, src, near)
    part, *held = call(edge_kernel, 14, (sums,) + (ext,) * 10, 8, input_output_aliases={4 + k: 1 + k for k in range(10)})(
        rxs, rdg, rnc, part, *held)
    mom, *held = call(far_kernel, 13, (VMEM((1, LANES), jnp.float32),) + (ext,) * 10, 8, input_output_aliases={3 + k: 1 + k for k in range(10)})(
        far, rfc, part, *held)
    _, sx, _, _, _, sc, _, _, w0, n0 = held

    n = nx_dev * ny_dev
    sent = jnp.broadcast_to(mom[None], (n, 1, LANES))
    got = lax.all_to_all(sent, both, 0, 0, tiled=True).reshape(n, LANES)
    whole = jax.ShapeDtypeStruct(density.shape, jnp.float32)
    plane = VMEM(density.shape, jnp.float32)
    return pl.pallas_call(
        last_kernel, out_shape=(whole, whole), in_specs=[vmem] * 5, out_specs=(hbm, hbm), name="last_kernel",
        scratch_shapes=[plane, plane, pltpu.SemaphoreType.DMA((2, nx))],
        compiler_params=pltpu.CompilerParams(vmem_limit_bytes=8 * MIB),
    )(got, sx, sc, w0, n0)


def solution(mesh):
    spec = P("gx", "gy", None)
    body = functools.partial(shards, mesh.shape["gx"], mesh.shape["gy"])
    return jax.shard_map(body, mesh=mesh, in_specs=(spec, spec), out_specs=(spec, spec), check_vma=False)
```

```python
import functools

import jax
import jax.numpy as jnp
from jax import lax
from jax.experimental import pallas as pl
from jax.experimental.pallas import tpu as pltpu
from jax.sharding import PartitionSpec as P


TILE = 8
LANES = 128
OFF = 16
DEEP = 3
ROWS = 5
PART = 16
SUMS = 5
MIB = 1 << 20
VMEM = pltpu.VMEM


def swaps(nx, ny):
    at = lambda x, y: x * ny + y
    near, far, ynear, yfar = [], [], [], []
    for x in range(nx):
        for y in range(ny):
            near.append((at(x, y), at(x ^ 1, y)))
            other = x - 1 if x % 2 == 0 else x + 1
            inside = 0 <= other < nx
            far.append((at(x, y), at(other, y) if inside else at(x, (y + ny // 2) % ny)))
            ynear.append((at(x, y), at(x, y ^ 1)))
            beside = y - 1 if y % 2 == 0 else y + 1
            within = 0 <= beside < ny
            yfar.append((at(x, y), at(x, beside) if within else at(x ^ 1, y)))
    return near, far, ynear, yfar


def position(sizes):
    ix, iy = lax.axis_index("gx"), lax.axis_index("gy")
    flags = (ix % 2 == 1, iy % 2 == 1, ix > 0, ix < sizes[0] - 1, iy > 0, iy < sizes[1] - 1)
    return [jnp.where(f, 1, 0) for f in flags]


def load_kernel(sizes, dens_hbm, src_hbm, far, near, xs, dg, dens, src, tall, sems):
    par = position(sizes)
    nx, ny, nz = dens.shape
    xodd, yodd = par[0] == 1, par[1] == 1
    order = [jnp.where(xodd, nx - 1 - k, k) for k in range(nx)]
    copies = []
    for k, at in enumerate(order):
        for i, (a, b) in enumerate(((dens_hbm, dens), (src_hbm, src))):
            copies.append(pltpu.make_async_copy(a.at[pl.ds(at, 1)], b.at[pl.ds(at, 1)], sems.at[2 * k + i]))
    for copy in copies:
        copy.start()
    for copy in copies[:6]:
        copy.wait()
    far[0] = dens[order[0]]
    far[1] = dens[order[1]]
    far[2] = src[order[0]]
    second = dens[order[1]]
    put_plane(tall, 0, slice(TILE, TILE + ny), 0.5 * second)
    lane = lax.broadcasted_iota(jnp.int32, (TILE, LANES), 1)
    inner, first = lane < LANES - 1, lane == 0
    for r in range(0, ny, TILE):
        here = pl.ds(r + TILE, TILE)
        c = [tall[0, h, here] for h, _ in halves(nz)]
        z_up, z_down, _ = depth_weights(c, inner, first)
        for h, lanes in halves(nz):
            beside = [0.5 * dens[order[k], pl.ds(r, TILE), lanes] for k in (0, 2)]
            beside += [tall[0, h, pl.ds(r + TILE + 1, TILE)], tall[0, h, pl.ds(r + TILE - 1, TILE)]]
            w = [1.0 / (c[h] + v) for v in beside]
            s = lax.rsqrt((w[0] + w[1]) + (w[2] + w[3]) + (z_up[h] + z_down[h]))
            far[3, pl.ds(r, TILE), lanes] = s * (s * src[order[1], pl.ds(r, TILE), lanes])
    for copy in copies[6:]:
        copy.wait()
    d, s = jnp.where(xodd, 0, nx - 3), jnp.where(xodd, 0, nx - 2)
    for k in range(3):
        near[k] = dens[d + k]
    for k in range(2):
        near[3 + k] = src[s + k]
    for j in range(ROWS):
        ref, at = (dens, j) if j < DEEP else (src, j - DEEP)
        down, up = ref[:, at, :], ref[:, ny - 1 - at, :]
        xs[j] = jnp.where(yodd, down, up)
        dg[j] = jnp.where(yodd, up, down)


def corner_kernel(sizes, rxs, rdg, dens, src, far, near):
    par = position(sizes)
    xodd, yodd = par[0] == 1, par[1] == 1
    nx, ny, _ = dens.shape
    for out, backward in ((far, xodd), (near, jnp.logical_not(xodd))):
        at = [jnp.where(backward, nx - 1 - k, k) for k in range(3)]
        for k in range(2):
            for j in range(ROWS):
                a, b = rxs[j, pl.ds(at[k], 1), :], rdg[j, pl.ds(at[k], 1), :]
                out[k, j:j + 1] = jnp.where(yodd, a, b)
                out[2 + k, j:j + 1] = jnp.where(yodd, b, a)
        for side, row in ((0, 0), (1, ny - 1)):
            out[2 * side + 1, ROWS:ROWS + 1] = dens[at[2], row:row + 1]
            out[2 * side + 1, ROWS + 1:ROWS + 2] = src[at[1], row:row + 1]


class Stores:
    def __init__(self, depth):
        self.depth, self.held = depth, []

    def put(self, items):
        self.held.append(items)
        if len(self.held) > self.depth:
            self.flush(1)

    def flush(self, count=None):
        for items in self.held[:count]:
            for ref, at, value in items:
                ref[at] = value
        self.held = [] if count is None else self.held[count:]


def halves(nz):
    return [(h, slice(h * LANES, (h + 1) * LANES)) for h in range(nz // LANES)]


def loop(count, step):
    def body(k, carry):
        step(k)
        return carry

    lax.fori_loop(0, count, body, 0)


def put_plane(ref, e, rows, value):
    for h, lanes in halves(value.shape[-1]):
        ref[e, h, rows] = value[:, lanes]


def put_row(dx, sx, planes, ny, j, low, high):
    ref, depth = (dx, j) if j < DEEP else (sx, j - DEEP)
    if j < DEEP:
        low, high = 0.5 * low, 0.5 * high
    for value, at in ((low, OFF - 1 - depth), (high, OFF + ny + depth)):
        for h, lanes in halves(value.shape[-1]):
            ref[planes, h, at, :] = value[:, lanes]


def depth_weights(c, inner, first):
    nh = len(c)
    turned = [pltpu.roll(v, LANES - 1, 1) for v in c]
    z_up, z_in = [], []
    for h in range(nh):
        w = 1.0 / (c[h] + jnp.where(inner, turned[h], turned[h + 1] if h + 1 < nh else 0.0))
        z_up.append(w)
        z_in.append(w if h + 1 < nh else jnp.where(inner, w, 0.0))
    back = [pltpu.roll(v, 1, 1) for v in z_in]
    z_down = [jnp.where(first, back[h - 1] if h else 1.0 / c[0], back[h]) for h in range(nh)]
    return z_up, z_down, z_in


def weigh(dx, sx, wx, wy, wz, sc, g0, lo, count, tiles, unroll=1):
    nh = dx.shape[1]
    lane = lax.broadcasted_iota(jnp.int32, (TILE, LANES), 1)
    inner, first = lane < LANES - 1, lane == 0
    for r in tiles:
        for h in range(nh):
            wx[lo - 1, h, pl.ds(r, TILE)] = 1.0 / (dx[lo - 1, h, pl.ds(r, TILE)] + dx[lo, h, pl.ds(r, TILE)])

    def plane(k, carry):
        e = lo + k
        stores = Stores(1)
        for r in tiles:
            here = pl.ds(r, TILE)
            c = [dx[e, h, here] for h in range(nh)]
            beside = [(dx[e + 1, h, here], wx[e - 1, h, here], dx[e, h, pl.ds(r + 1, TILE)], dx[e, h, pl.ds(r - 1, TILE)], sx[e, h, here])
                      for h in range(nh)]
            z_up, z_down, z_in = depth_weights(c, inner, first)
            items = [(wz, (e, h, here), z_in[h]) for h in range(nh)]
            for h in range(nh):
                above, x_down, after, before, source = beside[h]
                x_up = 1.0 / (c[h] + above)
                y_up = 1.0 / (c[h] + after)
                y_down = 1.0 / (c[h] + before)
                diag = (x_up + x_down) + (y_up + y_down) + (z_up[h] + z_down[h])
                s = lax.rsqrt(diag)
                items += [(wx, (e, h, here), x_up), (wy, (e, h, here), y_up), (sc, (e, h, here), s), (g0, (e, h, here), s * (s * source))]
            stores.put(items)
        stores.flush()
        return carry

    lax.fori_loop(0, count, plane, 0, unroll=unroll)


def couple(g, wx, wy, wz, e, r, nh, inner, first):
    here = pl.ds(r, TILE)
    c = [g[e, h, here] for h in range(nh)]
    w = [wz[e, h, here] for h in range(nh)]
    ahead = [pltpu.roll(v, LANES - 1, 1) for v in c]
    behind = [pltpu.roll(a * b, 1, 1) for a, b in zip(w, c)]
    out = []
    for h in range(nh):
        t = wx[e, h, here] * g[e + 1, h, here] + wx[e - 1, h, here] * g[e - 1, h, here]
        t = t + (wy[e, h, here] * g[e, h, pl.ds(r + 1, TILE)] + wy[e, h, pl.ds(r - 1, TILE)] * g[e, h, pl.ds(r - 1, TILE)])
        after = jnp.where(inner, ahead[h], ahead[h + 1]) if h + 1 < nh else ahead[h]
        before = jnp.where(first, behind[h - 1], behind[h])
        out.append(t + (w[h] * after + before))
    return out


def apply_first(sx, wx, wy, wz, sc, g0, g1, w0, lo, count, tiles, unroll=1):
    nh = sx.shape[1]
    lane = lax.broadcasted_iota(jnp.int32, (TILE, LANES), 1)
    inner, first = lane < LANES - 1, lane == 0

    def plane(k, carry):
        e = lo + k
        stores = Stores(1)
        for r in tiles:
            here = pl.ds(r, TILE)
            t = couple(g0, wx, wy, wz, e, r, nh, inner, first)
            items = []
            for h in range(nh):
                s = sc[e, h, here]
                v = s * sx[e, h, here] - s * t[h]
                items += [(w0, (e, h, here), v), (g1, (e, h, here), s * v)]
            stores.put(items)
        stores.flush()
        return carry

    lax.fori_loop(0, count, plane, 0, unroll=unroll)


def clear_rows(par, g1):
    _, nh, rows, _ = g1.shape
    zero = jnp.zeros((TILE, LANES), jnp.float32)
    for flag, at in ((par[4], OFF - TILE), (par[5], rows - OFF)):

        @pl.when(flag == 0)
        def _():
            for k in range(g1.shape[0]):
                for h in range(nh):
                    g1[k, h, pl.ds(at, TILE)] = zero


def clear_plane(g1, e, has, tiles):
    zero = jnp.zeros((TILE, LANES), jnp.float32)

    @pl.when(has == 0)
    def _():
        for r in tiles:
            for h in range(g1.shape[1]):
                g1[e, h, pl.ds(r, TILE)] = zero


def apply_second(sx, wx, wy, wz, sc, g1, w0, n0, lo, count, tiles, sums, unroll=1):
    nh = sx.shape[1]
    lane = lax.broadcasted_iota(jnp.int32, (TILE, LANES), 1)
    inner, first = lane < LANES - 1, lane == 0

    def plane(k, sums):
        e = lo + k
        sums = list(sums)
        stores = Stores(2)
        for r in tiles:
            t = couple(g1, wx, wy, wz, e, r, nh, inner, first)
            for h in range(nh):
                s = sc[e, h, pl.ds(r, TILE)]
                a = s * sx[e, h, pl.ds(r, TILE)]
                b = w0[e, h, pl.ds(r, TILE)]
                c = b - s * t[h]
                stores.put([(n0, (e, h, pl.ds(r, TILE)), c)])
                for i, term in enumerate((a * a, b * a, b * b, c * b, c * a)):
                    sums[i] = sums[i] + term
        stores.flush()
        return tuple(sums)

    return lax.fori_loop(0, count, plane, tuple(sums), unroll=unroll)


def beyond(nx, upper, depth):
    return jnp.where(upper, nx + DEEP - 1 + depth, DEEP - depth)


def put_corners(dx, sx, corners, upper, has_down, has_up):
    nx, ny = dx.shape[0] - 2 * DEEP, dx.shape[2] - 2 * OFF
    for k in range(2):
        e = beyond(nx, upper, k + 1)
        for j in range(ROWS):
            low, high = corners[k, j:j + 1], corners[2 + k, j:j + 1]
            put_row(dx, sx, pl.ds(e, 1), ny, j, jnp.where(has_down, low, 0.0), jnp.where(has_up, high, 0.0))


def row_tiles(ny, inset):
    return list(range(OFF + inset * TILE, OFF + ny - inset * TILE, TILE))


def outer_tiles(ny, reach, inset):
    inside = row_tiles(ny, inset)
    return [r for r in row_tiles(ny, -reach) if r not in inside]


def near_side(par):
    xodd = par[0] == 1
    return jnp.where(xodd, 1, 4), jnp.where(xodd, 2, 5), jnp.where(xodd, 3, 6), jnp.where(xodd, par[2], par[3])


def inner_kernel(sizes, dens, src, near, dx, sx, wx, wy, wz, sc, g0, g1, w0):
    par = position(sizes)
    nx, ny, _ = dens.shape
    xodd = par[0] == 1
    first, second, _, has = near_side(par)
    has_near = has == 1
    own = slice(OFF, OFF + ny)

    def fill(k):
        put_plane(dx, k + DEEP, own, 0.5 * dens[k])
        put_plane(sx, k + DEEP, own, src[k])

    loop(nx, fill)
    near_third, near_beyond = jnp.where(xodd, 0, nx + 3), jnp.where(xodd, 1, nx + 3)
    loop(3, lambda k: put_plane(dx, near_third + k, own, jnp.where(has_near, 0.5 * near[k], 0.0)))
    loop(2, lambda k: put_plane(sx, near_beyond + k, own, jnp.where(has_near, near[3 + k], 0.0)))
    weigh(dx, sx, wx, wy, wz, sc, g0, first, nx + 1, row_tiles(ny, 1), unroll=3)
    apply_first(sx, wx, wy, wz, sc, g0, g1, w0, second, nx - 1, row_tiles(ny, 2), unroll=7)
    clear_plane(g1, jnp.where(xodd, 2, nx + 3), has, row_tiles(ny, 2))


def inner_second_kernel(sizes, sx, wx, wy, wz, sc, g1, w0, n0, mom):
    par = position(sizes)
    nx, ny = sx.shape[0] - 2 * DEEP, sx.shape[2] - 2 * OFF
    third = near_side(par)[2]
    zero = jnp.zeros((TILE, LANES), jnp.float32)
    sums = apply_second(sx, wx, wy, wz, sc, g1, w0, n0, third, nx - 3, row_tiles(ny, 3), (zero,) * SUMS, unroll=5)
    for i in range(SUMS):
        mom[i] = sums[i]


def edge_kernel(sizes, rxs, rdg, rnc, part, *refs):
    par = position(sizes)
    mom, dx, sx, wx, wy, wz, sc, g0, g1, w0, n0 = refs[10:]
    nx = dx.shape[0] - 2 * DEEP
    ny = dx.shape[2] - 2 * OFF
    xodd, yodd = par[0] == 1, par[1] == 1
    first, second, third, has = near_side(par)
    has_near, has_down, has_up = has == 1, par[4] == 1, par[5] == 1
    for j in range(ROWS):
        a, b = rxs[j], rdg[j]
        low, high = jnp.where(yodd, a, b), jnp.where(yodd, b, a)
        put_row(dx, sx, pl.ds(DEEP, nx), ny, j, jnp.where(has_down, low, 0.0), jnp.where(has_up, high, 0.0))
    put_corners(dx, sx, rnc, jnp.logical_not(xodd), jnp.logical_and(has_near, has_down), jnp.logical_and(has_near, has_up))
    weigh(dx, sx, wx, wy, wz, sc, g0, first, nx + 1, outer_tiles(ny, 1, 1), unroll=3)
    apply_first(sx, wx, wy, wz, sc, g0, g1, w0, second, nx - 1, outer_tiles(ny, 1, 2), unroll=7)
    clear_plane(g1, jnp.where(xodd, 2, nx + 3), has, outer_tiles(ny, 1, 2))
    clear_rows(par, g1)
    sums = apply_second(sx, wx, wy, wz, sc, g1, w0, n0, third, nx - 3, outer_tiles(ny, 0, 3), [part[i] for i in range(SUMS)], unroll=5)
    for i in range(SUMS):
        mom[i] = sums[i]


def far_kernel(sizes, far, rfc, part, dx_in, sx_in, wx_in, wy_in, wz_in, sc_in, g0_in, g1_in, w0_in, n0_in,
               mom, dx, sx, wx, wy, wz, sc, g0, g1, w0, n0):
    par = position(sizes)
    ny, nz = far.shape[1:]
    nx = dx.shape[0] - 2 * DEEP
    xodd = par[0] == 1
    has = jnp.where(xodd, par[3], par[2])
    has_far = has == 1
    has_down, has_up = jnp.logical_and(has_far, par[4] == 1), jnp.logical_and(has_far, par[5] == 1)
    own = slice(OFF, OFF + ny)
    e1, e2, _ = (beyond(nx, xodd, d) for d in (1, 2, 3))
    put_plane(dx, e1, own, jnp.where(has_far, 0.5 * far[0], 0.0))
    put_plane(dx, e2, own, jnp.where(has_far, 0.5 * far[1], 0.0))
    put_plane(sx, e1, own, jnp.where(has_far, far[2], 0.0))
    put_plane(g0, e2, own, jnp.where(has_far, far[3], 0.0))
    put_corners(dx, sx, rfc, xodd, has_down, has_up)
    lane = lax.broadcasted_iota(jnp.int32, (TILE, LANES), 1)
    row = lax.broadcasted_iota(jnp.int32, (TILE, LANES), 0)
    inner, first = lane < LANES - 1, lane == 0
    for side, r in ((0, OFF), (1, OFF + ny - TILE)):
        here = pl.ds(r, TILE)
        c = [dx[e2, h, here] for h, _ in halves(nz)]
        z_up, z_down, _ = depth_weights(c, inner, first)
        for h, lanes in halves(nz):
            third = jnp.where(has_far, 0.5 * rfc[2 * side + 1, ROWS:ROWS + 1, lanes], 0.0)
            source = jnp.where(has_far, rfc[2 * side + 1, ROWS + 1:ROWS + 2, lanes], 0.0)
            w = [1.0 / (c[h] + v) for v in (third, dx[e1, h, here], dx[e2, h, pl.ds(r + 1, TILE)], dx[e2, h, pl.ds(r - 1, TILE)])]
            s = lax.rsqrt((w[0] + w[1]) + (w[2] + w[3]) + (z_up[h] + z_down[h]))
            g0[e2, h, here] = jnp.where(row == side * (TILE - 1), s * (s * source), g0[e2, h, here])
    weigh(dx, sx, wx, wy, wz, sc, g0, jnp.where(xodd, nx + 2, 2), 2, row_tiles(ny, -1))
    apply_first(sx, wx, wy, wz, sc, g0, g1, w0, jnp.where(xodd, nx + 1, 2), 3, row_tiles(ny, -1), unroll=3)
    clear_plane(g1, e1, has, row_tiles(ny, -1))
    clear_rows(par, g1)
    sums = apply_second(sx, wx, wy, wz, sc, g1, w0, n0, jnp.where(xodd, nx, 3), 3, row_tiles(ny, 0), [part[i] for i in range(SUMS)], unroll=3)
    place = lax.broadcasted_iota(jnp.int32, (1, LANES), 1) // PART
    out = jnp.zeros((1, LANES), jnp.float32)
    for k, v in enumerate(sums):
        p = jnp.sum(v, axis=0, keepdims=True)
        width = LANES // 2
        while width >= PART:
            p = p + pltpu.roll(p, width, 1)
            width //= 2
        out = jnp.where(place == k, p, out)
    mom[...] = out


def last_kernel(mom, sx, sc, w0, n0, p_out, r_out, p_buf, r_buf, sems):
    place = lax.broadcasted_iota(jnp.int32, mom.shape, 1) // PART
    m = mom[...]

    def whole(v):
        return jnp.sum(jnp.sum(v, axis=0, keepdims=True), axis=1, keepdims=True)

    def lanes(k):
        return pltpu.roll(m, (LANES - k * PART) % LANES, 1) if k else m

    head = place == 0
    m0, m1, m2, m3, m4 = (jnp.where(head, lanes(k), 0.0) for k in range(SUMS))
    gamma0 = whole(m0)
    delta0 = whole(m1)
    a0 = gamma0 / delta0
    gamma1 = whole(m0 - a0 * (m1 + m1 - a0 * m2))
    delta1 = whole(m1 - a0 * (m4 + m2 - a0 * m3))
    b1 = gamma1 / gamma0
    a1 = gamma1 / (delta1 - b1 * gamma1 / a0)
    nx, ny, nz = p_out.shape
    c = jnp.broadcast_to(a0 + (a1 + a1 * b1), (TILE, LANES))
    d = jnp.broadcast_to(a0 * a1, (TILE, LANES))

    def out(i):
        return (pltpu.make_async_copy(p_buf.at[pl.ds(i, 1)], p_out.at[pl.ds(i, 1)], sems.at[0, i]),
                pltpu.make_async_copy(r_buf.at[pl.ds(i, 1)], r_out.at[pl.ds(i, 1)], sems.at[1, i]))

    def plane(i, carry):
        e = i + DEEP
        for r in range(0, ny, TILE):
            for h, at in halves(nz):
                here = pl.ds(OFF + r, TILE)
                s = sc[e, h, here]
                r0 = s * sx[e, h, here]
                v0 = w0[e, h, here]
                p_buf[i, pl.ds(r, TILE), at] = s * (c * r0 - d * v0)
                r_buf[i, pl.ds(r, TILE), at] = r0 - c * v0 + d * n0[e, h, here]
        for copy in out(i):
            copy.start()
        return carry

    lax.fori_loop(0, nx, plane, 0)
    for i in range(nx):
        for copy in out(i):
            copy.wait()


def shards(nx_dev, ny_dev, source, density):
    both = ("gx", "gy")
    near_pairs, far_pairs, ynear_pairs, yfar_pairs = swaps(nx_dev, ny_dev)
    nx, ny, nz = density.shape
    sizes = (nx_dev, ny_dev)
    vmem = pl.BlockSpec(memory_space=VMEM)
    hbm = pl.BlockSpec(memory_space=pltpu.HBM)

    def call(body, n_in, outs, limit, **more):
        return pl.pallas_call(
            functools.partial(body, sizes), out_shape=outs, in_specs=[vmem] * n_in, out_specs=jax.tree.map(lambda _: vmem, outs),
            compiler_params=pltpu.CompilerParams(vmem_limit_bytes=limit * MIB), **more,
        )

    def send(value, pairs):
        return lax.ppermute(value, both, pairs)

    few, planes, rows, block = (VMEM(v, jnp.float32) for v in ((4, ny, nz), (5, ny, nz), (ROWS, nx, nz), density.shape))
    shapes = (few, planes, rows, rows, block, block)
    far, near, xs, dg, dens, src = pl.pallas_call(
        functools.partial(load_kernel, sizes), out_shape=shapes, in_specs=[hbm] * 2, out_specs=(vmem,) * 6, name="load_kernel",
        scratch_shapes=[VMEM((1, nz // LANES, ny + 2 * TILE, LANES), jnp.float32), pltpu.SemaphoreType.DMA((2 * nx,))], compiler_params=pltpu.CompilerParams(vmem_limit_bytes=8 * MIB),
    )(*(pltpu.with_memory_space_constraint(v, pltpu.HBM) for v in (density, source)))
    far = send(far, far_pairs)
    near = send(near, near_pairs)
    rxs = send(xs, ynear_pairs)
    rdg = send(dg, yfar_pairs)
    corner = VMEM((4, TILE, nz), jnp.float32)
    rfc, rnc = call(corner_kernel, 4, (corner, corner), 4)(rxs, rdg, dens, src)
    rfc = send(rfc, far_pairs)
    rnc = send(rnc, near_pairs)

    ext = VMEM((nx + 2 * DEEP, nz // LANES, ny + 2 * OFF, LANES), jnp.float32)
    sums = VMEM((SUMS, TILE, LANES), jnp.float32)
    held = call(inner_kernel, 3, (ext,) * 9, 8)(dens, src, near)
    dx, sx, wx, wy, wz, sc, g0, g1, w0 = held
    n0, part = call(inner_second_kernel, 7, (ext, sums), 8)(sx, wx, wy, wz, sc, g1, w0)
    held = (*held, n0)
    part, *held = call(edge_kernel, 14, (sums,) + (ext,) * 10, 8, input_output_aliases={4 + k: 1 + k for k in range(10)})(
        rxs, rdg, rnc, part, *held)
    mom, *held = call(far_kernel, 13, (VMEM((1, LANES), jnp.float32),) + (ext,) * 10, 8, input_output_aliases={3 + k: 1 + k for k in range(10)})(
        far, rfc, part, *held)
    dx, sx, wx, wy, wz, sc, g0, g1, w0, n0 = held

    n = nx_dev * ny_dev
    sent = jnp.broadcast_to(mom[None], (n, 1, LANES))
    got = lax.all_to_all(sent, both, 0, 0, tiled=True).reshape(n, LANES)
    whole = jax.ShapeDtypeStruct(density.shape, jnp.float32)
    plane = VMEM(density.shape, jnp.float32)
    return pl.pallas_call(
        last_kernel, out_shape=(whole, whole), in_specs=[vmem] * 5, out_specs=(hbm, hbm), name="last_kernel",
        scratch_shapes=[plane, plane, pltpu.SemaphoreType.DMA((2, nx))],
        compiler_params=pltpu.CompilerParams(vmem_limit_bytes=8 * MIB),
    )(got, sx, sc, w0, n0)


def solution(mesh):
    spec = P("gx", "gy", None)
    body = functools.partial(shards, mesh.shape["gx"], mesh.shape["gy"])
    return jax.shard_map(body, mesh=mesh, in_specs=(spec, spec), out_specs=(spec, spec), check_vma=False)
```

```python
import functools

import jax
import jax.numpy as jnp
from jax import lax
from jax.experimental import pallas as pl
from jax.experimental.pallas import tpu as pltpu
from jax.sharding import PartitionSpec as P


TILE = 8
LANES = 128
OFF = 16
DEEP = 3
ROWS = 5
STEP = 2
PART = 16
SUMS = 5
MIB = 1 << 20
VMEM = pltpu.VMEM


def swaps(nx, ny):
    at = lambda x, y: x * ny + y
    near, far, ynear, yfar = [], [], [], []
    for x in range(nx):
        for y in range(ny):
            near.append((at(x, y), at(x ^ 1, y)))
            other = x - 1 if x % 2 == 0 else x + 1
            inside = 0 <= other < nx
            far.append((at(x, y), at(other, y) if inside else at(x, (y + ny // 2) % ny)))
            ynear.append((at(x, y), at(x, y ^ 1)))
            beside = y - 1 if y % 2 == 0 else y + 1
            within = 0 <= beside < ny
            yfar.append((at(x, y), at(x, beside) if within else at(x ^ 1, y)))
    return near, far, ynear, yfar


def position(sizes):
    ix, iy = lax.axis_index("gx"), lax.axis_index("gy")
    flags = (ix % 2 == 1, iy % 2 == 1, ix > 0, ix < sizes[0] - 1, iy > 0, iy < sizes[1] - 1)
    return [jnp.where(f, 1, 0) for f in flags]


def load_kernel(sizes, dens_hbm, src_hbm, far, near, xs, dg, dens, src, tall, sems):
    par = position(sizes)
    nx, ny, nz = dens.shape
    xodd, yodd = par[0] == 1, par[1] == 1
    order = [jnp.where(xodd, nx - 1 - k, k) for k in range(nx)]
    copies = []
    for k, at in enumerate(order):
        for i, (a, b) in enumerate(((dens_hbm, dens), (src_hbm, src))):
            copies.append(pltpu.make_async_copy(a.at[pl.ds(at, 1)], b.at[pl.ds(at, 1)], sems.at[2 * k + i]))
    for copy in copies:
        copy.start()
    for copy in copies[:6]:
        copy.wait()
    far[0] = dens[order[0]]
    far[1] = dens[order[1]]
    far[2] = src[order[0]]
    second = dens[order[1]]
    put_plane(tall, 0, slice(TILE, TILE + ny), 0.5 * second)
    lane = lax.broadcasted_iota(jnp.int32, (TILE, LANES), 1)
    inner, first = lane < LANES - 1, lane == 0
    for r in range(0, ny, TILE):
        here = pl.ds(r + TILE, TILE)
        c = [tall[0, h, here] for h, _ in halves(nz)]
        z_up, z_down, _ = depth_weights(c, inner, first)
        for h, lanes in halves(nz):
            beside = [0.5 * dens[order[k], pl.ds(r, TILE), lanes] for k in (0, 2)]
            beside += [tall[0, h, pl.ds(r + TILE + 1, TILE)], tall[0, h, pl.ds(r + TILE - 1, TILE)]]
            w = [1.0 / (c[h] + v) for v in beside]
            s = lax.rsqrt((w[0] + w[1]) + (w[2] + w[3]) + (z_up[h] + z_down[h]))
            far[3, pl.ds(r, TILE), lanes] = s * (s * src[order[1], pl.ds(r, TILE), lanes])
    for copy in copies[6:]:
        copy.wait()
    d, s = jnp.where(xodd, 0, nx - 3), jnp.where(xodd, 0, nx - 2)
    for k in range(3):
        near[k] = dens[d + k]
    for k in range(2):
        near[3 + k] = src[s + k]
    for j in range(ROWS):
        ref, at = (dens, j) if j < DEEP else (src, j - DEEP)
        down, up = ref[:, at, :], ref[:, ny - 1 - at, :]
        xs[j] = jnp.where(yodd, down, up)
        dg[j] = jnp.where(yodd, up, down)


def corner_kernel(sizes, rxs, rdg, dens, src, far, near):
    par = position(sizes)
    xodd, yodd = par[0] == 1, par[1] == 1
    nx, ny, _ = dens.shape
    for out, backward in ((far, xodd), (near, jnp.logical_not(xodd))):
        at = [jnp.where(backward, nx - 1 - k, k) for k in range(3)]
        for k in range(2):
            for j in range(ROWS):
                a, b = rxs[j, pl.ds(at[k], 1), :], rdg[j, pl.ds(at[k], 1), :]
                out[k, j:j + 1] = jnp.where(yodd, a, b)
                out[2 + k, j:j + 1] = jnp.where(yodd, b, a)
        for side, row in ((0, 0), (1, ny - 1)):
            out[2 * side + 1, ROWS:ROWS + 1] = dens[at[2], row:row + 1]
            out[2 * side + 1, ROWS + 1:ROWS + 2] = src[at[1], row:row + 1]


class Stores:
    def __init__(self, depth):
        self.depth, self.held = depth, []

    def put(self, items):
        self.held.append(items)
        if len(self.held) > self.depth:
            self.flush(1)

    def flush(self, count=None):
        for items in self.held[:count]:
            for ref, at, value in items:
                ref[at] = value
        self.held = [] if count is None else self.held[count:]


def halves(nz):
    return [(h, slice(h * LANES, (h + 1) * LANES)) for h in range(nz // LANES)]


def loop(count, step):
    def body(k, carry):
        step(k)
        return carry

    lax.fori_loop(0, count, body, 0)


def put_plane(ref, e, rows, value):
    for h, lanes in halves(value.shape[-1]):
        ref[e, h, rows] = value[:, lanes]


def put_row(dx, sx, planes, ny, j, low, high):
    ref, depth = (dx, j) if j < DEEP else (sx, j - DEEP)
    if j < DEEP:
        low, high = 0.5 * low, 0.5 * high
    for value, at in ((low, OFF - 1 - depth), (high, OFF + ny + depth)):
        for h, lanes in halves(value.shape[-1]):
            ref[planes, h, at, :] = value[:, lanes]


def depth_weights(c, inner, first):
    nh = len(c)
    turned = [pltpu.roll(v, LANES - 1, 1) for v in c]
    z_up, z_in = [], []
    for h in range(nh):
        w = 1.0 / (c[h] + jnp.where(inner, turned[h], turned[h + 1] if h + 1 < nh else 0.0))
        z_up.append(w)
        z_in.append(w if h + 1 < nh else jnp.where(inner, w, 0.0))
    back = [pltpu.roll(v, 1, 1) for v in z_in]
    z_down = [jnp.where(first, back[h - 1] if h else 1.0 / c[0], back[h]) for h in range(nh)]
    return z_up, z_down, z_in


def weigh(dx, sx, wx, wy, wz, sc, g0, lo, count, tiles, unroll=1):
    nh = dx.shape[1]
    lane = lax.broadcasted_iota(jnp.int32, (TILE, LANES), 1)
    inner, first = lane < LANES - 1, lane == 0
    for r in tiles:
        for h in range(nh):
            wx[lo - 1, h, pl.ds(r, TILE)] = 1.0 / (dx[lo - 1, h, pl.ds(r, TILE)] + dx[lo, h, pl.ds(r, TILE)])

    def plane(k, carry):
        e = lo + k
        stores = Stores(1)
        for r in tiles:
            here = pl.ds(r, TILE)
            c = [dx[e, h, here] for h in range(nh)]
            beside = [(dx[e + 1, h, here], wx[e - 1, h, here], dx[e, h, pl.ds(r + 1, TILE)], dx[e, h, pl.ds(r - 1, TILE)], sx[e, h, here])
                      for h in range(nh)]
            z_up, z_down, z_in = depth_weights(c, inner, first)
            items = [(wz, (e, h, here), z_in[h]) for h in range(nh)]
            for h in range(nh):
                above, x_down, after, before, source = beside[h]
                x_up = 1.0 / (c[h] + above)
                y_up = 1.0 / (c[h] + after)
                y_down = 1.0 / (c[h] + before)
                diag = (x_up + x_down) + (y_up + y_down) + (z_up[h] + z_down[h])
                s = lax.rsqrt(diag)
                items += [(wx, (e, h, here), x_up), (wy, (e, h, here), y_up), (sc, (e, h, here), s), (g0, (e, h, here), s * (s * source))]
            stores.put(items)
        stores.flush()
        return carry

    lax.fori_loop(0, count, plane, 0, unroll=unroll)


def couple(g, wx, wy, wz, e, r, nh, inner, first):
    here = pl.ds(r, TILE)
    c = [g[e, h, here] for h in range(nh)]
    w = [wz[e, h, here] for h in range(nh)]
    ahead = [pltpu.roll(v, LANES - 1, 1) for v in c]
    behind = [pltpu.roll(a * b, 1, 1) for a, b in zip(w, c)]
    out = []
    for h in range(nh):
        t = wx[e, h, here] * g[e + 1, h, here] + wx[e - 1, h, here] * g[e - 1, h, here]
        t = t + (wy[e, h, here] * g[e, h, pl.ds(r + 1, TILE)] + wy[e, h, pl.ds(r - 1, TILE)] * g[e, h, pl.ds(r - 1, TILE)])
        after = jnp.where(inner, ahead[h], ahead[h + 1]) if h + 1 < nh else ahead[h]
        before = jnp.where(first, behind[h - 1], behind[h])
        out.append(t + (w[h] * after + before))
    return out


def apply_first(sx, wx, wy, wz, sc, g0, g1, w0, lo, count, tiles, unroll=1):
    nh = sx.shape[1]
    lane = lax.broadcasted_iota(jnp.int32, (TILE, LANES), 1)
    inner, first = lane < LANES - 1, lane == 0

    def plane(k, carry):
        e = lo + k
        stores = Stores(1)
        for r in tiles:
            here = pl.ds(r, TILE)
            t = couple(g0, wx, wy, wz, e, r, nh, inner, first)
            items = []
            for h in range(nh):
                s = sc[e, h, here]
                v = s * sx[e, h, here] - s * t[h]
                items += [(w0, (e, h, here), v), (g1, (e, h, here), s * v)]
            stores.put(items)
        stores.flush()
        return carry

    lax.fori_loop(0, count, plane, 0, unroll=unroll)


def clear_rows(par, g1):
    _, nh, rows, _ = g1.shape
    zero = jnp.zeros((TILE, LANES), jnp.float32)
    for flag, at in ((par[4], OFF - TILE), (par[5], rows - OFF)):

        @pl.when(flag == 0)
        def _():
            for k in range(g1.shape[0]):
                for h in range(nh):
                    g1[k, h, pl.ds(at, TILE)] = zero


def clear_plane(g1, e, has, tiles):
    zero = jnp.zeros((TILE, LANES), jnp.float32)

    @pl.when(has == 0)
    def _():
        for r in tiles:
            for h in range(g1.shape[1]):
                g1[e, h, pl.ds(r, TILE)] = zero


def apply_second(sx, wx, wy, wz, sc, g1, w0, n0, lo, count, tiles, sums, unroll=1):
    nh = sx.shape[1]
    lane = lax.broadcasted_iota(jnp.int32, (TILE, LANES), 1)
    inner, first = lane < LANES - 1, lane == 0

    def plane(k, sums):
        e = lo + k
        sums = list(sums)
        stores = Stores(2)
        for r in tiles:
            t = couple(g1, wx, wy, wz, e, r, nh, inner, first)
            for h in range(nh):
                s = sc[e, h, pl.ds(r, TILE)]
                a = s * sx[e, h, pl.ds(r, TILE)]
                b = w0[e, h, pl.ds(r, TILE)]
                c = b - s * t[h]
                stores.put([(n0, (e, h, pl.ds(r, TILE)), c)])
                for i, term in enumerate((a * a, b * a, b * b, c * b, c * a)):
                    sums[i] = sums[i] + term
        stores.flush()
        return tuple(sums)

    return lax.fori_loop(0, count, plane, tuple(sums), unroll=unroll)


def beyond(nx, upper, depth):
    return jnp.where(upper, nx + DEEP - 1 + depth, DEEP - depth)


def put_corners(dx, sx, corners, upper, has_down, has_up):
    nx, ny = dx.shape[0] - 2 * DEEP, dx.shape[2] - 2 * OFF
    for k in range(2):
        e = beyond(nx, upper, k + 1)
        for j in range(ROWS):
            low, high = corners[k, j:j + 1], corners[2 + k, j:j + 1]
            put_row(dx, sx, pl.ds(e, 1), ny, j, jnp.where(has_down, low, 0.0), jnp.where(has_up, high, 0.0))


def row_tiles(ny, inset):
    return list(range(OFF + inset * TILE, OFF + ny - inset * TILE, TILE))


def outer_tiles(ny, reach, inset):
    inside = row_tiles(ny, inset)
    return [r for r in row_tiles(ny, -reach) if r not in inside]


def near_side(par):
    xodd = par[0] == 1
    return jnp.where(xodd, 1, 4), jnp.where(xodd, 2, 5), jnp.where(xodd, 3, 6), jnp.where(xodd, par[2], par[3])


def inner_kernel(sizes, dens, src, dx, sx, wx, wy, wz, sc, g0, g1, w0):
    nx, ny, _ = dens.shape
    own = slice(OFF, OFF + ny)

    def fill(k):
        put_plane(dx, k + DEEP, own, 0.5 * dens[k])
        put_plane(sx, k + DEEP, own, src[k])

    loop(nx, fill)
    weigh(dx, sx, wx, wy, wz, sc, g0, DEEP + 1, nx - 2, row_tiles(ny, 1), unroll=2)
    apply_first(sx, wx, wy, wz, sc, g0, g1, w0, DEEP + 2, nx - 4, row_tiles(ny, 2), unroll=4)


def beside_kernel(sizes, near, *refs):
    dx, sx, wx, wy, wz, sc, g0, g1, w0 = refs[9:]
    par = position(sizes)
    ny = near.shape[1]
    nx = dx.shape[0] - 2 * DEEP
    xodd = par[0] == 1
    has = near_side(par)[3]
    has_near = has == 1
    own = slice(OFF, OFF + ny)
    near_third, near_beyond = jnp.where(xodd, 0, nx + 3), jnp.where(xodd, 1, nx + 3)
    loop(3, lambda k: put_plane(dx, near_third + k, own, jnp.where(has_near, 0.5 * near[k], 0.0)))
    loop(2, lambda k: put_plane(sx, near_beyond + k, own, jnp.where(has_near, near[3 + k], 0.0)))
    weigh(dx, sx, wx, wy, wz, sc, g0, jnp.where(xodd, 1, nx + 2), 3, row_tiles(ny, 1), unroll=1)
    apply_first(sx, wx, wy, wz, sc, g0, g1, w0, jnp.where(xodd, 2, nx + 1), 3, row_tiles(ny, 2), unroll=3)
    clear_plane(g1, jnp.where(xodd, 2, nx + 3), has, row_tiles(ny, 2))


def inner_second_kernel(sizes, sx, wx, wy, wz, sc, g1, w0, n0, mom):
    par = position(sizes)
    nx, ny = sx.shape[0] - 2 * DEEP, sx.shape[2] - 2 * OFF
    third = near_side(par)[2]
    zero = jnp.zeros((TILE, LANES), jnp.float32)
    sums = apply_second(sx, wx, wy, wz, sc, g1, w0, n0, third, nx - 3, row_tiles(ny, 3), (zero,) * SUMS, unroll=5)
    for i in range(SUMS):
        mom[i] = sums[i]


def edge_kernel(sizes, rxs, rdg, rnc, part, *refs):
    par = position(sizes)
    mom, dx, sx, wx, wy, wz, sc, g0, g1, w0, n0 = refs[10:]
    nx = dx.shape[0] - 2 * DEEP
    ny = dx.shape[2] - 2 * OFF
    xodd, yodd = par[0] == 1, par[1] == 1
    first, second, third, has = near_side(par)
    has_near, has_down, has_up = has == 1, par[4] == 1, par[5] == 1
    for j in range(ROWS):
        a, b = rxs[j], rdg[j]
        low, high = jnp.where(yodd, a, b), jnp.where(yodd, b, a)
        put_row(dx, sx, pl.ds(DEEP, nx), ny, j, jnp.where(has_down, low, 0.0), jnp.where(has_up, high, 0.0))
    put_corners(dx, sx, rnc, jnp.logical_not(xodd), jnp.logical_and(has_near, has_down), jnp.logical_and(has_near, has_up))
    weigh(dx, sx, wx, wy, wz, sc, g0, first, nx + 1, outer_tiles(ny, 1, 1), unroll=3)
    apply_first(sx, wx, wy, wz, sc, g0, g1, w0, second, nx - 1, outer_tiles(ny, 1, 2), unroll=7)
    clear_plane(g1, jnp.where(xodd, 2, nx + 3), has, outer_tiles(ny, 1, 2))
    clear_rows(par, g1)
    sums = apply_second(sx, wx, wy, wz, sc, g1, w0, n0, third, nx - 3, outer_tiles(ny, 0, 3), [part[i] for i in range(SUMS)], unroll=5)
    for i in range(SUMS):
        mom[i] = sums[i]


def far_kernel(sizes, far, rfc, part, dx_in, sx_in, wx_in, wy_in, wz_in, sc_in, g0_in, g1_in, w0_in, n0_in,
               mom, dx, sx, wx, wy, wz, sc, g0, g1, w0, n0):
    par = position(sizes)
    ny, nz = far.shape[1:]
    nx = dx.shape[0] - 2 * DEEP
    xodd = par[0] == 1
    has = jnp.where(xodd, par[3], par[2])
    has_far = has == 1
    has_down, has_up = jnp.logical_and(has_far, par[4] == 1), jnp.logical_and(has_far, par[5] == 1)
    own = slice(OFF, OFF + ny)
    e1, e2, _ = (beyond(nx, xodd, d) for d in (1, 2, 3))
    put_plane(dx, e1, own, jnp.where(has_far, 0.5 * far[0], 0.0))
    put_plane(dx, e2, own, jnp.where(has_far, 0.5 * far[1], 0.0))
    put_plane(sx, e1, own, jnp.where(has_far, far[2], 0.0))
    put_plane(g0, e2, own, jnp.where(has_far, far[3], 0.0))
    put_corners(dx, sx, rfc, xodd, has_down, has_up)
    lane = lax.broadcasted_iota(jnp.int32, (TILE, LANES), 1)
    row = lax.broadcasted_iota(jnp.int32, (TILE, LANES), 0)
    inner, first = lane < LANES - 1, lane == 0
    for side, r in ((0, OFF), (1, OFF + ny - TILE)):
        here = pl.ds(r, TILE)
        c = [dx[e2, h, here] for h, _ in halves(nz)]
        z_up, z_down, _ = depth_weights(c, inner, first)
        for h, lanes in halves(nz):
            third = jnp.where(has_far, 0.5 * rfc[2 * side + 1, ROWS:ROWS + 1, lanes], 0.0)
            source = jnp.where(has_far, rfc[2 * side + 1, ROWS + 1:ROWS + 2, lanes], 0.0)
            w = [1.0 / (c[h] + v) for v in (third, dx[e1, h, here], dx[e2, h, pl.ds(r + 1, TILE)], dx[e2, h, pl.ds(r - 1, TILE)])]
            s = lax.rsqrt((w[0] + w[1]) + (w[2] + w[3]) + (z_up[h] + z_down[h]))
            g0[e2, h, here] = jnp.where(row == side * (TILE - 1), s * (s * source), g0[e2, h, here])
    weigh(dx, sx, wx, wy, wz, sc, g0, jnp.where(xodd, nx + 2, 2), 2, row_tiles(ny, -1))
    apply_first(sx, wx, wy, wz, sc, g0, g1, w0, jnp.where(xodd, nx + 1, 2), 3, row_tiles(ny, -1), unroll=3)
    clear_plane(g1, e1, has, row_tiles(ny, -1))
    clear_rows(par, g1)
    sums = apply_second(sx, wx, wy, wz, sc, g1, w0, n0, jnp.where(xodd, nx, 3), 3, row_tiles(ny, 0), [part[i] for i in range(SUMS)], unroll=3)
    place = lax.broadcasted_iota(jnp.int32, (1, LANES), 1) // PART
    out = jnp.zeros((1, LANES), jnp.float32)
    for k, v in enumerate(sums):
        p = jnp.sum(v, axis=0, keepdims=True)
        width = LANES // 2
        while width >= PART:
            p = p + pltpu.roll(p, width, 1)
            width //= 2
        out = jnp.where(place == k, p, out)
    mom[...] = out


def last_kernel(mom, sx, sc, w0, n0, p_out, r_out, p_buf, r_buf, sems):
    place = lax.broadcasted_iota(jnp.int32, mom.shape, 1) // PART
    m = mom[...]

    def whole(v):
        return jnp.sum(jnp.sum(v, axis=0, keepdims=True), axis=1, keepdims=True)

    def lanes(k):
        return pltpu.roll(m, (LANES - k * PART) % LANES, 1) if k else m

    head = place == 0
    m0, m1, m2, m3, m4 = (jnp.where(head, lanes(k), 0.0) for k in range(SUMS))
    gamma0 = whole(m0)
    delta0 = whole(m1)
    a0 = gamma0 / delta0
    gamma1 = whole(m0 - a0 * (m1 + m1 - a0 * m2))
    delta1 = whole(m1 - a0 * (m4 + m2 - a0 * m3))
    b1 = gamma1 / gamma0
    a1 = gamma1 / (delta1 - b1 * gamma1 / a0)
    nx, ny, nz = p_out.shape
    c = jnp.broadcast_to(a0 + (a1 + a1 * b1), (TILE, LANES))
    d = jnp.broadcast_to(a0 * a1, (TILE, LANES))

    def out(i):
        here = pl.ds(i * STEP, STEP)
        return (pltpu.make_async_copy(p_buf.at[here], p_out.at[here], sems.at[0, i]),
                pltpu.make_async_copy(r_buf.at[here], r_out.at[here], sems.at[1, i]))

    def group(i, carry):
        for k in range(STEP):
            plane = i * STEP + k
            e = plane + DEEP
            stores = Stores(2)
            for r in range(0, ny, TILE):
                here, there = pl.ds(OFF + r, TILE), pl.ds(r, TILE)
                items = []
                for h, at in halves(nz):
                    s, q, v0, v1 = sc[e, h, here], sx[e, h, here], w0[e, h, here], n0[e, h, here]
                    r0 = s * q
                    items.append((p_buf, (plane, there, at), s * (c * r0 - d * v0)))
                    items.append((r_buf, (plane, there, at), r0 - c * v0 + d * v1))
                stores.put(items)
            stores.flush()
        for copy in out(i):
            copy.start()
        return carry

    lax.fori_loop(0, nx // STEP, group, 0)
    for i in range(nx // STEP):
        for copy in out(i):
            copy.wait()


def shards(nx_dev, ny_dev, source, density):
    both = ("gx", "gy")
    near_pairs, far_pairs, ynear_pairs, yfar_pairs = swaps(nx_dev, ny_dev)
    nx, ny, nz = density.shape
    sizes = (nx_dev, ny_dev)
    vmem = pl.BlockSpec(memory_space=VMEM)
    hbm = pl.BlockSpec(memory_space=pltpu.HBM)

    def call(body, n_in, outs, limit, **more):
        return pl.pallas_call(
            functools.partial(body, sizes), out_shape=outs, in_specs=[vmem] * n_in, out_specs=jax.tree.map(lambda _: vmem, outs),
            compiler_params=pltpu.CompilerParams(vmem_limit_bytes=limit * MIB), **more,
        )

    def send(value, pairs):
        return lax.ppermute(value, both, pairs)

    few, planes, rows, block = (VMEM(v, jnp.float32) for v in ((4, ny, nz), (5, ny, nz), (ROWS, nx, nz), density.shape))
    shapes = (few, planes, rows, rows, block, block)
    far, near, xs, dg, dens, src = pl.pallas_call(
        functools.partial(load_kernel, sizes), out_shape=shapes, in_specs=[hbm] * 2, out_specs=(vmem,) * 6, name="load_kernel",
        scratch_shapes=[VMEM((1, nz // LANES, ny + 2 * TILE, LANES), jnp.float32), pltpu.SemaphoreType.DMA((2 * nx,))], compiler_params=pltpu.CompilerParams(vmem_limit_bytes=8 * MIB),
    )(*(pltpu.with_memory_space_constraint(v, pltpu.HBM) for v in (density, source)))
    far = send(far, far_pairs)
    near = send(near, near_pairs)
    rxs = send(xs, ynear_pairs)
    rdg = send(dg, yfar_pairs)
    corner = VMEM((4, TILE, nz), jnp.float32)
    rfc, rnc = call(corner_kernel, 4, (corner, corner), 4)(rxs, rdg, dens, src)
    rfc = send(rfc, far_pairs)
    rnc = send(rnc, near_pairs)

    ext = VMEM((nx + 2 * DEEP, nz // LANES, ny + 2 * OFF, LANES), jnp.float32)
    sums = VMEM((SUMS, TILE, LANES), jnp.float32)
    held = call(inner_kernel, 2, (ext,) * 9, 8)(dens, src)
    held = call(beside_kernel, 10, (ext,) * 9, 8, input_output_aliases={1 + k: k for k in range(9)})(near, *held)
    dx, sx, wx, wy, wz, sc, g0, g1, w0 = held
    n0, part = call(inner_second_kernel, 7, (ext, sums), 8)(sx, wx, wy, wz, sc, g1, w0)
    held = (*held, n0)
    part, *held = call(edge_kernel, 14, (sums,) + (ext,) * 10, 8, input_output_aliases={4 + k: 1 + k for k in range(10)})(
        rxs, rdg, rnc, part, *held)
    mom, *held = call(far_kernel, 13, (VMEM((1, LANES), jnp.float32),) + (ext,) * 10, 8, input_output_aliases={3 + k: 1 + k for k in range(10)})(
        far, rfc, part, *held)
    dx, sx, wx, wy, wz, sc, g0, g1, w0, n0 = held

    n = nx_dev * ny_dev
    sent = jnp.broadcast_to(mom[None], (n, 1, LANES))
    got = lax.all_to_all(sent, both, 0, 0, tiled=True).reshape(n, LANES)
    whole = jax.ShapeDtypeStruct(density.shape, jnp.float32)
    plane = VMEM(density.shape, jnp.float32)
    return pl.pallas_call(
        last_kernel, out_shape=(whole, whole), in_specs=[vmem] * 5, out_specs=(hbm, hbm), name="last_kernel",
        scratch_shapes=[plane, plane, pltpu.SemaphoreType.DMA((2, nx))],
        compiler_params=pltpu.CompilerParams(vmem_limit_bytes=8 * MIB),
    )(got, sx, sc, w0, n0)


def solution(mesh):
    spec = P("gx", "gy", None)
    body = functools.partial(shards, mesh.shape["gx"], mesh.shape["gy"])
    return jax.shard_map(body, mesh=mesh, in_specs=(spec, spec), out_specs=(spec, spec), check_vma=False)
```

```python
import functools

import jax
import jax.numpy as jnp
from jax import lax
from jax.experimental import pallas as pl
from jax.experimental.pallas import tpu as pltpu
from jax.sharding import PartitionSpec as P


TILE = 8
LANES = 128
OFF = 16
DEEP = 3
ROWS = 5
STEP = 2
HALF = TILE // 2
PART = 16
SUMS = 5
MIB = 1 << 20
VMEM = pltpu.VMEM


def swaps(nx, ny):
    at = lambda x, y: x * ny + y
    near, far, ynear, yfar = [], [], [], []
    for x in range(nx):
        for y in range(ny):
            near.append((at(x, y), at(x ^ 1, y)))
            other = x - 1 if x % 2 == 0 else x + 1
            inside = 0 <= other < nx
            far.append((at(x, y), at(other, y) if inside else at(x, (y + ny // 2) % ny)))
            ynear.append((at(x, y), at(x, y ^ 1)))
            beside = y - 1 if y % 2 == 0 else y + 1
            within = 0 <= beside < ny
            yfar.append((at(x, y), at(x, beside) if within else at(x ^ 1, y)))
    return near, far, ynear, yfar


def position(sizes):
    ix, iy = lax.axis_index("gx"), lax.axis_index("gy")
    flags = (ix % 2 == 1, iy % 2 == 1, ix > 0, ix < sizes[0] - 1, iy > 0, iy < sizes[1] - 1)
    return [jnp.where(f, 1, 0) for f in flags]


def load_far_kernel(sizes, dens_hbm, src_hbm, far, dens, src, tall, sems):
    par = position(sizes)
    nx, ny, nz = dens_hbm.shape
    xodd = par[0] == 1
    copies = []
    for k in range(3):
        at = jnp.where(xodd, nx - 1 - k, k)
        for i, (a, b) in enumerate(((dens_hbm, dens), (src_hbm, src))):
            if k < 2 or a is dens_hbm:
                copies.append(pltpu.make_async_copy(a.at[pl.ds(at, 1)], b.at[pl.ds(k, 1)], sems.at[2 * k + i]))
    for copy in copies:
        copy.start()
    for copy in copies:
        copy.wait()
    far[0] = dens[0]
    far[1] = dens[1]
    far[2] = src[0]
    second = dens[1]
    put_plane(tall, 0, slice(TILE, TILE + ny), 0.5 * second)
    lane = lax.broadcasted_iota(jnp.int32, (TILE, LANES), 1)
    inner, first = lane < LANES - 1, lane == 0
    for r in range(0, ny, TILE):
        here = pl.ds(r + TILE, TILE)
        c = [tall[0, h, here] for h, _ in halves(nz)]
        z_up, z_down, _ = depth_weights(c, inner, first)
        for h, lanes in halves(nz):
            beside = [0.5 * dens[k, pl.ds(r, TILE), lanes] for k in (0, 2)]
            beside += [tall[0, h, pl.ds(r + TILE + 1, TILE)], tall[0, h, pl.ds(r + TILE - 1, TILE)]]
            w = [1.0 / (c[h] + v) for v in beside]
            s = lax.rsqrt((w[0] + w[1]) + (w[2] + w[3]) + (z_up[h] + z_down[h]))
            far[3, pl.ds(r, TILE), lanes] = s * (s * src[1, pl.ds(r, TILE), lanes])


def pack_kernel(sizes, dens, src, near, xs, dg):
    par = position(sizes)
    nx, ny, _ = dens.shape
    xodd, yodd = par[0] == 1, par[1] == 1
    d, s = jnp.where(xodd, 0, nx - 3), jnp.where(xodd, 0, nx - 2)
    for k in range(3):
        near[k] = dens[d + k]
    for k in range(2):
        near[3 + k] = src[s + k]
    for j in range(ROWS):
        ref, at = (dens, j) if j < DEEP else (src, j - DEEP)
        down, up = ref[:, at, :], ref[:, ny - 1 - at, :]
        xs[j] = jnp.where(yodd, down, up)
        dg[j] = jnp.where(yodd, up, down)


def corner_kernel(sizes, rxs, rdg, dens, src, far, near):
    par = position(sizes)
    xodd, yodd = par[0] == 1, par[1] == 1
    nx, ny, _ = dens.shape
    for out, backward in ((far, xodd), (near, jnp.logical_not(xodd))):
        at = [jnp.where(backward, nx - 1 - k, k) for k in range(3)]
        for k in range(2):
            for j in range(ROWS):
                a, b = rxs[j, pl.ds(at[k], 1), :], rdg[j, pl.ds(at[k], 1), :]
                out[k, j:j + 1] = jnp.where(yodd, a, b)
                out[2 + k, j:j + 1] = jnp.where(yodd, b, a)
        for side, row in ((0, 0), (1, ny - 1)):
            out[2 * side + 1, ROWS:ROWS + 1] = dens[at[2], row:row + 1]
            out[2 * side + 1, ROWS + 1:ROWS + 2] = src[at[1], row:row + 1]


class Stores:
    def __init__(self, depth):
        self.depth, self.held = depth, []

    def put(self, items):
        self.held.append(items)
        if len(self.held) > self.depth:
            self.flush(1)

    def flush(self, count=None):
        for items in self.held[:count]:
            for ref, at, value in items:
                ref[at] = value
        self.held = [] if count is None else self.held[count:]


def halves(nz):
    return [(h, slice(h * LANES, (h + 1) * LANES)) for h in range(nz // LANES)]


def loop(count, step):
    def body(k, carry):
        step(k)
        return carry

    lax.fori_loop(0, count, body, 0)


def put_plane(ref, e, rows, value):
    for h, lanes in halves(value.shape[-1]):
        ref[e, h, rows] = value[:, lanes]


def put_row(dx, sx, planes, ny, j, low, high):
    ref, depth = (dx, j) if j < DEEP else (sx, j - DEEP)
    if j < DEEP:
        low, high = 0.5 * low, 0.5 * high
    for value, at in ((low, OFF - 1 - depth), (high, OFF + ny + depth)):
        for h, lanes in halves(value.shape[-1]):
            ref[planes, h, at, :] = value[:, lanes]


def depth_weights(c, inner, first):
    nh = len(c)
    turned = [pltpu.roll(v, LANES - 1, 1) for v in c]
    z_up, z_in = [], []
    for h in range(nh):
        w = 1.0 / (c[h] + jnp.where(inner, turned[h], turned[h + 1] if h + 1 < nh else 0.0))
        z_up.append(w)
        z_in.append(w if h + 1 < nh else jnp.where(inner, w, 0.0))
    back = [pltpu.roll(v, 1, 1) for v in z_in]
    z_down = [jnp.where(first, back[h - 1] if h else 1.0 / c[0], back[h]) for h in range(nh)]
    return z_up, z_down, z_in


def weigh(dx, sx, wx, wy, wz, sc, g0, lo, count, tiles, unroll=1):
    nh = dx.shape[1]
    lane = lax.broadcasted_iota(jnp.int32, (TILE, LANES), 1)
    inner, first = lane < LANES - 1, lane == 0
    for r in tiles:
        for h in range(nh):
            wx[lo - 1, h, pl.ds(r, TILE)] = 1.0 / (dx[lo - 1, h, pl.ds(r, TILE)] + dx[lo, h, pl.ds(r, TILE)])

    def plane(k, carry):
        e = lo + k
        stores = Stores(1)
        for r in tiles:
            here = pl.ds(r, TILE)
            c = [dx[e, h, here] for h in range(nh)]
            beside = [(dx[e + 1, h, here], wx[e - 1, h, here], dx[e, h, pl.ds(r + 1, TILE)], dx[e, h, pl.ds(r - 1, TILE)], sx[e, h, here])
                      for h in range(nh)]
            z_up, z_down, z_in = depth_weights(c, inner, first)
            items = [(wz, (e, h, here), z_in[h]) for h in range(nh)]
            for h in range(nh):
                above, x_down, after, before, source = beside[h]
                x_up = 1.0 / (c[h] + above)
                y_up = 1.0 / (c[h] + after)
                y_down = 1.0 / (c[h] + before)
                diag = (x_up + x_down) + (y_up + y_down) + (z_up[h] + z_down[h])
                s = lax.rsqrt(diag)
                items += [(wx, (e, h, here), x_up), (wy, (e, h, here), y_up), (sc, (e, h, here), s), (g0, (e, h, here), s * (s * source))]
            stores.put(items)
        stores.flush()
        return carry

    lax.fori_loop(0, count, plane, 0, unroll=unroll)


def couple(g, wx, wy, wz, e, r, nh, inner, first):
    here = pl.ds(r, TILE)
    c = [g[e, h, here] for h in range(nh)]
    w = [wz[e, h, here] for h in range(nh)]
    ahead = [pltpu.roll(v, LANES - 1, 1) for v in c]
    behind = [pltpu.roll(a * b, 1, 1) for a, b in zip(w, c)]
    out = []
    for h in range(nh):
        t = wx[e, h, here] * g[e + 1, h, here] + wx[e - 1, h, here] * g[e - 1, h, here]
        t = t + (wy[e, h, here] * g[e, h, pl.ds(r + 1, TILE)] + wy[e, h, pl.ds(r - 1, TILE)] * g[e, h, pl.ds(r - 1, TILE)])
        after = jnp.where(inner, ahead[h], ahead[h + 1]) if h + 1 < nh else ahead[h]
        before = jnp.where(first, behind[h - 1], behind[h])
        out.append(t + (w[h] * after + before))
    return out


def apply_first(sx, wx, wy, wz, sc, g0, g1, w0, lo, count, tiles, unroll=1):
    nh = sx.shape[1]
    lane = lax.broadcasted_iota(jnp.int32, (TILE, LANES), 1)
    inner, first = lane < LANES - 1, lane == 0

    def plane(k, carry):
        e = lo + k
        stores = Stores(1)
        for r in tiles:
            here = pl.ds(r, TILE)
            t = couple(g0, wx, wy, wz, e, r, nh, inner, first)
            items = []
            for h in range(nh):
                s = sc[e, h, here]
                v = s * sx[e, h, here] - s * t[h]
                items += [(w0, (e, h, here), v), (g1, (e, h, here), s * v)]
            stores.put(items)
        stores.flush()
        return carry

    lax.fori_loop(0, count, plane, 0, unroll=unroll)


def clear_rows(par, g1):
    _, nh, rows, _ = g1.shape
    zero = jnp.zeros((TILE, LANES), jnp.float32)
    for flag, at in ((par[4], OFF - TILE), (par[5], rows - OFF)):

        @pl.when(flag == 0)
        def _():
            for k in range(g1.shape[0]):
                for h in range(nh):
                    g1[k, h, pl.ds(at, TILE)] = zero


def clear_plane(g1, e, has, tiles):
    zero = jnp.zeros((TILE, LANES), jnp.float32)

    @pl.when(has == 0)
    def _():
        for r in tiles:
            for h in range(g1.shape[1]):
                g1[e, h, pl.ds(r, TILE)] = zero


def apply_second(sx, wx, wy, wz, sc, g1, w0, n0, lo, count, tiles, sums, unroll=1, edges=False):
    row = lax.broadcasted_iota(jnp.int32, (TILE, LANES), 0)
    nh = sx.shape[1]
    lane = lax.broadcasted_iota(jnp.int32, (TILE, LANES), 1)
    inner, first = lane < LANES - 1, lane == 0

    def plane(k, sums):
        e = lo + k
        sums = list(sums)
        stores = Stores(2)
        for r in tiles:
            t = couple(g1, wx, wy, wz, e, r, nh, inner, first)
            for h in range(nh):
                s = sc[e, h, pl.ds(r, TILE)]
                a = s * sx[e, h, pl.ds(r, TILE)]
                b = w0[e, h, pl.ds(r, TILE)]
                c = b - s * t[h]
                stores.put([(n0, (e, h, pl.ds(r, TILE)), c)])
                if edges:
                    own = row >= HALF if r < OFF else row < HALF
                    a, b, c = (jnp.where(own, v, 0.0) for v in (a, b, c))
                for i, term in enumerate((a * a, b * a, b * b, c * b, c * a)):
                    sums[i] = sums[i] + term
        stores.flush()
        return tuple(sums)

    return lax.fori_loop(0, count, plane, tuple(sums), unroll=unroll)


def beyond(nx, upper, depth):
    return jnp.where(upper, nx + DEEP - 1 + depth, DEEP - depth)


def put_corners(dx, sx, corners, upper, has_down, has_up):
    nx, ny = dx.shape[0] - 2 * DEEP, dx.shape[2] - 2 * OFF
    for k in range(2):
        e = beyond(nx, upper, k + 1)
        for j in range(ROWS):
            low, high = corners[k, j:j + 1], corners[2 + k, j:j + 1]
            put_row(dx, sx, pl.ds(e, 1), ny, j, jnp.where(has_down, low, 0.0), jnp.where(has_up, high, 0.0))


def row_tiles(first, last):
    tiles = list(range(first, last - TILE + 1, TILE))
    if tiles[-1] + TILE < last:
        tiles.append(last - TILE)
    return [OFF + r for r in tiles]


def edge_tiles(ny):
    return [OFF - HALF, OFF + ny - HALF]


def near_side(par):
    xodd = par[0] == 1
    return jnp.where(xodd, 1, 4), jnp.where(xodd, 2, 5), jnp.where(xodd, 3, 6), jnp.where(xodd, par[2], par[3])


def inner_kernel(sizes, dens, src, dx, sx, wx, wy, wz, sc, g0, g1, w0, n0, mom):
    nx, ny, _ = dens.shape
    own = slice(OFF, OFF + ny)

    def fill(k):
        put_plane(dx, k + DEEP, own, 0.5 * dens[k])
        put_plane(sx, k + DEEP, own, src[k])

    loop(nx, fill)
    weigh(dx, sx, wx, wy, wz, sc, g0, DEEP + 1, nx - 2, row_tiles(1, ny - 1), unroll=2)
    apply_first(sx, wx, wy, wz, sc, g0, g1, w0, DEEP + 2, nx - 4, row_tiles(2, ny - 2), unroll=4)
    zero = jnp.zeros((TILE, LANES), jnp.float32)
    sums = apply_second(sx, wx, wy, wz, sc, g1, w0, n0, DEEP + 3, nx - 6, row_tiles(HALF, ny - HALF), (zero,) * SUMS)
    for i in range(SUMS):
        mom[i] = sums[i]


def beside_kernel(sizes, near, *refs):
    dx, sx, wx, wy, wz, sc, g0, g1, w0 = refs[9:]
    par = position(sizes)
    ny = near.shape[1]
    nx = dx.shape[0] - 2 * DEEP
    xodd = par[0] == 1
    has = near_side(par)[3]
    has_near = has == 1
    own = slice(OFF, OFF + ny)
    near_third, near_beyond = jnp.where(xodd, 0, nx + 3), jnp.where(xodd, 1, nx + 3)
    loop(3, lambda k: put_plane(dx, near_third + k, own, jnp.where(has_near, 0.5 * near[k], 0.0)))
    loop(2, lambda k: put_plane(sx, near_beyond + k, own, jnp.where(has_near, near[3 + k], 0.0)))
    weigh(dx, sx, wx, wy, wz, sc, g0, jnp.where(xodd, 1, nx + 2), 3, row_tiles(1, ny - 1), unroll=1)
    apply_first(sx, wx, wy, wz, sc, g0, g1, w0, jnp.where(xodd, 2, nx + 1), 3, row_tiles(2, ny - 2), unroll=3)
    clear_plane(g1, jnp.where(xodd, 2, nx + 3), has, row_tiles(2, ny - 2))


def inner_second_kernel(sizes, sx, wx, wy, wz, sc, g1, w0, part, n0_in, n0, mom):
    par = position(sizes)
    nx, ny = sx.shape[0] - 2 * DEEP, sx.shape[2] - 2 * OFF
    third = jnp.where(par[0] == 1, DEEP, nx)
    sums = apply_second(sx, wx, wy, wz, sc, g1, w0, n0, third, 3, row_tiles(HALF, ny - HALF), [part[i] for i in range(SUMS)], unroll=3)
    for i in range(SUMS):
        mom[i] = sums[i]


def edge_kernel(sizes, rxs, rdg, rnc, part, *refs):
    par = position(sizes)
    mom, dx, sx, wx, wy, wz, sc, g0, g1, w0, n0 = refs[10:]
    nx = dx.shape[0] - 2 * DEEP
    ny = dx.shape[2] - 2 * OFF
    xodd, yodd = par[0] == 1, par[1] == 1
    first, second, third, has = near_side(par)
    has_near, has_down, has_up = has == 1, par[4] == 1, par[5] == 1
    for j in range(ROWS):
        a, b = rxs[j], rdg[j]
        low, high = jnp.where(yodd, a, b), jnp.where(yodd, b, a)
        put_row(dx, sx, pl.ds(DEEP, nx), ny, j, jnp.where(has_down, low, 0.0), jnp.where(has_up, high, 0.0))
    put_corners(dx, sx, rnc, jnp.logical_not(xodd), jnp.logical_and(has_near, has_down), jnp.logical_and(has_near, has_up))
    weigh(dx, sx, wx, wy, wz, sc, g0, first, nx + 1, edge_tiles(ny), unroll=9)
    apply_first(sx, wx, wy, wz, sc, g0, g1, w0, second, nx - 1, edge_tiles(ny), unroll=7)
    clear_plane(g1, jnp.where(xodd, 2, nx + 3), has, edge_tiles(ny))
    clear_rows(par, g1)
    sums = apply_second(sx, wx, wy, wz, sc, g1, w0, n0, third, nx - 3, edge_tiles(ny), [part[i] for i in range(SUMS)], unroll=5, edges=True)
    for i in range(SUMS):
        mom[i] = sums[i]


def far_side(par, nx):
    xodd = par[0] == 1
    return jnp.where(xodd, nx + 2, 2), jnp.where(xodd, nx + 1, 2), jnp.where(xodd, nx, 3), jnp.where(xodd, par[3], par[2])


def far_kernel(sizes, far, part, *refs):
    mom, dx, sx, wx, wy, wz, sc, g0, g1, w0, n0 = refs[10:]
    par = position(sizes)
    ny = far.shape[1]
    nx = dx.shape[0] - 2 * DEEP
    first, second, third, has = far_side(par, nx)
    has_far = has == 1
    own = slice(OFF, OFF + ny)
    e1, e2 = (beyond(nx, par[0] == 1, d) for d in (1, 2))
    put_plane(dx, e1, own, jnp.where(has_far, 0.5 * far[0], 0.0))
    put_plane(dx, e2, own, jnp.where(has_far, 0.5 * far[1], 0.0))
    put_plane(sx, e1, own, jnp.where(has_far, far[2], 0.0))
    put_plane(g0, e2, own, jnp.where(has_far, far[3], 0.0))
    weigh(dx, sx, wx, wy, wz, sc, g0, first, 2, row_tiles(1, ny - 1))
    apply_first(sx, wx, wy, wz, sc, g0, g1, w0, second, 3, row_tiles(2, ny - 2), unroll=3)
    clear_plane(g1, e1, has, row_tiles(2, ny - 2))
    sums = apply_second(sx, wx, wy, wz, sc, g1, w0, n0, third, 3, row_tiles(HALF, ny - HALF), [part[i] for i in range(SUMS)], unroll=3)
    for i in range(SUMS):
        mom[i] = sums[i]


def far_edge_kernel(sizes, rfc, part, *refs):
    mom, dx, sx, wx, wy, wz, sc, g0, g1, w0, n0 = refs[10:]
    par = position(sizes)
    nx, ny = dx.shape[0] - 2 * DEEP, dx.shape[2] - 2 * OFF
    nz = rfc.shape[-1]
    xodd = par[0] == 1
    first_plane, second, third, has = far_side(par, nx)
    has_far = has == 1
    has_down, has_up = jnp.logical_and(has_far, par[4] == 1), jnp.logical_and(has_far, par[5] == 1)
    e1, e2 = (beyond(nx, xodd, d) for d in (1, 2))
    put_corners(dx, sx, rfc, xodd, has_down, has_up)
    lane = lax.broadcasted_iota(jnp.int32, (TILE, LANES), 1)
    row = lax.broadcasted_iota(jnp.int32, (TILE, LANES), 0)
    inner, first = lane < LANES - 1, lane == 0
    for side, r in ((0, OFF), (1, OFF + ny - TILE)):
        here = pl.ds(r, TILE)
        c = [dx[e2, h, here] for h, _ in halves(nz)]
        z_up, z_down, _ = depth_weights(c, inner, first)
        for h, lanes in halves(nz):
            density = jnp.where(has_far, 0.5 * rfc[2 * side + 1, ROWS:ROWS + 1, lanes], 0.0)
            source = jnp.where(has_far, rfc[2 * side + 1, ROWS + 1:ROWS + 2, lanes], 0.0)
            w = [1.0 / (c[h] + v) for v in (density, dx[e1, h, here], dx[e2, h, pl.ds(r + 1, TILE)], dx[e2, h, pl.ds(r - 1, TILE)])]
            s = lax.rsqrt((w[0] + w[1]) + (w[2] + w[3]) + (z_up[h] + z_down[h]))
            g0[e2, h, here] = jnp.where(row == side * (TILE - 1), s * (s * source), g0[e2, h, here])
    weigh(dx, sx, wx, wy, wz, sc, g0, first_plane, 2, edge_tiles(ny), unroll=2)
    apply_first(sx, wx, wy, wz, sc, g0, g1, w0, second, 3, edge_tiles(ny), unroll=3)
    clear_plane(g1, e1, has, edge_tiles(ny))
    clear_rows(par, g1)
    sums = apply_second(sx, wx, wy, wz, sc, g1, w0, n0, third, 3, edge_tiles(ny), [part[i] for i in range(SUMS)], unroll=3, edges=True)
    place = lax.broadcasted_iota(jnp.int32, (1, LANES), 1) // PART
    out = jnp.zeros((1, LANES), jnp.float32)
    for k, v in enumerate(sums):
        p = jnp.sum(v, axis=0, keepdims=True)
        width = LANES // 2
        while width >= PART:
            p = p + pltpu.roll(p, width, 1)
            width //= 2
        out = jnp.where(place == k, p, out)
    mom[...] = out


def last_kernel(mom, sx, sc, w0, n0, p_out, r_out, p_buf, r_buf, sems):
    place = lax.broadcasted_iota(jnp.int32, mom.shape, 1) // PART
    m = mom[...]

    def whole(v):
        return jnp.sum(jnp.sum(v, axis=0, keepdims=True), axis=1, keepdims=True)

    def lanes(k):
        return pltpu.roll(m, (LANES - k * PART) % LANES, 1) if k else m

    head = place == 0
    m0, m1, m2, m3, m4 = (jnp.where(head, lanes(k), 0.0) for k in range(SUMS))
    gamma0 = whole(m0)
    delta0 = whole(m1)
    a0 = gamma0 / delta0
    gamma1 = whole(m0 - a0 * (m1 + m1 - a0 * m2))
    delta1 = whole(m1 - a0 * (m4 + m2 - a0 * m3))
    b1 = gamma1 / gamma0
    a1 = gamma1 / (delta1 - b1 * gamma1 / a0)
    nx, ny, nz = p_out.shape
    c = jnp.broadcast_to(a0 + (a1 + a1 * b1), (TILE, LANES))
    d = jnp.broadcast_to(a0 * a1, (TILE, LANES))

    def out(i):
        here = pl.ds(i * STEP, STEP)
        return (pltpu.make_async_copy(p_buf.at[here], p_out.at[here], sems.at[0, i]),
                pltpu.make_async_copy(r_buf.at[here], r_out.at[here], sems.at[1, i]))

    def group(i, carry):
        for k in range(STEP):
            plane = i * STEP + k
            e = plane + DEEP
            stores = Stores(2)
            for r in range(0, ny, TILE):
                here, there = pl.ds(OFF + r, TILE), pl.ds(r, TILE)
                items = []
                for h, at in halves(nz):
                    s, q, v0, v1 = sc[e, h, here], sx[e, h, here], w0[e, h, here], n0[e, h, here]
                    r0 = s * q
                    items.append((p_buf, (plane, there, at), s * (c * r0 - d * v0)))
                    items.append((r_buf, (plane, there, at), r0 - c * v0 + d * v1))
                stores.put(items)
            stores.flush()
        for copy in out(i):
            copy.start()
        return carry

    lax.fori_loop(0, nx // STEP, group, 0)
    for i in range(nx // STEP):
        for copy in out(i):
            copy.wait()


def shards(nx_dev, ny_dev, source, density):
    both = ("gx", "gy")
    near_pairs, far_pairs, ynear_pairs, yfar_pairs = swaps(nx_dev, ny_dev)
    nx, ny, nz = density.shape
    sizes = (nx_dev, ny_dev)
    vmem = pl.BlockSpec(memory_space=VMEM)
    hbm = pl.BlockSpec(memory_space=pltpu.HBM)

    def call(body, n_in, outs, limit, **more):
        return pl.pallas_call(
            functools.partial(body, sizes), out_shape=outs, in_specs=[vmem] * n_in, out_specs=jax.tree.map(lambda _: vmem, outs),
            compiler_params=pltpu.CompilerParams(vmem_limit_bytes=limit * MIB), **more,
        )

    def send(value, pairs):
        return lax.ppermute(value, both, pairs)

    few, planes, rows = (VMEM(v, jnp.float32) for v in ((4, ny, nz), (5, ny, nz), (ROWS, nx, nz)))
    far = pl.pallas_call(
        functools.partial(load_far_kernel, sizes), out_shape=few, in_specs=[hbm] * 2, out_specs=vmem, name="load_far_kernel",
        scratch_shapes=[VMEM((3, ny, nz), jnp.float32), VMEM((2, ny, nz), jnp.float32),
                        VMEM((1, nz // LANES, ny + 2 * TILE, LANES), jnp.float32), pltpu.SemaphoreType.DMA((5,))],
        compiler_params=pltpu.CompilerParams(vmem_limit_bytes=8 * MIB),
    )(*(pltpu.with_memory_space_constraint(v, pltpu.HBM) for v in (density, source)))
    dens, src = density, source
    near, xs, dg = call(pack_kernel, 2, (planes, rows, rows), 4)(dens, src)
    far = send(far, far_pairs)
    near = send(near, near_pairs)
    rxs = send(xs, ynear_pairs)
    rdg = send(dg, yfar_pairs)
    corner = VMEM((4, TILE, nz), jnp.float32)
    rfc, rnc = call(corner_kernel, 4, (corner, corner), 4)(rxs, rdg, dens, src)
    rfc = send(rfc, far_pairs)
    rnc = send(rnc, near_pairs)

    ext = VMEM((nx + 2 * DEEP, nz // LANES, ny + 2 * OFF, LANES), jnp.float32)
    sums = VMEM((SUMS, TILE, LANES), jnp.float32)
    *held, n0, part = call(inner_kernel, 2, (ext,) * 10 + (sums,), 8)(dens, src)
    held = call(beside_kernel, 10, (ext,) * 9, 8, input_output_aliases={1 + k: k for k in range(9)})(near, *held)
    dx, sx, wx, wy, wz, sc, g0, g1, w0 = held
    n0, part = call(inner_second_kernel, 9, (ext, sums), 8, input_output_aliases={8: 0})(sx, wx, wy, wz, sc, g1, w0, part, n0)
    held = (*held, n0)
    part, *held = call(edge_kernel, 14, (sums,) + (ext,) * 10, 8, input_output_aliases={4 + k: 1 + k for k in range(10)})(
        rxs, rdg, rnc, part, *held)
    part, *held = call(far_kernel, 12, (sums,) + (ext,) * 10, 8, input_output_aliases={2 + k: 1 + k for k in range(10)})(
        far, part, *held)
    mom, *held = call(far_edge_kernel, 12, (VMEM((1, LANES), jnp.float32),) + (ext,) * 10, 8, input_output_aliases={2 + k: 1 + k for k in range(10)})(
        rfc, part, *held)
    dx, sx, wx, wy, wz, sc, g0, g1, w0, n0 = held

    n = nx_dev * ny_dev
    sent = jnp.broadcast_to(mom[None], (n, 1, LANES))
    got = lax.all_to_all(sent, both, 0, 0, tiled=True).reshape(n, LANES)
    whole = jax.ShapeDtypeStruct(density.shape, jnp.float32)
    plane = VMEM(density.shape, jnp.float32)
    return pl.pallas_call(
        last_kernel, out_shape=(whole, whole), in_specs=[vmem] * 5, out_specs=(hbm, hbm), name="last_kernel",
        scratch_shapes=[plane, plane, pltpu.SemaphoreType.DMA((2, nx))],
        compiler_params=pltpu.CompilerParams(vmem_limit_bytes=8 * MIB),
    )(got, sx, sc, w0, n0)


def solution(mesh):
    spec = P("gx", "gy", None)
    body = functools.partial(shards, mesh.shape["gx"], mesh.shape["gy"])
    return jax.shard_map(body, mesh=mesh, in_specs=(spec, spec), out_specs=(spec, spec), check_vma=False)
```

```python
import functools

import jax
import jax.numpy as jnp
from jax import lax
from jax.experimental import pallas as pl
from jax.experimental.pallas import tpu as pltpu
from jax.sharding import PartitionSpec as P


TILE = 8
LANES = 128
OFF = 16
DEEP = 3
ROWS = 5
STEP = 1
HALF = TILE // 2
PART = 16
SUMS = 5
MIB = 1 << 20
VMEM = pltpu.VMEM


def swaps(nx, ny):
    at = lambda x, y: x * ny + y
    near, far, ynear, yfar = [], [], [], []
    for x in range(nx):
        for y in range(ny):
            near.append((at(x, y), at(x ^ 1, y)))
            other = x - 1 if x % 2 == 0 else x + 1
            inside = 0 <= other < nx
            far.append((at(x, y), at(other, y) if inside else at(x, (y + ny // 2) % ny)))
            ynear.append((at(x, y), at(x, y ^ 1)))
            beside = y - 1 if y % 2 == 0 else y + 1
            within = 0 <= beside < ny
            yfar.append((at(x, y), at(x, beside) if within else at(x ^ 1, y)))
    return near, far, ynear, yfar


def position(sizes):
    ix, iy = lax.axis_index("gx"), lax.axis_index("gy")
    flags = (ix % 2 == 1, iy % 2 == 1, ix > 0, ix < sizes[0] - 1, iy > 0, iy < sizes[1] - 1)
    return [jnp.where(f, 1, 0) for f in flags]


def load_far_kernel(sizes, dens_hbm, src_hbm, far, dens, src, tall, sems):
    par = position(sizes)
    nx, ny, nz = dens_hbm.shape
    xodd = par[0] == 1
    copies = []
    for k in range(3):
        at = jnp.where(xodd, nx - 1 - k, k)
        for i, (a, b) in enumerate(((dens_hbm, dens), (src_hbm, src))):
            if k < 2 or a is dens_hbm:
                copies.append(pltpu.make_async_copy(a.at[pl.ds(at, 1)], b.at[pl.ds(k, 1)], sems.at[2 * k + i]))
    for copy in copies:
        copy.start()
    for copy in copies:
        copy.wait()
    far[0] = dens[0]
    far[1] = dens[1]
    far[2] = src[0]
    second = dens[1]
    put_plane(tall, 0, slice(TILE, TILE + ny), 0.5 * second)
    lane = lax.broadcasted_iota(jnp.int32, (TILE, LANES), 1)
    inner, first = lane < LANES - 1, lane == 0
    for r in range(0, ny, TILE):
        here = pl.ds(r + TILE, TILE)
        c = [tall[0, h, here] for h, _ in halves(nz)]
        z_up, z_down, _ = depth_weights(c, inner, first)
        for h, lanes in halves(nz):
            beside = [0.5 * dens[k, pl.ds(r, TILE), lanes] for k in (0, 2)]
            beside += [tall[0, h, pl.ds(r + TILE + 1, TILE)], tall[0, h, pl.ds(r + TILE - 1, TILE)]]
            w = [1.0 / (c[h] + v) for v in beside]
            s = lax.rsqrt((w[0] + w[1]) + (w[2] + w[3]) + (z_up[h] + z_down[h]))
            far[3, pl.ds(r, TILE), lanes] = s * (s * src[1, pl.ds(r, TILE), lanes])


def pack_kernel(sizes, dens, src, near, xs, dg):
    par = position(sizes)
    nx, ny, _ = dens.shape
    xodd, yodd = par[0] == 1, par[1] == 1
    d, s = jnp.where(xodd, 0, nx - 3), jnp.where(xodd, 0, nx - 2)
    for k in range(3):
        near[k] = dens[d + k]
    for k in range(2):
        near[3 + k] = src[s + k]
    for j in range(ROWS):
        ref, at = (dens, j) if j < DEEP else (src, j - DEEP)
        down, up = ref[:, at, :], ref[:, ny - 1 - at, :]
        xs[j] = jnp.where(yodd, down, up)
        dg[j] = jnp.where(yodd, up, down)


def corner_kernel(sizes, rxs, rdg, dens, src, far, near):
    par = position(sizes)
    xodd, yodd = par[0] == 1, par[1] == 1
    nx, ny, _ = dens.shape
    for out, backward in ((far, xodd), (near, jnp.logical_not(xodd))):
        at = [jnp.where(backward, nx - 1 - k, k) for k in range(3)]
        for k in range(2):
            for j in range(ROWS):
                a, b = rxs[j, pl.ds(at[k], 1), :], rdg[j, pl.ds(at[k], 1), :]
                out[k, j:j + 1] = jnp.where(yodd, a, b)
                out[2 + k, j:j + 1] = jnp.where(yodd, b, a)
        for side, row in ((0, 0), (1, ny - 1)):
            out[2 * side + 1, ROWS:ROWS + 1] = dens[at[2], row:row + 1]
            out[2 * side + 1, ROWS + 1:ROWS + 2] = src[at[1], row:row + 1]


class Stores:
    def __init__(self, depth):
        self.depth, self.held = depth, []

    def put(self, items):
        self.held.append(items)
        if len(self.held) > self.depth:
            self.flush(1)

    def flush(self, count=None):
        for items in self.held[:count]:
            for ref, at, value in items:
                ref[at] = value
        self.held = [] if count is None else self.held[count:]


def halves(nz):
    return [(h, slice(h * LANES, (h + 1) * LANES)) for h in range(nz // LANES)]


def loop(count, step):
    def body(k, carry):
        step(k)
        return carry

    lax.fori_loop(0, count, body, 0)


def put_plane(ref, e, rows, value):
    for h, lanes in halves(value.shape[-1]):
        ref[e, h, rows] = value[:, lanes]


def put_row(dx, sx, planes, ny, j, low, high):
    ref, depth = (dx, j) if j < DEEP else (sx, j - DEEP)
    if j < DEEP:
        low, high = 0.5 * low, 0.5 * high
    for value, at in ((low, OFF - 1 - depth), (high, OFF + ny + depth)):
        for h, lanes in halves(value.shape[-1]):
            ref[planes, h, at, :] = value[:, lanes]


def depth_weights(c, inner, first):
    nh = len(c)
    turned = [pltpu.roll(v, LANES - 1, 1) for v in c]
    z_up, z_in = [], []
    for h in range(nh):
        w = 1.0 / (c[h] + jnp.where(inner, turned[h], turned[h + 1] if h + 1 < nh else 0.0))
        z_up.append(w)
        z_in.append(w if h + 1 < nh else jnp.where(inner, w, 0.0))
    back = [pltpu.roll(v, 1, 1) for v in z_in]
    z_down = [jnp.where(first, back[h - 1] if h else 1.0 / c[0], back[h]) for h in range(nh)]
    return z_up, z_down, z_in


def weigh(dx, sx, wx, wy, wz, sc, g0, lo, count, tiles, unroll=1):
    nh = dx.shape[1]
    lane = lax.broadcasted_iota(jnp.int32, (TILE, LANES), 1)
    inner, first = lane < LANES - 1, lane == 0
    for r in tiles:
        for h in range(nh):
            wx[lo - 1, h, pl.ds(r, TILE)] = 1.0 / (dx[lo - 1, h, pl.ds(r, TILE)] + dx[lo, h, pl.ds(r, TILE)])

    def plane(k, carry):
        e = lo + k
        stores = Stores(1)
        for r in tiles:
            here = pl.ds(r, TILE)
            c = [dx[e, h, here] for h in range(nh)]
            beside = [(dx[e + 1, h, here], wx[e - 1, h, here], dx[e, h, pl.ds(r + 1, TILE)], dx[e, h, pl.ds(r - 1, TILE)], sx[e, h, here])
                      for h in range(nh)]
            z_up, z_down, z_in = depth_weights(c, inner, first)
            items = [(wz, (e, h, here), z_in[h]) for h in range(nh)]
            for h in range(nh):
                above, x_down, after, before, source = beside[h]
                x_up = 1.0 / (c[h] + above)
                y_up = 1.0 / (c[h] + after)
                y_down = 1.0 / (c[h] + before)
                diag = (x_up + x_down) + (y_up + y_down) + (z_up[h] + z_down[h])
                s = lax.rsqrt(diag)
                items += [(wx, (e, h, here), x_up), (wy, (e, h, here), y_up), (sc, (e, h, here), s), (g0, (e, h, here), s * (s * source))]
            stores.put(items)
        stores.flush()
        return carry

    lax.fori_loop(0, count, plane, 0, unroll=unroll)


def couple(g, wx, wy, wz, e, r, nh, inner, first):
    here = pl.ds(r, TILE)
    c = [g[e, h, here] for h in range(nh)]
    w = [wz[e, h, here] for h in range(nh)]
    ahead = [pltpu.roll(v, LANES - 1, 1) for v in c]
    behind = [pltpu.roll(a * b, 1, 1) for a, b in zip(w, c)]
    out = []
    for h in range(nh):
        t = wx[e, h, here] * g[e + 1, h, here] + wx[e - 1, h, here] * g[e - 1, h, here]
        t = t + (wy[e, h, here] * g[e, h, pl.ds(r + 1, TILE)] + wy[e, h, pl.ds(r - 1, TILE)] * g[e, h, pl.ds(r - 1, TILE)])
        after = jnp.where(inner, ahead[h], ahead[h + 1]) if h + 1 < nh else ahead[h]
        before = jnp.where(first, behind[h - 1], behind[h])
        out.append(t + (w[h] * after + before))
    return out


def apply_first(sx, wx, wy, wz, sc, g0, g1, w0, lo, count, tiles, unroll=1):
    nh = sx.shape[1]
    lane = lax.broadcasted_iota(jnp.int32, (TILE, LANES), 1)
    inner, first = lane < LANES - 1, lane == 0

    def plane(k, carry):
        e = lo + k
        stores = Stores(1)
        for r in tiles:
            here = pl.ds(r, TILE)
            t = couple(g0, wx, wy, wz, e, r, nh, inner, first)
            items = []
            for h in range(nh):
                s = sc[e, h, here]
                v = s * sx[e, h, here] - s * t[h]
                items += [(w0, (e, h, here), v), (g1, (e, h, here), s * v)]
            stores.put(items)
        stores.flush()
        return carry

    lax.fori_loop(0, count, plane, 0, unroll=unroll)


def clear_rows(par, g1):
    _, nh, rows, _ = g1.shape
    zero = jnp.zeros((TILE, LANES), jnp.float32)
    for flag, at in ((par[4], OFF - TILE), (par[5], rows - OFF)):

        @pl.when(flag == 0)
        def _():
            for k in range(g1.shape[0]):
                for h in range(nh):
                    g1[k, h, pl.ds(at, TILE)] = zero


def clear_plane(g1, e, has, tiles):
    zero = jnp.zeros((TILE, LANES), jnp.float32)

    @pl.when(has == 0)
    def _():
        for r in tiles:
            for h in range(g1.shape[1]):
                g1[e, h, pl.ds(r, TILE)] = zero


def apply_second(sx, wx, wy, wz, sc, g1, w0, n0, lo, count, tiles, sums, unroll=1, edges=False):
    row = lax.broadcasted_iota(jnp.int32, (TILE, LANES), 0)
    nh = sx.shape[1]
    lane = lax.broadcasted_iota(jnp.int32, (TILE, LANES), 1)
    inner, first = lane < LANES - 1, lane == 0

    def plane(k, sums):
        e = lo + k
        sums = list(sums)
        stores = Stores(2)
        for r in tiles:
            t = couple(g1, wx, wy, wz, e, r, nh, inner, first)
            for h in range(nh):
                s = sc[e, h, pl.ds(r, TILE)]
                a = s * sx[e, h, pl.ds(r, TILE)]
                b = w0[e, h, pl.ds(r, TILE)]
                c = b - s * t[h]
                stores.put([(n0, (e, h, pl.ds(r, TILE)), c)])
                if edges:
                    own = row >= HALF if r < OFF else row < HALF
                    a, b, c = (jnp.where(own, v, 0.0) for v in (a, b, c))
                for i, term in enumerate((a * a, b * a, b * b, c * b, c * a)):
                    sums[i] = sums[i] + term
        stores.flush()
        return tuple(sums)

    return lax.fori_loop(0, count, plane, tuple(sums), unroll=unroll)


def beyond(nx, upper, depth):
    return jnp.where(upper, nx + DEEP - 1 + depth, DEEP - depth)


def put_corners(dx, sx, corners, upper, has_down, has_up):
    nx, ny = dx.shape[0] - 2 * DEEP, dx.shape[2] - 2 * OFF
    for k in range(2):
        e = beyond(nx, upper, k + 1)
        for j in range(ROWS):
            low, high = corners[k, j:j + 1], corners[2 + k, j:j + 1]
            put_row(dx, sx, pl.ds(e, 1), ny, j, jnp.where(has_down, low, 0.0), jnp.where(has_up, high, 0.0))


def row_tiles(first, last):
    tiles = list(range(first, last - TILE + 1, TILE))
    if tiles[-1] + TILE < last:
        tiles.append(last - TILE)
    return [OFF + r for r in tiles]


def edge_tiles(ny):
    return [OFF - HALF, OFF + ny - HALF]


def near_side(par):
    xodd = par[0] == 1
    return jnp.where(xodd, 1, 4), jnp.where(xodd, 2, 5), jnp.where(xodd, 3, 6), jnp.where(xodd, par[2], par[3])


def inner_kernel(sizes, dens, src, dx, sx, wx, wy, wz, sc, g0, g1, w0):
    nx, ny, _ = dens.shape
    own = slice(OFF, OFF + ny)

    def fill(k):
        put_plane(dx, k + DEEP, own, 0.5 * dens[k])
        put_plane(sx, k + DEEP, own, src[k])

    loop(nx, fill)
    weigh(dx, sx, wx, wy, wz, sc, g0, DEEP + 1, nx - 2, row_tiles(1, ny - 1), unroll=2)
    apply_first(sx, wx, wy, wz, sc, g0, g1, w0, DEEP + 2, nx - 4, row_tiles(2, ny - 2), unroll=4)


def beside_kernel(sizes, near, *refs):
    dx, sx, wx, wy, wz, sc, g0, g1, w0 = refs[9:]
    par = position(sizes)
    ny = near.shape[1]
    nx = dx.shape[0] - 2 * DEEP
    xodd = par[0] == 1
    has = near_side(par)[3]
    has_near = has == 1
    own = slice(OFF, OFF + ny)
    near_third, near_beyond = jnp.where(xodd, 0, nx + 3), jnp.where(xodd, 1, nx + 3)
    loop(3, lambda k: put_plane(dx, near_third + k, own, jnp.where(has_near, 0.5 * near[k], 0.0)))
    loop(2, lambda k: put_plane(sx, near_beyond + k, own, jnp.where(has_near, near[3 + k], 0.0)))
    weigh(dx, sx, wx, wy, wz, sc, g0, jnp.where(xodd, 1, nx + 2), 3, row_tiles(1, ny - 1), unroll=1)
    apply_first(sx, wx, wy, wz, sc, g0, g1, w0, jnp.where(xodd, 2, nx + 1), 3, row_tiles(2, ny - 2), unroll=3)
    clear_plane(g1, jnp.where(xodd, 2, nx + 3), has, row_tiles(2, ny - 2))


def inner_second_kernel(sizes, sx, wx, wy, wz, sc, g1, w0, n0, mom):
    par = position(sizes)
    nx, ny = sx.shape[0] - 2 * DEEP, sx.shape[2] - 2 * OFF
    third = near_side(par)[2]
    zero = jnp.zeros((TILE, LANES), jnp.float32)
    sums = apply_second(sx, wx, wy, wz, sc, g1, w0, n0, third, nx - 3, row_tiles(HALF, ny - HALF), (zero,) * SUMS, unroll=5)
    for i in range(SUMS):
        mom[i] = sums[i]


def edge_kernel(sizes, rxs, rdg, rnc, part, *refs):
    par = position(sizes)
    mom, dx, sx, wx, wy, wz, sc, g0, g1, w0, n0 = refs[10:]
    nx = dx.shape[0] - 2 * DEEP
    ny = dx.shape[2] - 2 * OFF
    xodd, yodd = par[0] == 1, par[1] == 1
    first, second, third, has = near_side(par)
    has_near, has_down, has_up = has == 1, par[4] == 1, par[5] == 1
    for j in range(ROWS):
        a, b = rxs[j], rdg[j]
        low, high = jnp.where(yodd, a, b), jnp.where(yodd, b, a)
        put_row(dx, sx, pl.ds(DEEP, nx), ny, j, jnp.where(has_down, low, 0.0), jnp.where(has_up, high, 0.0))
    put_corners(dx, sx, rnc, jnp.logical_not(xodd), jnp.logical_and(has_near, has_down), jnp.logical_and(has_near, has_up))
    weigh(dx, sx, wx, wy, wz, sc, g0, first, nx + 1, edge_tiles(ny), unroll=9)
    apply_first(sx, wx, wy, wz, sc, g0, g1, w0, second, nx - 1, edge_tiles(ny), unroll=7)
    clear_plane(g1, jnp.where(xodd, 2, nx + 3), has, edge_tiles(ny))
    clear_rows(par, g1)
    sums = apply_second(sx, wx, wy, wz, sc, g1, w0, n0, third, nx - 3, edge_tiles(ny), [part[i] for i in range(SUMS)], unroll=5, edges=True)
    for i in range(SUMS):
        mom[i] = sums[i]


def far_side(par, nx):
    xodd = par[0] == 1
    return jnp.where(xodd, nx + 2, 2), jnp.where(xodd, nx + 1, 2), jnp.where(xodd, nx, 3), jnp.where(xodd, par[3], par[2])


def far_kernel(sizes, far, part, *refs):
    mom, dx, sx, wx, wy, wz, sc, g0, g1, w0, n0 = refs[10:]
    par = position(sizes)
    ny = far.shape[1]
    nx = dx.shape[0] - 2 * DEEP
    first, second, third, has = far_side(par, nx)
    has_far = has == 1
    own = slice(OFF, OFF + ny)
    e1, e2 = (beyond(nx, par[0] == 1, d) for d in (1, 2))
    put_plane(dx, e1, own, jnp.where(has_far, 0.5 * far[0], 0.0))
    put_plane(dx, e2, own, jnp.where(has_far, 0.5 * far[1], 0.0))
    put_plane(sx, e1, own, jnp.where(has_far, far[2], 0.0))
    put_plane(g0, e2, own, jnp.where(has_far, far[3], 0.0))
    weigh(dx, sx, wx, wy, wz, sc, g0, first, 2, row_tiles(1, ny - 1))
    apply_first(sx, wx, wy, wz, sc, g0, g1, w0, second, 3, row_tiles(2, ny - 2), unroll=3)
    clear_plane(g1, e1, has, row_tiles(2, ny - 2))
    sums = apply_second(sx, wx, wy, wz, sc, g1, w0, n0, third, 3, row_tiles(HALF, ny - HALF), [part[i] for i in range(SUMS)], unroll=3)
    for i in range(SUMS):
        mom[i] = sums[i]


def far_edge_kernel(sizes, rfc, part, *refs):
    mom, dx, sx, wx, wy, wz, sc, g0, g1, w0, n0 = refs[10:]
    par = position(sizes)
    nx, ny = dx.shape[0] - 2 * DEEP, dx.shape[2] - 2 * OFF
    nz = rfc.shape[-1]
    xodd = par[0] == 1
    first_plane, second, third, has = far_side(par, nx)
    has_far = has == 1
    has_down, has_up = jnp.logical_and(has_far, par[4] == 1), jnp.logical_and(has_far, par[5] == 1)
    e1, e2 = (beyond(nx, xodd, d) for d in (1, 2))
    put_corners(dx, sx, rfc, xodd, has_down, has_up)
    lane = lax.broadcasted_iota(jnp.int32, (TILE, LANES), 1)
    row = lax.broadcasted_iota(jnp.int32, (TILE, LANES), 0)
    inner, first = lane < LANES - 1, lane == 0
    for side, r in ((0, OFF), (1, OFF + ny - TILE)):
        here = pl.ds(r, TILE)
        c = [dx[e2, h, here] for h, _ in halves(nz)]
        z_up, z_down, _ = depth_weights(c, inner, first)
        for h, lanes in halves(nz):
            density = jnp.where(has_far, 0.5 * rfc[2 * side + 1, ROWS:ROWS + 1, lanes], 0.0)
            source = jnp.where(has_far, rfc[2 * side + 1, ROWS + 1:ROWS + 2, lanes], 0.0)
            w = [1.0 / (c[h] + v) for v in (density, dx[e1, h, here], dx[e2, h, pl.ds(r + 1, TILE)], dx[e2, h, pl.ds(r - 1, TILE)])]
            s = lax.rsqrt((w[0] + w[1]) + (w[2] + w[3]) + (z_up[h] + z_down[h]))
            g0[e2, h, here] = jnp.where(row == side * (TILE - 1), s * (s * source), g0[e2, h, here])
    weigh(dx, sx, wx, wy, wz, sc, g0, first_plane, 2, edge_tiles(ny), unroll=2)
    apply_first(sx, wx, wy, wz, sc, g0, g1, w0, second, 3, edge_tiles(ny), unroll=3)
    clear_plane(g1, e1, has, edge_tiles(ny))
    clear_rows(par, g1)
    sums = apply_second(sx, wx, wy, wz, sc, g1, w0, n0, third, 3, edge_tiles(ny), [part[i] for i in range(SUMS)], unroll=3, edges=True)
    place = lax.broadcasted_iota(jnp.int32, (1, LANES), 1) // PART
    out = jnp.zeros((1, LANES), jnp.float32)
    for k, v in enumerate(sums):
        p = jnp.sum(v, axis=0, keepdims=True)
        width = LANES // 2
        while width >= PART:
            p = p + pltpu.roll(p, width, 1)
            width //= 2
        out = jnp.where(place == k, p, out)
    mom[...] = out


def last_kernel(mom, sx, sc, w0, n0, p_out, r_out, p_buf, r_buf, sems):
    place = lax.broadcasted_iota(jnp.int32, mom.shape, 1) // PART
    m = mom[...]

    def whole(v):
        return jnp.sum(jnp.sum(v, axis=0, keepdims=True), axis=1, keepdims=True)

    def lanes(k):
        return pltpu.roll(m, (LANES - k * PART) % LANES, 1) if k else m

    head = place == 0
    m0, m1, m2, m3, m4 = (jnp.where(head, lanes(k), 0.0) for k in range(SUMS))
    gamma0 = whole(m0)
    delta0 = whole(m1)
    a0 = gamma0 / delta0
    gamma1 = whole(m0 - a0 * (m1 + m1 - a0 * m2))
    delta1 = whole(m1 - a0 * (m4 + m2 - a0 * m3))
    b1 = gamma1 / gamma0
    a1 = gamma1 / (delta1 - b1 * gamma1 / a0)
    nx, ny, nz = p_out.shape
    c = jnp.broadcast_to(a0 + (a1 + a1 * b1), (TILE, LANES))
    d = jnp.broadcast_to(a0 * a1, (TILE, LANES))

    def out(i):
        here = pl.ds(i * STEP, STEP)
        return (pltpu.make_async_copy(p_buf.at[here], p_out.at[here], sems.at[0, i]),
                pltpu.make_async_copy(r_buf.at[here], r_out.at[here], sems.at[1, i]))

    def group(i, carry):
        for k in range(STEP):
            plane = i * STEP + k
            e = plane + DEEP
            stores = Stores(2)
            for r in range(0, ny, TILE):
                here, there = pl.ds(OFF + r, TILE), pl.ds(r, TILE)
                items = []
                for h, at in halves(nz):
                    s, q, v0, v1 = sc[e, h, here], sx[e, h, here], w0[e, h, here], n0[e, h, here]
                    r0 = s * q
                    items.append((p_buf, (plane, there, at), s * (c * r0 - d * v0)))
                    items.append((r_buf, (plane, there, at), r0 - c * v0 + d * v1))
                stores.put(items)
            stores.flush()
        for copy in out(i):
            copy.start()
        return carry

    lax.fori_loop(0, nx // STEP, group, 0)
    for i in range(nx // STEP):
        for copy in out(i):
            copy.wait()


def shards(nx_dev, ny_dev, source, density):
    both = ("gx", "gy")
    near_pairs, far_pairs, ynear_pairs, yfar_pairs = swaps(nx_dev, ny_dev)
    nx, ny, nz = density.shape
    sizes = (nx_dev, ny_dev)
    vmem = pl.BlockSpec(memory_space=VMEM)
    hbm = pl.BlockSpec(memory_space=pltpu.HBM)

    def call(body, n_in, outs, limit, **more):
        return pl.pallas_call(
            functools.partial(body, sizes), out_shape=outs, in_specs=[vmem] * n_in, out_specs=jax.tree.map(lambda _: vmem, outs),
            compiler_params=pltpu.CompilerParams(vmem_limit_bytes=limit * MIB), **more,
        )

    def send(value, pairs):
        return lax.ppermute(value, both, pairs)

    few, planes, rows = (VMEM(v, jnp.float32) for v in ((4, ny, nz), (5, ny, nz), (ROWS, nx, nz)))
    far = pl.pallas_call(
        functools.partial(load_far_kernel, sizes), out_shape=few, in_specs=[hbm] * 2, out_specs=vmem, name="load_far_kernel",
        scratch_shapes=[VMEM((3, ny, nz), jnp.float32), VMEM((2, ny, nz), jnp.float32),
                        VMEM((1, nz // LANES, ny + 2 * TILE, LANES), jnp.float32), pltpu.SemaphoreType.DMA((5,))],
        compiler_params=pltpu.CompilerParams(vmem_limit_bytes=8 * MIB),
    )(*(pltpu.with_memory_space_constraint(v, pltpu.HBM) for v in (density, source)))
    dens, src = density, source
    near, xs, dg = call(pack_kernel, 2, (planes, rows, rows), 4)(dens, src)
    far = send(far, far_pairs)
    near = send(near, near_pairs)
    rxs = send(xs, ynear_pairs)
    rdg = send(dg, yfar_pairs)
    corner = VMEM((4, TILE, nz), jnp.float32)
    rfc, rnc = call(corner_kernel, 4, (corner, corner), 4)(rxs, rdg, dens, src)
    rfc = send(rfc, far_pairs)
    rnc = send(rnc, near_pairs)

    ext = VMEM((nx + 2 * DEEP, nz // LANES, ny + 2 * OFF, LANES), jnp.float32)
    sums = VMEM((SUMS, TILE, LANES), jnp.float32)
    held = call(inner_kernel, 2, (ext,) * 9, 8)(dens, src)
    held = call(beside_kernel, 10, (ext,) * 9, 8, input_output_aliases={1 + k: k for k in range(9)})(near, *held)
    dx, sx, wx, wy, wz, sc, g0, g1, w0 = held
    n0, part = call(inner_second_kernel, 7, (ext, sums), 8)(sx, wx, wy, wz, sc, g1, w0)
    held = (*held, n0)
    part, *held = call(edge_kernel, 14, (sums,) + (ext,) * 10, 8, input_output_aliases={4 + k: 1 + k for k in range(10)})(
        rxs, rdg, rnc, part, *held)
    part, *held = call(far_kernel, 12, (sums,) + (ext,) * 10, 8, input_output_aliases={2 + k: 1 + k for k in range(10)})(
        far, part, *held)
    mom, *held = call(far_edge_kernel, 12, (VMEM((1, LANES), jnp.float32),) + (ext,) * 10, 8, input_output_aliases={2 + k: 1 + k for k in range(10)})(
        rfc, part, *held)
    dx, sx, wx, wy, wz, sc, g0, g1, w0, n0 = held

    n = nx_dev * ny_dev
    sent = jnp.broadcast_to(mom[None], (n, 1, LANES))
    got = lax.all_to_all(sent, both, 0, 0, tiled=True).reshape(n, LANES)
    whole = jax.ShapeDtypeStruct(density.shape, jnp.float32)
    plane = VMEM(density.shape, jnp.float32)
    return pl.pallas_call(
        last_kernel, out_shape=(whole, whole), in_specs=[vmem] * 5, out_specs=(hbm, hbm), name="last_kernel",
        scratch_shapes=[plane, plane, pltpu.SemaphoreType.DMA((2, nx))],
        compiler_params=pltpu.CompilerParams(vmem_limit_bytes=8 * MIB),
    )(got, sx, sc, w0, n0)


def solution(mesh):
    spec = P("gx", "gy", None)
    body = functools.partial(shards, mesh.shape["gx"], mesh.shape["gy"])
    return jax.shard_map(body, mesh=mesh, in_specs=(spec, spec), out_specs=(spec, spec), check_vma=False)
```
